32 devices in a mesh: wide: 16 (over z, y, core), narrow: 2 (over x).
Axes of the slice: x: 2, y: 2, z: 4, core: 2. Of those that a mesh axis runs over, the one named last changes fastest.
Arguments:
- tokens: bfloat16 [1024, 64, 768], P(('wide', 'narrow')), may hold values from -6 to 6
- cotangent: bfloat16 [1024, 64, 768], P(('wide', 'narrow')), may hold values from -0.3125 to 0.3125
- groups: int32 [512], replicated, may hold values from 0 to 108, as said below
- qkv_weight: bfloat16 [768, 2304], replicated, may hold values from -0.21875 to 0.21875
- query_bias: float32 [768], replicated, may hold values from -1.25 to 1.25
- value_bias: float32 [768], replicated, may hold values from -1.25 to 1.25
- out_weight: bfloat16 [768, 768], replicated, may hold values from -0.625 to 0.625
- out_bias: float32 [768], replicated, may hold values from -1.25 to 1.25
- gain_one: float32 [768], replicated, may hold values from 0.5 to 1.5
- shift_one: float32 [768], replicated, may hold values from -1.25 to 1.25
- up_weight: bfloat16 [768, 3072], replicated, may hold values from -0.21875 to 0.21875
- up_bias: float32 [3072], replicated, may hold values from -1.25 to 1.25
- down_weight: bfloat16 [3072, 768], replicated, may hold values from -0.109375 to 0.109375
- down_bias: float32 [768], replicated, may hold values from -1.25 to 1.25
- gain_two: float32 [768], replicated, may hold values from 0.5 to 1.5
- shift_two: float32 [768], replicated, may hold values from -1.25 to 1.25
Outputs:
- loss: float32 [], replicated
- block_out: bfloat16 [1024, 64, 768], P(('wide', 'narrow'))
- input_grad: float32 [1024, 64, 768], P(('wide', 'narrow'))
- qkv_weight_grad: float32 [768, 2304], P('wide')
- query_bias_grad: float32 [768], P('wide')
- value_bias_grad: float32 [768], P('wide')
- out_weight_grad: float32 [768, 768], P('wide')
- out_bias_grad: float32 [768], P('wide')
- gain_one_grad: float32 [768], P('wide')
- shift_one_grad: float32 [768], P('wide')
- up_weight_grad: float32 [768, 3072], P('wide')
- up_bias_grad: float32 [3072], P('wide')
- down_weight_grad: float32 [3072, 768], P('wide')
- down_bias_grad: float32 [768], P('wide')
- gain_two_grad: float32 [768], P('wide')
- shift_two_grad: float32 [768], P('wide')
The draws below stay inside these ranges and needn't reach their ends.
Inputs may be any that keep to these rules, and one draw needn't show every extreme that they name: A pair's in-batch negatives are the other pairs of its language group, among 109 groups of uneven size; the pairs of a group may lie anywhere in the batch.
All inputs are finite; a program needn't handle non-finite values.
Results may differ from the reference program's by a relative error of at most 0.014.
Values may be sent and summed in bfloat16 or wider, within the bound.
A program may use at most 320 MiB of HBM per device.

```python
import jax
import jax.numpy as jnp
from jax import lax

D = 768
HEADS = 12
HEAD_DIM = 64
FF = 3072
SEQ = 64
GROUPS = 109
NPAIRS = 512
NSENT = 1024
N_WIDE = 16
N_NARROW = 2


def draw_groups(key, part):
    raw = jax.random.randint(jax.random.fold_in(key, 17), (NPAIRS,), 0, GROUPS * GROUPS).astype(jnp.int32)
    bounds = jnp.arange(1, GROUPS, dtype=jnp.int32)
    bounds = bounds * bounds
    picked = jnp.sum((raw[:, None] >= bounds[None, :]).astype(jnp.int32), 1).astype(jnp.int32)
    spanning = jax.random.randint(jax.random.fold_in(key, 29), (), 0, GROUPS).astype(jnp.int32)
    picked = picked.at[0].set(spanning)
    picked = picked.at[NPAIRS // 2].set(spanning)
    picked = picked.at[NPAIRS - 1].set(spanning)
    picked = picked.at[1].set(0)
    picked = picked.at[NPAIRS - 2].set(GROUPS - 1)
    return picked.astype(jnp.int32)


def level_of(own_key, dims, shards, low, high):
    level, own = 1.0, jax.random.fold_in(own_key, 6)
    for axis_at, shards_of in shards:
        heights = jnp.exp(jax.random.uniform(jax.random.fold_in(own, axis_at), (shards_of,), jnp.float32, low / len(shards), high / len(shards)))
        level = level * jnp.repeat(heights, dims[axis_at] // shards_of).reshape([-1 if axis == axis_at else 1 for axis in range(len(dims))])
    return level


def normal_values(rng, dims, scale, reach, cuts=(), held_as=jnp.bfloat16):
    level = level_of(rng, dims, cuts, -0.22, 0.18) if cuts else 1.0
    result = jax.random.normal(rng, dims, jnp.float32) * scale * level
    return jnp.minimum(jnp.maximum(result, -reach), reach).astype(held_as)


def setup_inputs(seed: int = 0) -> dict:
    seeds = jax.random.split(jax.random.key(seed), 17)
    tokens = normal_values(seeds[0], (NSENT, SEQ, D), 1.0, 6.0, ((0, 32),))
    cotangent = normal_values(seeds[1], (NSENT, SEQ, D), 0.05, 0.3125, ((0, 32),))
    groups = draw_groups(jax.random.fold_in(seeds[16], 71), 0)
    qkv_weight = normal_values(seeds[3], (D, 3 * D), D ** -0.5, 0.21875)
    query_bias = normal_values(seeds[4], (D,), 0.2, 1.25, (), jnp.float32)
    value_bias = normal_values(seeds[5], (D,), 0.2, 1.25, (), jnp.float32)
    out_weight = normal_values(seeds[6], (D, D), (D // 8) ** -0.5, 0.625)
    out_bias = normal_values(seeds[7], (D,), 0.2, 1.25, (), jnp.float32)
    gain_one = jnp.clip(1.0 + 0.1 * jax.random.normal(seeds[8], (D,), jnp.float32), 0.5, 1.5)
    shift_one = normal_values(seeds[9], (D,), 0.2, 1.25, (), jnp.float32)
    up_weight = normal_values(seeds[10], (D, FF), D ** -0.5, 0.21875)
    up_bias = normal_values(seeds[11], (FF,), 0.2, 1.25, (), jnp.float32)
    down_weight = normal_values(seeds[12], (FF, D), FF ** -0.5, 0.109375)
    down_bias = normal_values(seeds[13], (D,), 0.2, 1.25, (), jnp.float32)
    gain_two = jnp.clip(1.0 + 0.1 * jax.random.normal(seeds[14], (D,), jnp.float32), 0.5, 1.5)
    shift_two = normal_values(seeds[15], (D,), 0.2, 1.25, (), jnp.float32)
    return {"tokens": tokens, "cotangent": cotangent, "groups": groups, "qkv_weight": qkv_weight, "query_bias": query_bias, "value_bias": value_bias, "out_weight": out_weight, "out_bias": out_bias, "gain_one": gain_one, "shift_one": shift_one, "up_weight": up_weight, "up_bias": up_bias, "down_weight": down_weight, "down_bias": down_bias, "gain_two": gain_two, "shift_two": shift_two}


@jax.custom_vjp
def low(v):
    return lax.optimization_barrier(v.astype(jnp.bfloat16)).astype(jnp.float32)

@jax.custom_vjp
def low_back(v):
    return v

def low_keep(v):
    return (low(v), None)

def low_pass(kept, grad):
    return (grad,)

def back_keep(v):
    return (v, None)

def back_low(kept, grad):
    return (low(grad),)
low.defvjp(low_keep, low_pass)
low_back.defvjp(back_keep, back_low)
sim_scale = 40.0
margin = 0.3
norm_eps = 1e-06

def layer_norm(values, gain, shift):
    row_mean = lax.optimization_barrier(jnp.mean(values, -1, keepdims=True))
    centred = values - row_mean
    variance = lax.optimization_barrier(jnp.mean(centred * centred, -1, keepdims=True))
    return centred * lax.rsqrt(variance + norm_eps) * gain + shift

def block_forward(inputs, params):
    qkv_weight, query_bias, value_bias, out_weight, out_bias, gain_one, shift_one, up_weight, up_bias, down_weight, down_bias, gain_two, shift_two = params
    sent_count = inputs.shape[0]
    highest = lax.Precision.HIGHEST
    token_rows = inputs.reshape(sent_count * SEQ, D)
    qkv_bias = jnp.concatenate([query_bias, jnp.zeros_like(query_bias), value_bias])
    qkv_rows = low(low_back(jnp.dot(token_rows, qkv_weight, precision=highest) + qkv_bias))
    split_rows = qkv_rows.reshape(sent_count, SEQ, 3, HEADS, HEAD_DIM)
    query_rows = split_rows[:, :, 0]
    key_rows = split_rows[:, :, 1]
    value_rows = split_rows[:, :, 2]
    scores = low_back(jnp.einsum('nqhd,nkhd->nhqk', query_rows, key_rows, precision=highest) * HEAD_DIM ** (-0.5))
    softmax_probs = jax.nn.softmax(scores, axis=-1)
    context = jnp.einsum('nhqk,nkhd->nqhd', low(softmax_probs), value_rows, precision=highest)
    context = low(low_back(context)).reshape(sent_count * SEQ, D)
    attn_out = low_back(jnp.dot(context, out_weight, precision=highest) + out_bias)
    normed = layer_norm(token_rows + attn_out, gain_one, shift_one)
    up_proj = low_back(jnp.dot(low(normed), up_weight, precision=highest) + up_bias)
    hidden = low(jax.nn.gelu(up_proj, approximate=False))
    down_proj = low_back(jnp.dot(hidden, down_weight, precision=highest) + down_bias)
    final_rows = layer_norm(normed + down_proj, gain_two, shift_two)
    return final_rows.reshape(sent_count, SEQ, D)

def ranking_loss(final_rows, groups):
    highest = lax.Precision.HIGHEST
    cls_rows = final_rows[:, 0, :]
    pooled = low(cls_rows * lax.rsqrt(lax.optimization_barrier(jnp.sum(cls_rows * cls_rows, -1, keepdims=True)) + norm_eps))
    sources = pooled[0::2]
    targets = pooled[1::2]
    pair_count = sources.shape[0]
    own_pair = jnp.eye(pair_count, dtype=jnp.float32)
    same_group = groups[:, None] == groups[None, :]

    def one_side(left_rows, right_rows):
        logits = low_back(sim_scale * jnp.dot(left_rows, right_rows.T, precision=highest)) - sim_scale * margin * own_pair
        masked = jnp.where(same_group, logits, -1e+30)
        return jnp.sum(jax.nn.logsumexp(masked, axis=1) - jnp.diagonal(logits))
    return one_side(sources, targets) + one_side(targets, sources)

def reference(tokens, cotangent, groups, qkv_weight, query_bias, value_bias, out_weight, out_bias, gain_one, shift_one, up_weight, up_bias, down_weight, down_bias, gain_two, shift_two):
    params = tuple((p.astype(jnp.float32) for p in (qkv_weight, query_bias, value_bias, out_weight, out_bias, gain_one, shift_one, up_weight, up_bias, down_weight, down_bias, gain_two, shift_two)))
    inputs = tokens.astype(jnp.float32)
    block_count = N_WIDE * N_NARROW // 4

    def forward(inputs, params):

        def run_block(piece):
            return block_forward(piece, params)
        blocks = inputs.reshape(block_count, NSENT // block_count, SEQ, D)
        final_rows = lax.map(jax.checkpoint(run_block), blocks).reshape(NSENT, SEQ, D)
        return (final_rows, ranking_loss(final_rows, groups))
    (final_rows, rank_loss), pullback = jax.vjp(forward, inputs, params)
    input_grad, grads = pullback((cotangent.astype(jnp.float32), jnp.ones((), jnp.float32)))
    return (rank_loss / NPAIRS, final_rows.astype(jnp.bfloat16), input_grad, grads[0], grads[1], grads[2], grads[3], grads[4], grads[5], grads[6], grads[7], grads[8], grads[9], grads[10], grads[11], grads[12])
```

```python
import functools

import jax
import jax.numpy as jnp
from jax import lax
from jax.experimental import pallas as pl
from jax.experimental.pallas import tpu as pltpu
from jax.sharding import PartitionSpec as P

BF = jnp.bfloat16
F32 = jnp.float32
MESH = pl.DeviceIdType.MESH

HEADS = 12
QUAD = 4
SCALE = 40.0
MARGIN = 0.3
EPS = 1e-06
SIDE = 8
VMEM_BYTES = 60 * 2**20


def nn(a, b):
    return lax.dot_general(a, b, (((1,), (0,)), ((), ())), preferred_element_type=F32)


def nt(a, b):
    return lax.dot_general(a, b, (((1,), (1,)), ((), ())), preferred_element_type=F32)


def tn(a, b):
    return lax.dot_general(a, b, (((0,), (0,)), ((), ())), preferred_element_type=F32)


def params(**more):
    return pltpu.CompilerParams(vmem_limit_bytes=VMEM_BYTES, **more)


def resident(shape):
    return pl.BlockSpec(shape, lambda *_: (0,) * len(shape), pipeline_mode=pl.Buffered(1))


def shape_of(shape, dtype):
    return jax.ShapeDtypeStruct(shape, dtype)


def blocked(rows, mask):
    return jnp.concatenate([rows] * QUAD, axis=0) * mask


def diagonal(full, seq):
    half = full.shape[1] // 2
    lane = lax.broadcasted_iota(jnp.int32, (seq, half), 1) < half // 2
    left = jnp.where(lane, full[:seq, :half], full[seq : 2 * seq, :half])
    right = jnp.where(lane, full[2 * seq : 3 * seq, half:], full[3 * seq :, half:])
    return jnp.concatenate([left, right], axis=1)


def attend_kernel(x_ref, w_ref, qb_ref, vb_ref, mask_ref, qkv_ref, p_ref, ctx_ref):
    sents, seq, width = x_ref.shape
    rows = x_ref[...].reshape(sents * seq, width)
    quad = mask_ref.shape[0]
    for part, bias in ((0, qb_ref), (1, None), (2, vb_ref)):
        cols = slice(part * width, (part + 1) * width)
        y = nn(rows, w_ref[:, cols])
        if bias is not None:
            y = y + bias[...]
        qkv_ref[:, cols] = y.astype(BF)
    mask = mask_ref[...]
    scale = (width // HEADS) ** -0.5
    for s in range(sents):
        at = slice(s * seq, (s + 1) * seq)
        for g in range(width // quad):
            q = qkv_ref[at, g * quad : (g + 1) * quad]
            k = qkv_ref[at, width + g * quad : width + (g + 1) * quad]
            v = qkv_ref[at, 2 * width + g * quad : 2 * width + (g + 1) * quad]
            scores = nt(k, blocked(q, mask)) * scale
            e = jnp.exp(scores - jnp.max(scores, axis=0, keepdims=True))
            p = (e * (1.0 / jnp.sum(e, axis=0, keepdims=True))).astype(BF)
            p_ref[s, :, g * quad : (g + 1) * quad] = p
            ctx_ref[at, g * quad : (g + 1) * quad] = diagonal(tn(p, v), seq).astype(BF)


def attend(tokens, qkv_weight, query_bias, value_bias, mask):
    sents, seq, width = tokens.shape
    rows = sents * seq
    side = SIDE * seq
    return pl.pallas_call(
        attend_kernel,
        grid=(sents // SIDE,),
        in_specs=[
            pl.BlockSpec((SIDE, seq, width), lambda i: (i, 0, 0)),
            resident((width, 3 * width)),
            resident((1, width)),
            resident((1, width)),
            resident(mask.shape),
        ],
        out_specs=[
            pl.BlockSpec((side, 3 * width), lambda i: (i, 0)),
            pl.BlockSpec((SIDE, seq, width), lambda i: (i, 0, 0)),
            pl.BlockSpec((side, width), lambda i: (i, 0)),
        ],
        out_shape=[
            shape_of((rows, 3 * width), BF),
            shape_of((sents, seq, width), BF),
            shape_of((rows, width), BF),
        ],
        compiler_params=params(),
        name="attend",
    )(tokens, qkv_weight, query_bias, value_bias, mask)


def norm(values):
    mean = jnp.mean(values, -1, keepdims=True)
    centred = values - mean
    root = lax.rsqrt(jnp.mean(centred * centred, -1, keepdims=True) + EPS)
    return centred * root, root


def place():
    wide, narrow = lax.axis_index("wide"), lax.axis_index("narrow")
    return wide, narrow, wide // 4, (wide // 2) % 2, wide % 2


def forward_kernel(
    x_ref, ctx_ref, ow_ref, ob_ref, g1_ref, s1_ref, uw_ref, ub_ref, dw_ref, db_ref, g2_ref, s2_ref,
    out_ref, low_ref, xh1_ref, rs1_ref, hid_ref, slope_ref, xh2_ref, rs2_ref, cls_ref, all_ref,
    rows_ref, buf, zs, zr, ys, yr, xs, xr, cs, cr, done,
):
    sents, part, width = x_ref.shape
    depth = uw_ref.shape[1]
    rows = sents * part
    step = pl.program_id(0)
    wide, narrow, z, y, core = place()
    nz, nx = buf.shape[0], buf.shape[3]
    wide_of = lambda a, b, c: (a * 2 + b) * 2 + c

    z_peers = [(lax.rem(z + k, nz), k) for k in range(1, nz)]
    x_peers = [(lax.rem(narrow + k, nx), k) for k in range(1, nx)]
    z_copies = [
        pltpu.make_async_remote_copy(
            src_ref=buf.at[z, y, core, narrow], dst_ref=buf.at[z, y, core, narrow],
            send_sem=zs.at[k - 1], recv_sem=zr.at[k - 1],
            device_id=(wide_of(to, y, core), narrow), device_id_type=MESH,
        )
        for to, k in z_peers
    ]
    y_copy = pltpu.make_async_remote_copy(
        src_ref=buf.at[:, y, core, narrow], dst_ref=buf.at[:, y, core, narrow],
        send_sem=ys, recv_sem=yr,
        device_id=(wide_of(z, 1 - y, core), narrow), device_id_type=MESH,
    )
    x_copies = [
        pltpu.make_async_remote_copy(
            src_ref=buf.at[:, :, core, narrow], dst_ref=buf.at[:, :, core, narrow],
            send_sem=xs.at[k - 1], recv_sem=xr.at[k - 1],
            device_id=(wide, to), device_id_type=MESH,
        )
        for to, k in x_peers
    ]
    core_copy = pltpu.make_async_remote_copy(
        src_ref=buf.at[:, :, core], dst_ref=buf.at[:, :, core],
        send_sem=cs, recv_sem=cr,
        device_id=(wide_of(z, y, 1 - core), narrow), device_id_type=MESH,
    )

    barrier = pltpu.get_barrier_semaphore()

    @pl.when(step == 0)
    def _():
        for to, _ in z_peers:
            pl.semaphore_signal(barrier, inc=1, device_id=(wide_of(to, y, core), narrow), device_id_type=MESH)
        pl.semaphore_signal(barrier, inc=1, device_id=(wide_of(z, 1 - y, core), narrow), device_id_type=MESH)
        for to, _ in x_peers:
            pl.semaphore_signal(barrier, inc=1, device_id=(wide, to), device_id_type=MESH)
        pl.semaphore_signal(barrier, inc=1, device_id=(wide_of(z, y, 1 - core), narrow), device_id_type=MESH)
        pl.semaphore_wait(barrier, nz + nx)

    block = lambda ref: ref[...].reshape(rows, ref.shape[2])

    def put(ref, value):
        ref[...] = value.astype(ref.dtype).reshape(ref.shape)

    pre_one = block(x_ref).astype(F32) + nn(block(ctx_ref), ow_ref[...]) + ob_ref[...]
    xh1, rs1 = norm(pre_one)
    normed = xh1 * g1_ref[...] + s1_ref[...]
    low = normed.astype(BF)
    put(low_ref, low)
    put(xh1_ref, xh1)
    put(rs1_ref, jnp.broadcast_to(rs1, (rows, 128)))
    total = normed + db_ref[...]
    for c in range(depth // width):
        cols = slice(c * width, (c + 1) * width)
        up = nn(low, uw_ref[:, cols]) + ub_ref[:, cols]
        cdf = 0.5 * (lax.erf(up * 0.7071067811865476) + 1.0)
        slope = cdf + up * (0.3989422804014327 * jnp.exp(-0.5 * up * up))
        hidden = (up * cdf).astype(BF)
        hid_ref[:, :, cols] = hidden.reshape(sents, part, width)
        slope_ref[:, :, cols] = slope.astype(BF).reshape(sents, part, width)
        total = total + nn(hidden, dw_ref[cols, :])
    xh2, rs2 = norm(total)
    final = xh2 * g2_ref[...] + s2_ref[...]
    put(out_ref, final)
    put(xh2_ref, xh2)
    put(rs2_ref, jnp.broadcast_to(rs2, (rows, 128)))

    @pl.when(step == 0)
    def _():
        for s in range(sents):
            cls_ref[s : s + 1, :] = final[s * part : s * part + 1, :]
        cls = cls_ref[...]
        pooled = cls * lax.rsqrt(jnp.sum(cls * cls, -1, keepdims=True) + EPS)
        for s in range(sents):
            half = slice(s % 2 * width, (s % 2 + 1) * width)
            rows_ref[s // 2 : s // 2 + 1, half] = pooled[s : s + 1, :]
        buf[z, y, core, narrow] = rows_ref[...].astype(BF)
        for copy in z_copies:
            copy.start()

    @pl.when(step == 1)
    def _():
        for copy in z_copies:
            copy.wait()
        y_copy.start()

    @pl.when(step == 2)
    def _():
        y_copy.wait()
        for copy in x_copies:
            copy.start()

    @pl.when(step == 3)
    def _():
        for copy in x_copies:
            copy.wait()
        core_copy.start()
        core_copy.wait()
        out = pltpu.make_async_copy(buf, all_ref, done)
        out.start()
        out.wait()


def forward(tokens, ctx, ow, ob, g1, s1, uw, ub, dw, db, g2, s2, sizes):
    sents, seq, width = tokens.shape
    depth = uw.shape[1]
    part = seq // 4
    nz, nx = sizes[0] // 4, sizes[1]
    tile = lambda lanes: pl.BlockSpec((sents, part, lanes), lambda i: (0, i, 0))
    whole = lambda lanes, dtype: shape_of((sents, seq, lanes), dtype)
    slots = (nz, 2, 2, nx, sents // 2, 2 * width)
    dma = pltpu.SemaphoreType.DMA
    return pl.pallas_call(
        forward_kernel,
        grid=(4,),
        in_specs=[
            tile(width), tile(width), resident(ow.shape), resident(ob.shape), resident(g1.shape),
            resident(s1.shape), resident(uw.shape), resident(ub.shape), resident(dw.shape),
            resident(db.shape), resident(g2.shape), resident(s2.shape),
        ],
        out_specs=[
            tile(width), tile(width), tile(width), tile(128), tile(depth), tile(depth), tile(width),
            tile(128), pl.BlockSpec((sents, width), lambda i: (0, 0)), pl.BlockSpec(memory_space=pl.ANY),
        ],
        out_shape=[
            whole(width, BF), whole(width, BF), whole(width, BF), whole(128, F32), whole(depth, BF),
            whole(depth, BF), whole(width, BF), whole(128, F32), shape_of((sents, width), F32),
            shape_of(slots, BF),
        ],
        scratch_shapes=[
            pltpu.VMEM((sents // 2, 2 * width), F32), pltpu.VMEM(slots, BF),
            dma((nz - 1,)), dma((nz - 1,)), dma, dma, dma((nx - 1,)), dma((nx - 1,)), dma, dma, dma,
        ],
        compiler_params=params(collective_id=0, has_side_effects=True),
        name="forward",
    )(tokens, ctx.reshape(sents, seq, width), ow, ob, g1, s1, uw, ub, dw, db, g2, s2)


def ranking_kernel(
    all_ref, mine_ref, grow_ref, gcol_ref, mygroup_ref, cls_ref, cot_ref, xh2_ref, rs2_ref, g2_ref,
    loss_ref, down_ref, sums_ref, dcls,
):
    pairs, width = all_ref.shape[0], all_ref.shape[1] // 2
    own = mine_ref.shape[0]
    step = pl.program_id(0)

    @pl.when(step == 0)
    def _():
        first = (lax.axis_index("wide") * lax.axis_size("narrow") + lax.axis_index("narrow")) * own
        strip = min(256, pairs)
        groups = grow_ref[...]

        def logits_of(left, right, start):
            count = left.shape[0]
            same_at = lax.broadcasted_iota(jnp.int32, (count, pairs), 0) + start
            pair_at = lax.broadcasted_iota(jnp.int32, (count, pairs), 1)
            hit = same_at == pair_at
            return nt(left, right) * SCALE - jnp.where(hit, SCALE * MARGIN, 0.0), hit

        def column_lse(left_at, right_at):
            right = all_ref[:, right_at * width : (right_at + 1) * width]

            def strip_step(at, carry):
                top, total, diag = carry
                start = pl.multiple_of(at * strip, strip)
                left = all_ref[pl.ds(start, strip), left_at * width : (left_at + 1) * width]
                logits, hit = logits_of(left, right, start)
                masked = jnp.where(gcol_ref[pl.ds(start, strip), :] == groups, logits, -1e30)
                peak = jnp.maximum(top, jnp.max(masked, axis=0, keepdims=True))
                total = total * jnp.exp(top - peak) + jnp.sum(jnp.exp(masked - peak), axis=0, keepdims=True)
                diag = diag + jnp.sum(jnp.where(hit, logits, 0.0), axis=0, keepdims=True)
                return peak, total, diag

            start = (jnp.full((1, pairs), -1e30, F32), jnp.zeros((1, pairs), F32), jnp.zeros((1, pairs), F32))
            top, total, diag = lax.fori_loop(0, pairs // strip, strip_step, start)
            return top + jnp.log(total), diag

        col_lse, diag = column_lse(0, 1)
        row_lse, diag_again = column_lse(1, 0)
        loss_ref[...] = jnp.sum(col_lse - diag + row_lse - diag_again, axis=1, keepdims=True) / pairs

        same = mygroup_ref[...] == groups

        def side(my_at, other_at, other_lse):
            other = all_ref[:, other_at * width : (other_at + 1) * width]
            mine = mine_ref[:, my_at * width : (my_at + 1) * width]
            logits, hit = logits_of(mine, other, first)
            eye = hit.astype(F32)
            masked = jnp.where(same, logits, -1e30)
            e = jnp.exp(masked - jnp.max(masked, axis=1, keepdims=True))
            d_mine = (e / jnp.sum(e, axis=1, keepdims=True) - eye).astype(BF)
            d_other = (jnp.where(same, jnp.exp(masked - other_lse), 0.0) - eye).astype(BF)
            return (nn(d_mine, other) + nn(d_other, other)) * SCALE

        for at, (other, lse) in enumerate(((1, col_lse), (0, row_lse))):
            terms = side(at, other, lse)
            for p in range(own):
                dcls[2 * p + at : 2 * p + at + 1, :] = terms[p : p + 1, :]
        d = dcls[...]
        c = cls_ref[...]
        root = lax.rsqrt(jnp.sum(c * c, -1, keepdims=True) + EPS)
        dcls[...] = root * d - root * root * root * c * jnp.sum(c * d, -1, keepdims=True)
        sums_ref[...] = jnp.zeros_like(sums_ref)

    side_sents, seq, _ = cot_ref.shape
    rows = side_sents * seq
    start = pl.multiple_of(step * side_sents, side_sents)
    extra = dcls[pl.ds(start, side_sents), :]
    at_zero = lax.broadcasted_iota(jnp.int32, (side_sents, seq, width), 1) == 0
    d_final = cot_ref[...].astype(F32) + jnp.where(at_zero, extra[:, None, :], 0.0)
    d_final = d_final.reshape(rows, width)
    xhat = xh2_ref[...].reshape(rows, width).astype(F32)
    root = rs2_ref[...].reshape(rows, 128)[:, :1]
    e = d_final * g2_ref[...]
    d_pre = (e - jnp.mean(e, -1, keepdims=True) - xhat * jnp.mean(e * xhat, -1, keepdims=True)) * root
    d_down = d_pre.astype(BF)
    down_ref[...] = d_down
    sums_ref[0:1, :] += jnp.sum(d_final * xhat, axis=0, keepdims=True)
    sums_ref[1:2, :] += jnp.sum(d_final, axis=0, keepdims=True)
    sums_ref[2:3, :] += jnp.sum(d_down.astype(F32), axis=0, keepdims=True)


def ranking(gathered, mine, groups, my_groups, cls, cotangent, xh2, rs2, g2):
    sents, seq, width = cotangent.shape
    pairs = gathered.shape[0]
    tile = lambda lanes: pl.BlockSpec((SIDE, seq, lanes), lambda i: (i, 0, 0))
    return pl.pallas_call(
        ranking_kernel,
        grid=(sents // SIDE,),
        in_specs=[
            resident(gathered.shape), resident(mine.shape), resident((1, pairs)), resident((pairs, 1)),
            resident(my_groups.shape), resident(cls.shape), tile(width), tile(width), tile(128),
            resident(g2.shape),
        ],
        out_specs=[
            pl.BlockSpec((1, 1), lambda i: (0, 0)),
            pl.BlockSpec((SIDE * seq, width), lambda i: (i, 0)),
            pl.BlockSpec((8, width), lambda i: (0, 0)),
        ],
        out_shape=[shape_of((1, 1), F32), shape_of((sents * seq, width), BF), shape_of((8, width), F32)],
        scratch_shapes=[pltpu.VMEM((sents, width), F32)],
        compiler_params=params(),
        name="ranking",
    )(gathered, mine, groups.reshape(1, pairs), groups.reshape(pairs, 1), my_groups, cls, cotangent, xh2, rs2, g2)


def hand_out(value, send_ref, keep_ref):
    count, rows, cols = send_ref.shape
    split = value.reshape(count, 2 * rows, cols)
    core = lax.axis_index("wide") % 2

    @pl.when(core == 0)
    def _():
        keep_ref[...] = split[:, :rows].astype(BF)
        send_ref[...] = split[:, rows:].astype(BF)

    @pl.when(core == 1)
    def _():
        keep_ref[...] = split[:, rows:].astype(BF)
        send_ref[...] = split[:, :rows].astype(BF)


def down_grad_kernel(hid_ref, down_ref, send_ref, keep_ref):
    hand_out(tn(hid_ref[...], down_ref[...]), send_ref, keep_ref)


def down_grad(hidden, d_down, n_wide):
    rows, depth = hidden.shape
    width = d_down.shape[1]
    shard = depth // n_wide
    count = width // (2 * shard)
    return pl.pallas_call(
        down_grad_kernel,
        grid=(depth // width,),
        in_specs=[pl.BlockSpec((rows, width), lambda i: (0, i)), resident((rows, width))],
        out_specs=[pl.BlockSpec((count, shard, width), lambda i: (i, 0, 0))] * 2,
        out_shape=[shape_of((n_wide // 2, shard, width), BF)] * 2,
        compiler_params=params(),
        name="down_grad",
    )(hidden, d_down)


def backward_kernel(
    down_ref, slope_ref, dw_ref, uw_ref, xh1_ref, rs1_ref, g1_ref, ow_ref,
    up_ref, attn_ref, ctx_ref, sums_ref, upsum_ref,
):
    rows, width = down_ref.shape
    depth = uw_ref.shape[1]

    @pl.when(pl.program_id(0) == 0)
    def _():
        sums_ref[...] = jnp.zeros_like(sums_ref)
        upsum_ref[...] = jnp.zeros_like(upsum_ref)

    d_down = down_ref[...]
    total = d_down.astype(F32)
    for c in range(depth // width):
        cols = slice(c * width, (c + 1) * width)
        d_up = (nt(d_down, dw_ref[cols, :]) * slope_ref[:, cols].astype(F32)).astype(BF)
        up_ref[:, cols] = d_up
        upsum_ref[:, cols] += jnp.sum(d_up.astype(F32), axis=0, keepdims=True)
        total = total + nt(d_up, uw_ref[:, cols])
    xhat = xh1_ref[...].astype(F32)
    root = rs1_ref[:, :1]
    e = total * g1_ref[...]
    d_pre = (e - jnp.mean(e, -1, keepdims=True) - xhat * jnp.mean(e * xhat, -1, keepdims=True)) * root
    d_attn = d_pre.astype(BF)
    attn_ref[...] = d_attn
    ctx_ref[...] = nt(d_attn, ow_ref[...]).astype(BF)
    sums_ref[0:1, :] += jnp.sum(total * xhat, axis=0, keepdims=True)
    sums_ref[1:2, :] += jnp.sum(total, axis=0, keepdims=True)
    sums_ref[2:3, :] += jnp.sum(d_attn.astype(F32), axis=0, keepdims=True)


def backward(d_down, slope, dw, uw, xh1, rs1, g1, ow):
    rows, width = d_down.shape
    depth = uw.shape[1]
    side = rows // 4
    tile = lambda lanes: pl.BlockSpec((side, lanes), lambda i: (i, 0))
    return pl.pallas_call(
        backward_kernel,
        grid=(4,),
        in_specs=[
            tile(width), tile(depth), resident(dw.shape), resident(uw.shape), tile(width), tile(128),
            resident(g1.shape), resident(ow.shape),
        ],
        out_specs=[
            tile(depth), tile(width), tile(width), pl.BlockSpec((8, width), lambda i: (0, 0)),
            pl.BlockSpec((1, depth), lambda i: (0, 0)),
        ],
        out_shape=[
            shape_of((rows, depth), BF), shape_of((rows, width), BF), shape_of((rows, width), BF),
            shape_of((8, width), F32), shape_of((1, depth), F32),
        ],
        compiler_params=params(),
        name="backward",
    )(d_down, slope, dw, uw, xh1, rs1, g1, ow)


def up_grad_kernel(low_ref, ctx_ref, up_ref, attn_ref, send_ref, keep_ref):
    last = pl.num_programs(0) - 1

    @pl.when(pl.program_id(0) < last)
    def _():
        hand_out(tn(low_ref[...], up_ref[...]), send_ref, keep_ref)

    @pl.when(pl.program_id(0) == last)
    def _():
        hand_out(tn(ctx_ref[...], attn_ref[...]), send_ref, keep_ref)


def up_grad(low, ctx, d_up, d_attn, n_wide):
    rows, depth = d_up.shape
    width = low.shape[1]
    shard = width // n_wide
    steps = depth // width
    return pl.pallas_call(
        up_grad_kernel,
        grid=(steps + 1,),
        in_specs=[
            resident((rows, width)), resident((rows, width)),
            pl.BlockSpec((rows, width), lambda i: (0, jnp.minimum(i, steps - 1))), resident((rows, width)),
        ],
        out_specs=[pl.BlockSpec((n_wide // 2, shard, width), lambda i: (0, 0, i))] * 2,
        out_shape=[shape_of((n_wide // 2, shard, depth + width), BF)] * 2,
        compiler_params=params(),
        name="up_grad",
    )(low, ctx, d_up, d_attn)


def attend_back_kernel(
    q_ref, k_ref, v_ref, dctx_ref, p_ref, x_ref, mask_ref, dqkv_ref, send_ref, keep_ref, qsum_ref, vsum_ref, acc
):
    sents, seq, quad = p_ref.shape
    step = pl.program_id(0)
    mask = mask_ref[...]
    scale = (quad // QUAD) ** -0.5
    for s in range(sents):
        at = slice(s * seq, (s + 1) * seq)
        k = k_ref[at, :]
        p_low = p_ref[s]
        p = p_low.astype(F32)
        dctx = blocked(dctx_ref[at, :], mask)
        d_probs = nt(v_ref[at, :], dctx)
        d_scores = (p * (d_probs - jnp.sum(p * d_probs, axis=0, keepdims=True))).astype(BF)
        dqkv_ref[at, :quad] = (diagonal(tn(d_scores, k), seq) * scale).astype(BF)
        dqkv_ref[at, quad : 2 * quad] = (nn(d_scores, blocked(q_ref[at, :], mask)) * scale).astype(BF)
        dqkv_ref[at, 2 * quad :] = nn(p_low, dctx).astype(BF)
    rows = dqkv_ref[...]
    part = tn(x_ref[...], rows)

    @pl.when(step == 0)
    def _():
        acc[...] = part
        qsum_ref[...] = jnp.zeros_like(qsum_ref)
        vsum_ref[...] = jnp.zeros_like(vsum_ref)

    @pl.when(step > 0)
    def _():
        acc[...] += part

    qsum_ref[...] += jnp.sum(rows[:, :quad].astype(F32), axis=0, keepdims=True)
    vsum_ref[...] += jnp.sum(rows[:, 2 * quad :].astype(F32), axis=0, keepdims=True)

    @pl.when(step == pl.num_programs(0) - 1)
    def _():
        hand_out(acc[...], send_ref, keep_ref)


def attend_back(qkv, d_ctx, probs, token_rows, mask, g, n_wide):
    sents, seq, width = probs.shape
    rows = sents * seq
    quad = mask.shape[0]
    quads = width // quad
    side = SIDE * seq
    cols = lambda at: pl.BlockSpec((side, quad), lambda i: (i, at))
    shard = width // n_wide
    once = lambda shape: pl.BlockSpec(shape, lambda i: (0,) * len(shape))
    return pl.pallas_call(
        attend_back_kernel,
        grid=(sents // SIDE,),
        in_specs=[
            cols(g), cols(quads + g), cols(2 * quads + g), cols(g),
            pl.BlockSpec((SIDE, seq, quad), lambda i: (i, 0, g)),
            pl.BlockSpec((side, width), lambda i: (i, 0)), resident(mask.shape),
        ],
        out_specs=[
            pl.BlockSpec((side, 3 * quad), lambda i: (i, 0)), once((n_wide // 2, shard, 3 * quad)),
            once((n_wide // 2, shard, 3 * quad)), once((1, quad)), once((1, quad)),
        ],
        out_shape=[
            shape_of((rows, 3 * quad), BF), shape_of((n_wide // 2, shard, 3 * quad), BF),
            shape_of((n_wide // 2, shard, 3 * quad), BF), shape_of((1, quad), F32), shape_of((1, quad), F32),
        ],
        scratch_shapes=[pltpu.VMEM((width, 3 * quad), F32)],
        compiler_params=params(),
        name=f"attend_back_{g}",
    )(qkv, qkv, qkv, d_ctx, probs, token_rows, mask)


def input_kernel(*refs):
    *quads, attn_ref, w_ref, out_ref = refs
    quad = quads[0].shape[1] // 3
    rows = jnp.concatenate([ref[:, p * quad : (p + 1) * quad] for p in range(3) for ref in quads], axis=1)
    out_ref[...] = attn_ref[...].astype(F32) + nt(rows, w_ref[...])


def input_grad_of(d_qkv, d_attn, qkv_weight):
    rows, width = d_attn.shape
    side = rows // 4
    tile = lambda lanes: pl.BlockSpec((side, lanes), lambda i: (i, 0))
    return pl.pallas_call(
        input_kernel,
        grid=(4,),
        in_specs=[tile(part.shape[1]) for part in d_qkv] + [tile(width), resident(qkv_weight.shape)],
        out_specs=tile(width),
        out_shape=shape_of((rows, width), F32),
        compiler_params=params(),
        name="input_grad",
    )(*d_qkv, d_attn, qkv_weight)


def reduce_piece(send, keep, sizes):
    n_wide, n_narrow = sizes
    nz = n_wide // 4
    wide, narrow, z, y, core = place()
    axes = ("wide", "narrow")
    index = lambda w, x: w * n_narrow + x

    def shift(array, to):
        pairs = [(index(w, x), index(*to(w, x))) for w in range(n_wide) for x in range(n_narrow)]
        return lax.ppermute(array, axes, pairs)

    def add(*terms):
        return sum(t.astype(F32) for t in terms).astype(BF)

    count, rows, cols = keep.shape
    got = shift(send, lambda w, x: (w ^ 1, x))
    acc = add(keep, got)
    part = cols // n_narrow
    piece = lambda at: lax.dynamic_slice_in_dim(acc, at * part, part, axis=2)
    got = [
        shift(piece(lax.rem(narrow + k, n_narrow)), lambda w, x, k=k: (w, (x + k) % n_narrow))
        for k in range(1, n_narrow)
    ]
    acc = add(piece(narrow), *got)
    acc = acc.reshape(nz, 2, rows, part)
    half = lambda at: lax.dynamic_index_in_dim(acc, at, axis=1, keepdims=False)
    got = shift(half(1 - y), lambda w, x: (w ^ 2, x))
    acc = add(half(y), got)
    own = lambda at: lax.dynamic_index_in_dim(acc, at, axis=0, keepdims=False)
    got = [
        shift(own(lax.rem(z + k, nz)), lambda w, x, k=k: ((w + 4 * k) % n_wide, x)) for k in range(1, nz)
    ]
    mine = add(own(z), *got)
    out = jnp.zeros((rows, cols), BF)
    out = lax.dynamic_update_slice_in_dim(out, mine, narrow * part, axis=1)
    for k in range(1, n_narrow):
        other = shift(mine, lambda w, x, k=k: (w, (x + k) % n_narrow))
        out = lax.dynamic_update_slice_in_dim(out, other, lax.rem(narrow + n_narrow - k, n_narrow) * part, axis=1)
    return out.astype(F32)


def per_device(
    sizes, tokens, cotangent, groups, qkv_weight, query_bias, value_bias, out_weight, out_bias, gain_one,
    shift_one, up_weight, up_bias, down_weight, down_bias, gain_two, shift_two,
):
    n_wide, n_narrow = sizes
    sents, seq, width = tokens.shape
    depth = up_weight.shape[1]
    rows = sents * seq
    head = width // HEADS
    quad = QUAD * head
    row = lambda v: v.reshape(1, -1)
    at = jnp.arange(quad, dtype=jnp.int32) // head
    mask = (at[:, None] == at[None, :]).astype(BF)

    qkv, probs, ctx = attend(tokens, qkv_weight, row(query_bias), row(value_bias), mask)
    block_out, low, xh1, rs1, hidden, slope, xh2, rs2, cls, slots = forward(
        tokens, ctx, out_weight, row(out_bias), row(gain_one), row(shift_one), up_weight, row(up_bias),
        down_weight, row(down_bias), row(gain_two), row(shift_two), sizes,
    )
    pairs = n_wide * n_narrow * (sents // 2)
    gathered = slots.reshape(pairs, 2 * width)
    first = (lax.axis_index("wide") * n_narrow + lax.axis_index("narrow")) * (sents // 2)
    mine = lax.dynamic_slice_in_dim(gathered, first, sents // 2)
    my_groups = lax.dynamic_slice_in_dim(groups, first, sents // 2).reshape(-1, 1)
    loss, d_down, sums_two = ranking(
        gathered, mine, groups, my_groups, cls, cotangent, xh2, rs2, row(gain_two)
    )
    flat = lambda v: v.reshape(rows, v.shape[-1])
    down_part = reduce_piece(*down_grad(flat(hidden), d_down, n_wide), sizes)
    d_up, d_attn, d_ctx, sums_one, up_sum = backward(
        d_down, flat(slope), down_weight, up_weight, flat(xh1), flat(rs1), row(gain_one), out_weight
    )
    up_part = reduce_piece(*up_grad(flat(low), ctx, d_up, d_attn, n_wide), sizes)
    token_rows = flat(tokens)
    d_qkv, parts, q_sums, v_sums = [], [], [], []
    for g in range(width // quad):
        rows_g, send, keep, q_sum, v_sum = attend_back(qkv, d_ctx, probs, token_rows, mask, g, n_wide)
        d_qkv.append(rows_g)
        q_sums.append(q_sum[0])
        v_sums.append(v_sum[0])
        if g == width // quad - 1:
            columns = jnp.concatenate(
                [
                    jnp.stack(
                        [
                            jnp.concatenate(q_sums), jnp.concatenate(v_sums), sums_one[2], sums_one[0],
                            sums_one[1], sums_two[2], sums_two[0], sums_two[1],
                        ],
                        axis=1,
                    ),
                    up_sum.reshape(width, depth // width),
                ],
                axis=1,
            )
            columns = jnp.pad(columns, ((0, 0), (0, 128 - columns.shape[1]))).astype(BF)
            columns = columns.reshape(n_wide // 2, 2, width // n_wide, 128)
            core = lax.axis_index("wide") % 2
            pick = lambda at: lax.dynamic_index_in_dim(columns, at, axis=1, keepdims=False)
            send = jnp.concatenate([send, pick(1 - core)], axis=2)
            keep = jnp.concatenate([keep, pick(core)], axis=2)
        parts.append(reduce_piece(send, keep, sizes))
    input_grad = input_grad_of(d_qkv, d_attn, qkv_weight).reshape(sents, seq, width)
    qkv_grad = jnp.concatenate(
        [part[:, p * quad : (p + 1) * quad] for p in range(3) for part in parts], axis=1
    )
    vectors = parts[-1][:, 3 * quad :]
    vector = lambda at: vectors[:, at]
    return (
        loss.reshape(()), block_out, input_grad, qkv_grad, vector(0), vector(1), up_part[:, depth:],
        vector(2), vector(3), vector(4), up_part[:, :depth],
        vectors[:, 8 : 8 + depth // width].reshape(-1), down_part, vector(5), vector(6), vector(7),
    )


def solution(mesh):
    sizes = (mesh.shape["wide"], mesh.shape["narrow"])
    split = P(("wide", "narrow"), None, None)
    matrix, vector = P("wide", None), P("wide")
    return jax.shard_map(
        functools.partial(per_device, sizes),
        mesh=mesh,
        in_specs=(split, split) + (P(),) * 14,
        out_specs=(
            P(), split, split, matrix, vector, vector, matrix, vector, vector, vector, matrix, vector,
            matrix, vector, vector, vector,
        ),
        check_vma=False,
    )
```

```python
import functools

import jax
import jax.numpy as jnp
from jax import lax
from jax.experimental import pallas as pl
from jax.experimental.pallas import tpu as pltpu
from jax.sharding import PartitionSpec as P

BF = jnp.bfloat16
F32 = jnp.float32
MESH = pl.DeviceIdType.MESH

HEADS = 12
QUAD = 4
SCALE = 40.0
MARGIN = 0.3
EPS = 1e-06
SIDE = 8
VMEM_BYTES = 60 * 2**20


def nn(a, b):
    return lax.dot_general(a, b, (((1,), (0,)), ((), ())), preferred_element_type=F32)


def nt(a, b):
    return lax.dot_general(a, b, (((1,), (1,)), ((), ())), preferred_element_type=F32)


def tn(a, b):
    return lax.dot_general(a, b, (((0,), (0,)), ((), ())), preferred_element_type=F32)


def params(**more):
    return pltpu.CompilerParams(vmem_limit_bytes=VMEM_BYTES, **more)


def resident(shape):
    return pl.BlockSpec(shape, lambda *_: (0,) * len(shape), pipeline_mode=pl.Buffered(1))


def shape_of(shape, dtype):
    return jax.ShapeDtypeStruct(shape, dtype)


def head_mask(quad):
    head = quad // QUAD
    at = lambda axis: lax.broadcasted_iota(jnp.int32, (quad, quad), axis) // head
    return (at(0) == at(1)).astype(F32).astype(BF)


def line(ref):
    return ref[...].reshape(1, ref.shape[0])


def blocked(rows, mask):
    return jnp.concatenate([rows] * QUAD, axis=0) * mask


def diagonal(full, seq):
    half = full.shape[1] // 2
    lane = lax.broadcasted_iota(jnp.int32, (seq, half), 1) < half // 2
    left = jnp.where(lane, full[:seq, :half], full[seq : 2 * seq, :half])
    right = jnp.where(lane, full[2 * seq : 3 * seq, half:], full[3 * seq :, half:])
    return jnp.concatenate([left, right], axis=1)


def attend_kernel(x_ref, w_ref, qb_ref, vb_ref, qkv_ref, p_ref, ctx_ref):
    sents, seq, width = x_ref.shape
    rows = x_ref[...].reshape(sents * seq, width)
    quad = width // QUADS
    for part, bias in ((0, qb_ref), (1, None), (2, vb_ref)):
        cols = slice(part * width, (part + 1) * width)
        y = nn(rows, w_ref[:, cols])
        if bias is not None:
            y = y + line(bias)
        qkv_ref[:, cols] = y.astype(BF)
    mask = head_mask(quad)
    scale = (width // HEADS) ** -0.5
    for s in range(sents):
        at = slice(s * seq, (s + 1) * seq)
        for g in range(width // quad):
            q = qkv_ref[at, g * quad : (g + 1) * quad]
            k = qkv_ref[at, width + g * quad : width + (g + 1) * quad]
            v = qkv_ref[at, 2 * width + g * quad : 2 * width + (g + 1) * quad]
            scores = nt(k, blocked(q, mask)) * scale
            e = jnp.exp(scores - jnp.max(scores, axis=0, keepdims=True))
            p = (e * (1.0 / jnp.sum(e, axis=0, keepdims=True))).astype(BF)
            p_ref[s, :, g * quad : (g + 1) * quad] = p
            ctx_ref[at, g * quad : (g + 1) * quad] = diagonal(tn(p, v), seq).astype(BF)


def attend(tokens, qkv_weight, query_bias, value_bias):
    sents, seq, width = tokens.shape
    rows = sents * seq
    side = SIDE * seq
    return pl.pallas_call(
        attend_kernel,
        grid=(sents // SIDE,),
        in_specs=[
            pl.BlockSpec((SIDE, seq, width), lambda i: (i, 0, 0)),
            resident((width, 3 * width)),
            resident((width,)),
            resident((width,)),
        ],
        out_specs=[
            pl.BlockSpec((side, 3 * width), lambda i: (i, 0)),
            pl.BlockSpec((SIDE, seq, width), lambda i: (i, 0, 0)),
            pl.BlockSpec((side, width), lambda i: (i, 0)),
        ],
        out_shape=[
            shape_of((rows, 3 * width), BF),
            shape_of((sents, seq, width), BF),
            shape_of((rows, width), BF),
        ],
        compiler_params=params(),
        name="attend",
    )(tokens, qkv_weight, query_bias, value_bias)


def norm(values):
    mean = jnp.mean(values, -1, keepdims=True)
    centred = values - mean
    root = lax.rsqrt(jnp.mean(centred * centred, -1, keepdims=True) + EPS)
    return centred * root, root


def place():
    wide, narrow = lax.axis_index("wide"), lax.axis_index("narrow")
    return wide, narrow, wide // 4, (wide // 2) % 2, wide % 2


def forward_kernel(
    x_ref, ctx_ref, ow_ref, ob_ref, g1_ref, s1_ref, uw_hbm, ub_ref, dw_hbm, db_ref, g2_ref, s2_ref,
    out_ref, low_ref, xh1_ref, rs1_ref, hid_ref, slope_ref, xh2_ref, rs2_ref, cls_ref, all_ref,
    rows_ref, uw_ref, dw_ref, w_sems, buf, zs, zr, ys, yr, xs, xr, cs, cr, done,
):
    sents, part, width = x_ref.shape
    depth = uw_ref.shape[1]
    rows = sents * part
    step = pl.program_id(0)
    wide, narrow, z, y, core = place()
    nz, nx = buf.shape[0], buf.shape[3]
    wide_of = lambda a, b, c: (a * 2 + b) * 2 + c

    z_peers = [(lax.rem(z + k, nz), k) for k in range(1, nz)]
    x_peers = [(lax.rem(narrow + k, nx), k) for k in range(1, nx)]
    z_copies = [
        pltpu.make_async_remote_copy(
            src_ref=buf.at[z, y, core, narrow], dst_ref=buf.at[z, y, core, narrow],
            send_sem=zs.at[k - 1], recv_sem=zr.at[k - 1],
            device_id=(wide_of(to, y, core), narrow), device_id_type=MESH,
        )
        for to, k in z_peers
    ]
    y_copy = pltpu.make_async_remote_copy(
        src_ref=buf.at[:, y, core, narrow], dst_ref=buf.at[:, y, core, narrow],
        send_sem=ys, recv_sem=yr,
        device_id=(wide_of(z, 1 - y, core), narrow), device_id_type=MESH,
    )
    x_copies = [
        pltpu.make_async_remote_copy(
            src_ref=buf.at[:, :, core, narrow], dst_ref=buf.at[:, :, core, narrow],
            send_sem=xs.at[k - 1], recv_sem=xr.at[k - 1],
            device_id=(wide, to), device_id_type=MESH,
        )
        for to, k in x_peers
    ]
    core_copy = pltpu.make_async_remote_copy(
        src_ref=buf.at[:, :, core], dst_ref=buf.at[:, :, core],
        send_sem=cs, recv_sem=cr,
        device_id=(wide_of(z, y, 1 - core), narrow), device_id_type=MESH,
    )

    barrier = pltpu.get_barrier_semaphore()
    weights = [
        pltpu.make_async_copy(uw_hbm, uw_ref, w_sems.at[0]), pltpu.make_async_copy(dw_hbm, dw_ref, w_sems.at[1])
    ]

    @pl.when(step == 0)
    def _():
        for copy in weights:
            copy.start()
        for to, _ in z_peers:
            pl.semaphore_signal(barrier, inc=1, device_id=(wide_of(to, y, core), narrow), device_id_type=MESH)
        pl.semaphore_signal(barrier, inc=1, device_id=(wide_of(z, 1 - y, core), narrow), device_id_type=MESH)
        for to, _ in x_peers:
            pl.semaphore_signal(barrier, inc=1, device_id=(wide, to), device_id_type=MESH)
        pl.semaphore_signal(barrier, inc=1, device_id=(wide_of(z, y, 1 - core), narrow), device_id_type=MESH)
        pl.semaphore_wait(barrier, nz + nx)

    block = lambda ref: ref[...].reshape(rows, ref.shape[2])

    def put(ref, value):
        ref[...] = value.astype(ref.dtype).reshape(ref.shape)

    pre_one = block(x_ref).astype(F32) + nn(block(ctx_ref), ow_ref[...]) + line(ob_ref)
    xh1, rs1 = norm(pre_one)
    normed = xh1 * line(g1_ref) + line(s1_ref)
    low = normed.astype(BF)
    put(low_ref, low)
    put(xh1_ref, xh1)
    put(rs1_ref, jnp.broadcast_to(rs1, (rows, 128)))
    total = normed + line(db_ref)

    @pl.when(step == 0)
    def _():
        for copy in weights:
            copy.wait()

    for c in range(depth // width):
        cols = slice(c * width, (c + 1) * width)
        up = nn(low, uw_ref[:, cols]) + ub_ref[cols].reshape(1, width)
        cdf = 0.5 * (lax.erf(up * 0.7071067811865476) + 1.0)
        slope = cdf + up * (0.3989422804014327 * jnp.exp(-0.5 * up * up))
        hidden = (up * cdf).astype(BF)
        hid_ref[:, :, cols] = hidden.reshape(sents, part, width)
        slope_ref[:, :, cols] = slope.astype(BF).reshape(sents, part, width)
        total = total + nn(hidden, dw_ref[cols, :])
    xh2, rs2 = norm(total)
    final = xh2 * line(g2_ref) + line(s2_ref)
    put(out_ref, final)
    put(xh2_ref, xh2)
    put(rs2_ref, jnp.broadcast_to(rs2, (rows, 128)))

    @pl.when(step == 0)
    def _():
        for s in range(sents):
            cls_ref[s : s + 1, :] = final[s * part : s * part + 1, :]
        cls = cls_ref[...]
        pooled = cls * lax.rsqrt(jnp.sum(cls * cls, -1, keepdims=True) + EPS)
        for s in range(sents):
            half = slice(s % 2 * width, (s % 2 + 1) * width)
            rows_ref[s // 2 : s // 2 + 1, half] = pooled[s : s + 1, :]
        buf[z, y, core, narrow] = rows_ref[...].astype(BF)
        for copy in z_copies:
            copy.start()

    @pl.when(step == 1)
    def _():
        for copy in z_copies:
            copy.wait()
        y_copy.start()

    @pl.when(step == 2)
    def _():
        y_copy.wait()
        for copy in x_copies:
            copy.start()

    @pl.when(step == 3)
    def _():
        for copy in x_copies:
            copy.wait()
        core_copy.start()
        core_copy.wait()
        out = pltpu.make_async_copy(buf, all_ref, done)
        out.start()
        out.wait()


def forward(tokens, ctx, ow, ob, g1, s1, uw, ub, dw, db, g2, s2, sizes):
    sents, seq, width = tokens.shape
    depth = uw.shape[1]
    part = seq // 4
    nz, nx = sizes[0] // 4, sizes[1]
    tile = lambda lanes: pl.BlockSpec((sents, part, lanes), lambda i: (0, i, 0))
    whole = lambda lanes, dtype: shape_of((sents, seq, lanes), dtype)
    slots = (nz, 2, 2, nx, sents // 2, 2 * width)
    dma = pltpu.SemaphoreType.DMA
    return pl.pallas_call(
        forward_kernel,
        grid=(4,),
        in_specs=[
            tile(width), tile(width), resident(ow.shape), resident(ob.shape), resident(g1.shape),
            resident(s1.shape), pl.BlockSpec(memory_space=pl.ANY), resident(ub.shape),
            pl.BlockSpec(memory_space=pl.ANY),
            resident(db.shape), resident(g2.shape), resident(s2.shape),
        ],
        out_specs=[
            tile(width), tile(width), tile(width), tile(128), tile(depth), tile(depth), tile(width),
            tile(128), pl.BlockSpec((sents, width), lambda i: (0, 0)), pl.BlockSpec(memory_space=pl.ANY),
        ],
        out_shape=[
            whole(width, BF), whole(width, BF), whole(width, BF), whole(128, F32), whole(depth, BF),
            whole(depth, BF), whole(width, BF), whole(128, F32), shape_of((sents, width), F32),
            shape_of(slots, BF),
        ],
        scratch_shapes=[
            pltpu.VMEM((sents // 2, 2 * width), F32), pltpu.VMEM(uw.shape, BF), pltpu.VMEM(dw.shape, BF), dma((2,)),
            pltpu.VMEM(slots, BF),
            dma((nz - 1,)), dma((nz - 1,)), dma, dma, dma((nx - 1,)), dma((nx - 1,)), dma, dma, dma,
        ],
        compiler_params=params(collective_id=0, has_side_effects=True),
        name="forward",
    )(tokens, ctx.reshape(sents, seq, width), ow, ob, g1, s1, uw, ub, dw, db, g2, s2)


def ranking_kernel(
    all_ref, group_ref, cls_ref, cot_ref, xh2_ref, rs2_ref, g2_ref,
    loss_ref, down_ref, sums_ref, dcls, gcol_ref,
):
    pairs, width = all_ref.shape[0], all_ref.shape[1] // 2
    own = cls_ref.shape[0] // 2
    step = pl.program_id(0)

    @pl.when(step == 0)
    def _():
        first = (lax.axis_index("wide") * lax.axis_size("narrow") + lax.axis_index("narrow")) * own
        strip = min(256, pairs)
        groups = line(group_ref)
        gcol_ref[...] = jnp.transpose(jnp.broadcast_to(groups, (128, pairs)))
        own_rows = pl.ds(pl.multiple_of(first, own), own)

        def logits_of(left, right, start):
            count = left.shape[0]
            same_at = lax.broadcasted_iota(jnp.int32, (count, pairs), 0) + start
            pair_at = lax.broadcasted_iota(jnp.int32, (count, pairs), 1)
            hit = same_at == pair_at
            return nt(left, right) * SCALE - jnp.where(hit, SCALE * MARGIN, 0.0), hit

        def column_lse(left_at, right_at):
            right = all_ref[:, right_at * width : (right_at + 1) * width]

            def strip_step(at, carry):
                top, total, diag = carry
                start = pl.multiple_of(at * strip, strip)
                left = all_ref[pl.ds(start, strip), left_at * width : (left_at + 1) * width]
                logits, hit = logits_of(left, right, start)
                masked = jnp.where(gcol_ref[pl.ds(start, strip), :1] == groups, logits, -1e30)
                peak = jnp.maximum(top, jnp.max(masked, axis=0, keepdims=True))
                total = total * jnp.exp(top - peak) + jnp.sum(jnp.exp(masked - peak), axis=0, keepdims=True)
                diag = diag + jnp.sum(jnp.where(hit, logits, 0.0), axis=0, keepdims=True)
                return peak, total, diag

            start = (jnp.full((1, pairs), -1e30, F32), jnp.zeros((1, pairs), F32), jnp.zeros((1, pairs), F32))
            top, total, diag = lax.fori_loop(0, pairs // strip, strip_step, start)
            return top + jnp.log(total), diag

        col_lse, diag = column_lse(0, 1)
        row_lse, diag_again = column_lse(1, 0)
        loss_ref[...] = jnp.sum(col_lse - diag + row_lse - diag_again, axis=1, keepdims=True) / pairs

        same = gcol_ref[own_rows, :1] == groups

        def side(my_at, other_at, other_lse):
            other = all_ref[:, other_at * width : (other_at + 1) * width]
            mine = all_ref[own_rows, my_at * width : (my_at + 1) * width]
            logits, hit = logits_of(mine, other, first)
            eye = hit.astype(F32)
            masked = jnp.where(same, logits, -1e30)
            e = jnp.exp(masked - jnp.max(masked, axis=1, keepdims=True))
            d_mine = (e / jnp.sum(e, axis=1, keepdims=True) - eye).astype(BF)
            d_other = (jnp.where(same, jnp.exp(masked - other_lse), 0.0) - eye).astype(BF)
            return (nn(d_mine, other) + nn(d_other, other)) * SCALE

        for at, (other, lse) in enumerate(((1, col_lse), (0, row_lse))):
            terms = side(at, other, lse)
            for p in range(own):
                dcls[2 * p + at : 2 * p + at + 1, :] = terms[p : p + 1, :]
        d = dcls[...]
        c = cls_ref[...]
        root = lax.rsqrt(jnp.sum(c * c, -1, keepdims=True) + EPS)
        dcls[...] = root * d - root * root * root * c * jnp.sum(c * d, -1, keepdims=True)
        sums_ref[...] = jnp.zeros_like(sums_ref)

    side_sents, seq, _ = cot_ref.shape
    rows = side_sents * seq
    start = pl.multiple_of(step * side_sents, side_sents)
    extra = dcls[pl.ds(start, side_sents), :]
    at_zero = lax.broadcasted_iota(jnp.int32, (side_sents, seq, width), 1) == 0
    d_final = cot_ref[...].astype(F32) + jnp.where(at_zero, extra[:, None, :], 0.0)
    d_final = d_final.reshape(rows, width)
    xhat = xh2_ref[...].reshape(rows, width).astype(F32)
    root = rs2_ref[...].reshape(rows, 128)[:, :1]
    e = d_final * line(g2_ref)
    d_pre = (e - jnp.mean(e, -1, keepdims=True) - xhat * jnp.mean(e * xhat, -1, keepdims=True)) * root
    d_down = d_pre.astype(BF)
    down_ref[...] = d_down
    sums_ref[0:1, :] += jnp.sum(d_final * xhat, axis=0, keepdims=True)
    sums_ref[1:2, :] += jnp.sum(d_final, axis=0, keepdims=True)
    sums_ref[2:3, :] += jnp.sum(d_down.astype(F32), axis=0, keepdims=True)


def ranking(gathered, groups, cls, cotangent, xh2, rs2, g2):
    sents, seq, width = cotangent.shape
    pairs = gathered.shape[0]
    tile = lambda lanes: pl.BlockSpec((SIDE, seq, lanes), lambda i: (i, 0, 0))
    return pl.pallas_call(
        ranking_kernel,
        grid=(sents // SIDE,),
        in_specs=[
            resident(gathered.shape), resident(groups.shape), resident(cls.shape), tile(width), tile(width), tile(128),
            resident(g2.shape),
        ],
        out_specs=[
            pl.BlockSpec((1, 1), lambda i: (0, 0)),
            pl.BlockSpec((SIDE * seq, width), lambda i: (i, 0)),
            pl.BlockSpec((8, width), lambda i: (0, 0)),
        ],
        out_shape=[shape_of((1, 1), F32), shape_of((sents * seq, width), BF), shape_of((8, width), F32)],
        scratch_shapes=[pltpu.VMEM((sents, width), F32), pltpu.VMEM((pairs, 128), jnp.int32)],
        compiler_params=params(),
        name="ranking",
    )(gathered, groups, cls, cotangent, xh2, rs2, g2)


def copy_to(src, dst, sends, recvs, at, device):
    return pltpu.make_async_remote_copy(
        src_ref=src, dst_ref=dst, send_sem=sends.at[at], recv_sem=recvs.at[at], device_id=device,
        device_id_type=MESH,
    )


def plus(*terms):
    return sum(t.astype(F32) for t in terms).astype(BF)


class Peers:
    def __init__(self, nz):
        self.nz = nz
        wide, self.x, self.z, self.y, self.core = place()
        self.sibling = (wide + 1 - 2 * self.core, self.x)
        self.over_x = (wide, 1 - self.x)
        self.over_y = (wide + 2 - 4 * self.y, self.x)
        self.zs = [lax.rem(self.z + k, nz) for k in range(1, nz)]
        self.over_z = [(lax.rem(wide + 4 * k, 4 * nz), self.x) for k in range(1, nz)]

    def greet(self, devices):
        barrier = pltpu.get_barrier_semaphore()
        for device in devices:
            pl.semaphore_signal(barrier, inc=1, device_id=device, device_id_type=MESH)
        pl.semaphore_wait(barrier, len(devices))


class Stages:
    SEMS = 9

    def __init__(self, peers, terms, got, sends, recvs):
        self.peers, self.terms, self.got, self.sends, self.recvs = peers, terms, got, sends, recvs
        self.third = got["xa"].shape[2]

    @staticmethod
    def scratch(nz, rows, cols):
        third = rows // 3
        return {
            "xa": (nz, 2, third, cols), "yb": (2, nz, rows - third, cols),
            "ya": (nz, third, cols), "xb": (nz, rows - third, cols),
        }

    def first(self):
        p, t = self.peers, self.third
        return [
            copy_to(self.terms.at[1 - p.x, :, :, :t], self.got["xa"], self.sends, self.recvs, 1, p.over_x),
            copy_to(self.terms.at[:, :, 1 - p.y, t:], self.got["yb"], self.sends, self.recvs, 2, p.over_y),
        ]

    def second(self):
        p, t = self.peers, self.third
        return [
            copy_to(self.terms.at[p.x, :, 1 - p.y, :t], self.got["ya"], self.sends, self.recvs, 3, p.over_y),
            copy_to(self.terms.at[1 - p.x, :, p.y, t:], self.got["xb"], self.sends, self.recvs, 4, p.over_x),
        ]

    def add_first(self):
        p, t = self.peers, self.third
        for copy in self.first():
            copy.wait()
        self.terms[p.x, :, :, :t] = plus(self.terms[p.x, :, :, :t], self.got["xa"][...])
        for h in range(2):
            self.terms[h, :, p.y, t:] = plus(self.terms[h, :, p.y, t:], self.got["yb"][h])

    def add_second(self):
        p, t = self.peers, self.third
        for copy in self.second():
            copy.wait()
        self.terms[p.x, :, p.y, :t] = plus(self.terms[p.x, :, p.y, :t], self.got["ya"][...])
        self.terms[p.x, :, p.y, t:] = plus(self.terms[p.x, :, p.y, t:], self.got["xb"][...])


class Finish:
    def __init__(self, peers, shard, got_z, mine, other, sends, recvs):
        self.peers, self.shard, self.got_z, self.mine, self.other = peers, shard, got_z, mine, other
        self.sends, self.recvs = sends, recvs

    def along_z(self):
        p = self.peers
        return [
            copy_to(self.shard(to), self.got_z.at[k], self.sends, self.recvs, 5 + k, device)
            for k, (to, device) in enumerate(zip(p.zs, p.over_z, strict=True))
        ]

    def along_x(self):
        return copy_to(self.mine, self.other, self.sends, self.recvs, 8, self.peers.over_x)

    def add(self):
        for copy in self.along_z():
            copy.wait()
        got = [self.got_z[k] for k in range(self.peers.nz - 1)]
        self.mine[...] = plus(self.shard(self.peers.z)[...], *got)


def hand_out(value, keep, send):
    halves, nz, ny, rows, cols = keep.shape
    split = value.reshape(nz * ny, 2 * rows, halves * cols)
    core = lax.axis_index("wide") % 2

    def put(ref, part):
        for h in range(halves):
            ref[h] = part[:, :, h * cols : (h + 1) * cols].astype(BF).reshape(nz, ny, rows, cols)

    @pl.when(core == 0)
    def _():
        put(keep, split[:, :rows])
        put(send, split[:, rows:])

    @pl.when(core == 1)
    def _():
        put(keep, split[:, rows:])
        put(send, split[:, :rows])


def backward_kernel(fused, nz, *refs):
    (down_ref, hid_ref, slope_ref, dw_hbm, uw_hbm, xh1_ref, rs1_ref, g1_ref, ow_ref, actx_ref) = refs[:10]
    (up_ref, attn_ref, ctx_ref, sums_ref, upsum_ref, owg_ref, dwg_ref) = refs[10:17]
    dw_ref, uw_ref, w_sems, owg, *comm = refs[17:]
    blocks = 4
    width = down_ref.shape[1]
    rows, depth = slope_ref.shape
    step = pl.program_id(0)
    weights = [
        pltpu.make_async_copy(dw_hbm, dw_ref, w_sems.at[0]), pltpu.make_async_copy(uw_hbm, uw_ref, w_sems.at[1])
    ]

    if fused:
        terms, send, got, xa, yb, ya, xb, c_send, c_recv, s_send, s_recv = comm
        peers = Peers(nz)
        stages = Stages(peers, terms, {"xa": xa, "yb": yb, "ya": ya, "xb": xb}, s_send, s_recv)

        def exchange(i):
            return copy_to(send.at[i % 2], got.at[i % 2], c_send, c_recv, i, peers.sibling)

    @pl.when(step == 0)
    def _():
        for copy in weights:
            copy.start()
        sums_ref[...] = jnp.zeros_like(sums_ref)
        upsum_ref[...] = jnp.zeros_like(upsum_ref)
        if fused:
            peers.greet([peers.sibling, peers.over_x, peers.over_y])

    if fused:
        for i in range(1, blocks + 1):

            @pl.when(step == i)
            def _(i=i):
                exchange(i - 1).wait()
                for h in range(2):
                    terms[h, i - 1] = plus(terms[h, i - 1], got[(i - 1) % 2, h, 0])

        @pl.when(step == blocks)
        def _():
            for copy in stages.first():
                copy.start()

        @pl.when(step == blocks + 2)
        def _():
            stages.add_first()
            for copy in stages.second():
                copy.start()

    @pl.when(step < blocks)
    def _():
        value = tn(hid_ref[...], down_ref[...])
        if fused:
            for i in range(blocks):

                @pl.when(step == i)
                def _(i=i):
                    hand_out(value, terms.at[:, i : i + 1], send.at[i % 2])
                    exchange(i).start()

        else:
            dwg_ref[...] = value.astype(BF)

    @pl.when(step == blocks)
    def _():
        for copy in weights:
            copy.wait()

    @pl.when(step >= blocks)
    def _():
        d_down = down_ref[pl.ds(pl.multiple_of((step - blocks) * rows, rows), rows), :]
        total = d_down.astype(F32)
        for c in range(depth // width):
            cols = slice(c * width, (c + 1) * width)
            d_up = (nt(d_down, dw_ref[cols, :]) * slope_ref[:, cols].astype(F32)).astype(BF)
            up_ref[:, cols] = d_up
            upsum_ref[:, cols] += jnp.sum(d_up.astype(F32), axis=0, keepdims=True)
            total = total + nt(d_up, uw_ref[:, cols])
        xhat = xh1_ref[...].astype(F32)
        root = rs1_ref[:, :1]
        e = total * g1_ref[...].reshape(1, width)
        d_pre = (e - jnp.mean(e, -1, keepdims=True) - xhat * jnp.mean(e * xhat, -1, keepdims=True)) * root
        d_attn = d_pre.astype(BF)
        attn_ref[...] = d_attn
        ctx_ref[...] = nt(d_attn, ow_ref[...]).astype(BF)
        sums_ref[0:1, :] += jnp.sum(total * xhat, axis=0, keepdims=True)
        sums_ref[1:2, :] += jnp.sum(total, axis=0, keepdims=True)
        sums_ref[2:3, :] += jnp.sum(d_attn.astype(F32), axis=0, keepdims=True)
        part = tn(actx_ref[...], d_attn)

        @pl.when(step == blocks)
        def _():
            owg[...] = part

        @pl.when(step > blocks)
        def _():
            owg[...] += part

    @pl.when(step == pl.num_programs(0) - 1)
    def _():
        owg_ref[...] = owg[...].astype(BF)
        if fused:
            stages.add_second()
            dwg_ref[...] = terms[peers.x, :, peers.y]


def backward(d_down, hidden, slope, dw, uw, xh1, rs1, g1, ow, ctx, sizes):
    fused = sizes == (16, 2)
    nz = sizes[0] // 4
    rows, width = d_down.shape
    depth = uw.shape[1]
    side = rows // 4
    tile = lambda lanes: pl.BlockSpec((side, lanes), lambda i: (jnp.maximum(i - 4, 0), 0))
    once = lambda *shape: pl.BlockSpec(shape, lambda i: (0,) * len(shape))
    shard = depth // sizes[0]
    half = width // 2
    dma = pltpu.SemaphoreType.DMA
    scratch = [
        pltpu.VMEM(dw.shape, BF), pltpu.VMEM(uw.shape, BF), dma((2,)), pltpu.VMEM((width, width), F32)
    ]
    if fused:
        scratch += [
            pltpu.VMEM((2, nz, 2, shard, half), BF), pltpu.VMEM((2, 2, 1, 2, shard, half), BF),
            pltpu.VMEM((2, 2, 1, 2, shard, half), BF),
        ]
        scratch += [pltpu.VMEM(s, BF) for s in Stages.scratch(nz, shard, half).values()]
        scratch += [dma((4,)), dma((4,)), dma((Stages.SEMS,)), dma((Stages.SEMS,))]
        dwg_spec, dwg_shape = once(nz, shard, half), (nz, shard, half)
        extra = dict(collective_id=1, has_side_effects=True)
    else:
        dwg_spec, dwg_shape = pl.BlockSpec((width, width), lambda i: (jnp.minimum(i, 3), 0)), (depth, width)
        extra = {}
    return pl.pallas_call(
        functools.partial(backward_kernel, fused, nz),
        grid=(8,),
        in_specs=[
            resident((rows, width)), pl.BlockSpec((rows, width), lambda i: (0, jnp.minimum(i, 3))), tile(depth),
            pl.BlockSpec(memory_space=pl.ANY), pl.BlockSpec(memory_space=pl.ANY), tile(width), tile(128),
            resident(g1.shape), resident(ow.shape), tile(width),
        ],
        out_specs=[
            tile(depth), tile(width), tile(width), once(8, width), once(1, depth), once(width, width), dwg_spec
        ],
        out_shape=[
            shape_of((rows, depth), BF), shape_of((rows, width), BF), shape_of((rows, width), BF),
            shape_of((8, width), F32), shape_of((1, depth), F32), shape_of((width, width), BF),
            shape_of(dwg_shape, BF),
        ],
        scratch_shapes=scratch,
        compiler_params=params(**extra),
        name="backward",
    )(d_down, hidden, slope, dw, uw, xh1, rs1, g1, ow, ctx)


UPS, QUADS, TILES = 4, 3, 4
FIRST_QUAD = UPS
FIRST_INPUT = UPS + QUADS * TILES
STEPS = FIRST_INPUT + TILES
OUT_PIECE = UPS
PIECES = UPS + 1 + QUADS
VECTORS = 16


def tail_kernel(fused, nz, *refs):
    (low_ref, up_ref, q_ref, k_ref, v_ref, dctx_ref, p_ref, x_ref, w_hbm, owg_ref, dsum_ref,
     one_ref, two_ref, upsum_ref) = refs[:14]
    out_ref, vec_out = refs[14:16]
    if fused:
        outs = refs[16:20]
        w_ref, w_sem, dqkv, acc, vec, *comm = refs[20:]
    else:
        upg_ref, qkvg_ref = refs[16:18]
        w_ref, w_sem, dqkv, acc, vec = refs[18:]
    rows, quad = q_ref.shape
    sents, seq, _ = p_ref.shape
    width = acc.shape[0]
    step = pl.program_id(0)
    weight = pltpu.make_async_copy(w_hbm, w_ref, w_sem)
    at_quad = jnp.clip(step - FIRST_QUAD, 0, QUADS * TILES - 1)
    g, tile = at_quad // TILES, at_quad % TILES

    events = {}

    def event(at):
        def add(action):
            events.setdefault(at, []).append(action)

        return add

    if fused:
        (mine, other, dmine, dother, terms, send, got, xa, yb, ya, xb, gz, dz, vgot, sends, recvs, d_sends, d_recvs, v_sends, v_recvs) = comm
        peers = Peers(nz)
        down = Finish(peers, lambda at: dsum_ref.at[at], dz, dmine, dother, d_sends, d_recvs)

        @event(0)
        def _():
            peers.greet([peers.sibling, peers.over_x, peers.over_y, *peers.over_z])
            for copy in down.along_z():
                copy.start()

        @event(4)
        def _():
            down.add()
            down.along_x().start()

        @event(7)
        def _():
            down.along_x().wait()

        def piece(n, ready, later):
            sent, recv = sends.at[n], recvs.at[n]
            stages = Stages(
                peers, terms.at[n], {"xa": xa.at[n], "yb": yb.at[n], "ya": ya.at[n], "xb": xb.at[n]}, sent, recv
            )
            finish = Finish(
                peers, lambda at: terms.at[n, peers.x, at, peers.y], gz.at[n], mine.at[n], other.at[n],
                sent, recv,
            )
            chip = copy_to(send.at[n % 2], got.at[n % 2], sent, recv, 0, peers.sibling)

            @event(ready + later[0])
            def _():
                chip.wait()
                for h in range(2):
                    terms[n, h] = plus(terms[n, h], got[n % 2, h])
                for copy in stages.first():
                    copy.start()

            @event(ready + later[1])
            def _():
                stages.add_first()
                for copy in stages.second():
                    copy.start()

            @event(ready + later[2])
            def _():
                stages.add_second()
                for copy in finish.along_z():
                    copy.start()

            @event(ready + later[3])
            def _():
                finish.add()
                finish.along_x().start()

            @event(ready + later[4])
            def _():
                finish.along_x().wait()

            return chip

        usual, hurried = (1, 3, 5, 7, 9), (1, 2, 3, 4, 5)
        ready = [*range(UPS), UPS] + [FIRST_QUAD + TILES * (q + 1) - 1 for q in range(QUADS)]
        chips = [piece(n, ready[n], hurried if n == PIECES - 1 else usual) for n in range(PIECES)]

        def vector_copy(n, device):
            return copy_to(vec, vgot.at[n], v_sends, v_recvs, n, device)

        routes = [[peers.sibling], [peers.over_x], [peers.over_y], peers.over_z]

        def vector_copies(hop):
            return [vector_copy(hop + k, device) for k, device in enumerate(routes[hop])]

        for hop in range(4):

            @event(FIRST_INPUT + hop + 1)
            def _(hop=hop):
                for copy in vector_copies(hop):
                    copy.wait()
                vec[...] += sum(vgot[hop + k] for k in range(len(routes[hop])))
                if hop < 3:
                    for copy in vector_copies(hop + 1):
                        copy.start()

    for at, actions in sorted(events.items()):
        if at < STEPS:

            @pl.when(step == at)
            def _(actions=actions):
                for action in actions:
                    action()

    @pl.when(step == 0)
    def _():
        weight.start()
        vec[...] = jnp.zeros_like(vec)
        vec[2:3, :] = one_ref[2:3, :]
        vec[3:5, :] = one_ref[0:2, :]
        vec[5:6, :] = two_ref[2:3, :]
        vec[6:8, :] = two_ref[0:2, :]
        for c in range(UPS):
            vec[8 + c : 9 + c, :] = upsum_ref[:, c * width : (c + 1) * width]

    def hand(n, value):
        hand_out(value, terms.at[n], send.at[n % 2])
        chips[n].start()

    @pl.when(step < UPS)
    def _():
        value = tn(low_ref[...], up_ref[...])
        if fused:
            for n in range(UPS):

                @pl.when(step == n)
                def _(n=n):
                    hand(n, value)

        else:
            upg_ref[...] = value.astype(BF)

    @pl.when((step >= FIRST_QUAD) & (step < FIRST_INPUT))
    def _():
        mask = head_mask(quad)
        scale = (quad // QUAD) ** -0.5
        here = lambda size, s=0: pl.ds(pl.multiple_of(tile * rows + s * seq, seq), size)
        for s in range(sents):
            at = slice(s * seq, (s + 1) * seq)
            k = k_ref[at, :]
            p_low = p_ref[s]
            p = p_low.astype(F32)
            dctx = blocked(dctx_ref[at, :], mask)
            d_probs = nt(v_ref[at, :], dctx)
            d_scores = (p * (d_probs - jnp.sum(p * d_probs, axis=0, keepdims=True))).astype(BF)
            dqkv[g, here(seq, s), :quad] = (diagonal(tn(d_scores, k), seq) * scale).astype(BF)
            dqkv[g, here(seq, s), quad : 2 * quad] = (nn(d_scores, blocked(q_ref[at, :], mask)) * scale).astype(BF)
            dqkv[g, here(seq, s), 2 * quad :] = nn(p_low, dctx).astype(BF)
        grads = dqkv[g, here(rows), :]
        part = tn(x_ref[...], grads)
        q_sum = jnp.sum(grads[:, :quad].astype(F32), axis=0, keepdims=True)
        v_sum = jnp.sum(grads[:, 2 * quad :].astype(F32), axis=0, keepdims=True)
        for q in range(QUADS):

            @pl.when(g == q)
            def _(q=q):
                vec[0:1, q * quad : (q + 1) * quad] += q_sum
                vec[1:2, q * quad : (q + 1) * quad] += v_sum

        @pl.when(tile == 0)
        def _():
            acc[...] = part

        @pl.when(tile > 0)
        def _():
            acc[...] += part

    if fused:

        @pl.when(step == UPS)
        def _():
            hand(OUT_PIECE, owg_ref[...])

        for q in range(QUADS):

            @pl.when(step == FIRST_QUAD + TILES * (q + 1) - 1)
            def _(q=q):
                hand(OUT_PIECE + 1 + q, acc[...])

        @pl.when(step == FIRST_INPUT - 1)
        def _():
            for copy in vector_copies(0):
                copy.start()

    else:

        @pl.when((step >= FIRST_QUAD) & (step < FIRST_INPUT) & (tile == TILES - 1))
        def _():
            qkvg_ref[...] = acc[...].astype(BF)

    @pl.when(step == FIRST_INPUT)
    def _():
        weight.wait()

    @pl.when(step >= FIRST_INPUT)
    def _():
        here = pl.ds(pl.multiple_of((step - FIRST_INPUT) * rows, rows), rows)
        grads = jnp.concatenate(
            [dqkv[q, here, part * quad : (part + 1) * quad] for part in range(3) for q in range(QUADS)], axis=1
        )
        out_ref[...] = nt(grads, w_ref[...]).astype(BF)

    @pl.when(step == STEPS - 1)
    def _():
        for at, actions in sorted(events.items()):
            if at >= STEPS:
                for action in actions:
                    action()
        vec_out[...] = vec[...]
        if fused:
            for ref, value in zip(outs, (mine, other, dmine, dother), strict=True):
                ref[...] = value[...]


def tail(low, d_up, qkv, d_ctx, probs, token_rows, qkv_weight, owg, dsum, one, two, upsum, sizes):
    fused = sizes == (16, 2)
    nz = sizes[0] // 4
    sents, seq, width = probs.shape
    rows = sents * seq
    side = rows // TILES
    quad = width // QUADS
    shard, half = width // sizes[0], width // 2
    at = lambda i: jnp.clip(i - FIRST_QUAD, 0, QUADS * TILES - 1)
    cols = lambda part: pl.BlockSpec((side, quad), lambda i: (at(i) % TILES, part * QUADS + at(i) // TILES))
    once = lambda *shape: pl.BlockSpec(shape, lambda i: (0,) * len(shape))
    finish = lambda lanes: pl.BlockSpec((side, lanes), lambda i: (jnp.maximum(i - FIRST_INPUT, 0), 0))
    dma = pltpu.SemaphoreType.DMA
    scratch = [
        pltpu.VMEM(qkv_weight.shape, BF), dma, pltpu.VMEM((QUADS, rows, width), BF),
        pltpu.VMEM((width, width), F32), pltpu.VMEM((VECTORS, width), F32),
    ]
    out_specs = [finish(width), once(VECTORS, width)]
    out_shape = [shape_of((rows, width), BF), shape_of((VECTORS, width), F32)]
    if fused:
        piece = (2, nz, 2, shard, half)
        scratch += [pltpu.VMEM((PIECES, shard, half), BF)] * 2 + [pltpu.VMEM(dsum.shape[1:], BF)] * 2
        scratch += [pltpu.VMEM((PIECES, *piece), BF), pltpu.VMEM((2, *piece), BF), pltpu.VMEM((2, *piece), BF)]
        scratch += [pltpu.VMEM((PIECES, *s), BF) for s in Stages.scratch(nz, shard, half).values()]
        scratch += [
            pltpu.VMEM((PIECES, nz - 1, shard, half), BF), pltpu.VMEM((nz - 1, *dsum.shape[1:]), BF),
            pltpu.VMEM((2 + nz, VECTORS, width), F32),
        ]
        scratch += [dma((PIECES, Stages.SEMS))] * 2 + [dma((Stages.SEMS,))] * 2 + [dma((2 + nz,))] * 2
        out_specs += [once(PIECES, shard, half)] * 2 + [once(*dsum.shape[1:])] * 2
        out_shape += [shape_of((PIECES, shard, half), BF)] * 2 + [shape_of(dsum.shape[1:], BF)] * 2
        extra = dict(collective_id=2, has_side_effects=True)
    else:
        out_specs += [
            pl.BlockSpec((width, width), lambda i: (0, jnp.minimum(i, UPS - 1))),
            pl.BlockSpec((width, width), lambda i: (0, at(i) // TILES)),
        ]
        out_shape += [shape_of((width, UPS * width), BF), shape_of((width, QUADS * width), BF)]
        extra = {}
    return pl.pallas_call(
        functools.partial(tail_kernel, fused, nz),
        grid=(STEPS,),
        in_specs=[
            resident((rows, width)), pl.BlockSpec((rows, width), lambda i: (0, jnp.minimum(i, UPS - 1))),
            cols(0), cols(1), cols(2), cols(0),
            pl.BlockSpec((SIDE, seq, quad), lambda i: (at(i) % TILES, 0, at(i) // TILES)),
            pl.BlockSpec((side, width), lambda i: (at(i) % TILES, 0)),
            pl.BlockSpec(memory_space=pl.ANY), resident(owg.shape), resident(dsum.shape), resident(one.shape),
            resident(two.shape), resident(upsum.shape),
        ],
        out_specs=out_specs,
        out_shape=out_shape,
        scratch_shapes=scratch,
        compiler_params=params(**extra),
        name="tail",
    )(low, d_up, qkv, qkv, qkv, d_ctx, probs, token_rows, qkv_weight, owg, dsum, one, two, upsum)


def finish_kernel(fused, part_ref, attn_ref, *refs):
    if not fused:
        (input_ref,) = refs
    else:
        (mine_ref, other_ref, dmine_ref, dother_ref, vec_ref, input_ref, qkv_ref, qb_ref, vb_ref, out_ref, ob_ref,
         g1_ref, s1_ref, up_ref, ub_ref, down_ref, db_ref, g2_ref, s2_ref) = refs
    input_ref[...] = part_ref[...].astype(F32) + attn_ref[...].astype(F32)
    if not fused:
        return

    @pl.when(pl.program_id(0) == 0)
    def _():
        wide, narrow, z, _, _ = place()
        width = vec_ref.shape[1]
        shard = qb_ref.shape[0]

        def whole(mine, other):
            mine, other = mine.astype(F32), other.astype(F32)
            return jnp.concatenate([jnp.where(narrow == 0, mine, other), jnp.where(narrow == 0, other, mine)], axis=-1)

        for n in range(UPS):
            up_ref[:, n * width : (n + 1) * width] = whole(mine_ref[n], other_ref[n])
        out_ref[...] = whole(mine_ref[OUT_PIECE], other_ref[OUT_PIECE])
        quad = width // QUADS
        for q in range(QUADS):
            block = whole(mine_ref[OUT_PIECE + 1 + q], other_ref[OUT_PIECE + 1 + q])
            for part in range(3):
                to = part * width + q * quad
                qkv_ref[:, to : to + quad] = block[:, part * quad : (part + 1) * quad]
        down_ref[...] = whole(dmine_ref[...], dother_ref[...])
        rolled = pltpu.roll(vec_ref[...], lax.rem(width - wide * shard, width), 1)
        for n, ref in enumerate((qb_ref, vb_ref, ob_ref, g1_ref, s1_ref, db_ref, g2_ref, s2_ref)):
            ref[...] = rolled[n, :shard]
        depth = ub_ref.shape[0]
        ups = jnp.concatenate([vec_ref[pl.ds(8 + z, 1), :]] * 8, axis=0)
        ub_ref[...] = pltpu.roll(ups, lax.rem(width - lax.rem(wide, 4) * depth, width), 1)[0, :depth]


def finish(part, d_attn, sums, sizes, depth):
    fused = bool(sums)
    rows, width = part.shape
    side = rows // TILES
    shard = width // sizes[0]
    tile = pl.BlockSpec((side, width), lambda i: (i, 0))
    shapes = [(rows, width)]
    if fused:
        up = depth // sizes[0]
        vector = (shard,)
        shapes += [
            (shard, 3 * width), vector, vector, (shard, width), vector, vector, vector, (shard, depth), (up,),
            (up, width), vector, vector, vector,
        ]
    return pl.pallas_call(
        functools.partial(finish_kernel, fused),
        grid=(TILES,),
        in_specs=[tile, tile] + [resident(a.shape) for a in sums],
        out_specs=[tile] + [pl.BlockSpec(s, lambda i, n=len(s): (0,) * n) for s in shapes[1:]],
        out_shape=[shape_of(s, F32) for s in shapes],
        compiler_params=params(),
        name="finish",
    )(part, d_attn, *sums)


def per_device(
    sizes, tokens, cotangent, groups, qkv_weight, query_bias, value_bias, out_weight, out_bias, gain_one,
    shift_one, up_weight, up_bias, down_weight, down_bias, gain_two, shift_two,
):
    n_wide, n_narrow = sizes
    sents, seq, width = tokens.shape
    depth = up_weight.shape[1]
    rows = sents * seq
    flat = lambda v: v.reshape(rows, v.shape[-1])

    qkv, probs, ctx = attend(tokens, qkv_weight, query_bias, value_bias)
    block_out, low, xh1, rs1, hidden, slope, xh2, rs2, cls, slots = forward(
        tokens, ctx, out_weight, out_bias, gain_one, shift_one, up_weight, up_bias, down_weight, down_bias,
        gain_two, shift_two, sizes,
    )
    gathered = slots.reshape(n_wide * n_narrow * (sents // 2), 2 * width)
    loss, d_down, sums_two = ranking(gathered, groups, cls, cotangent, xh2, rs2, gain_two)
    d_up, d_attn, d_ctx, sums_one, up_sum, out_terms, down_terms = backward(
        d_down, flat(hidden), flat(slope), down_weight, up_weight, flat(xh1), flat(rs1), gain_one, out_weight,
        ctx, sizes,
    )
    part, vectors, *sums = tail(
        flat(low), d_up, qkv, d_ctx, probs, flat(tokens), qkv_weight, out_terms, down_terms, sums_one, sums_two,
        up_sum, sizes,
    )
    if sizes == (16, 2):
        input_grad, *grads = finish(part, d_attn, [*sums, vectors], sizes, depth)
    else:
        (input_grad,) = finish(part, d_attn, [], sizes, depth)
        up_terms, qkv_terms = sums
        quad = width // QUADS
        qkv_terms = qkv_terms.reshape(width, QUADS, 3, quad).transpose(0, 2, 1, 3).reshape(width, 3 * width)
        total = lambda v: lax.psum(
            lax.psum_scatter(v, "wide", scatter_dimension=0, tiled=True).astype(F32), "narrow"
        )
        vector = lambda n: total(vectors[n])
        grads = (
            total(qkv_terms), vector(0), vector(1), total(out_terms), vector(2), vector(3), vector(4),
            total(up_terms), total(vectors[8 : 8 + UPS].reshape(-1)), total(down_terms), vector(5), vector(6),
            vector(7),
        )
    return (loss.reshape(()), block_out, input_grad.reshape(sents, seq, width), *grads)


def solution(mesh):
    sizes = (mesh.shape["wide"], mesh.shape["narrow"])
    split = P(("wide", "narrow"), None, None)
    matrix, vector = P("wide", None), P("wide")
    return jax.shard_map(
        functools.partial(per_device, sizes),
        mesh=mesh,
        in_specs=(split, split) + (P(),) * 14,
        out_specs=(
            P(), split, split, matrix, vector, vector, matrix, vector, vector, vector, matrix, vector,
            matrix, vector, vector, vector,
        ),
        check_vma=False,
    )
```

```python
import functools

import jax
import jax.numpy as jnp
from jax import lax
from jax.experimental import pallas as pl
from jax.experimental.pallas import tpu as pltpu
from jax.sharding import PartitionSpec as P

BF = jnp.bfloat16
F32 = jnp.float32
MESH = pl.DeviceIdType.MESH

HEADS = 12
QUAD = 4
SCALE = 40.0
MARGIN = 0.3
EPS = 1e-06
SIDE = 8
VMEM_BYTES = 60 * 2**20


def nn(a, b):
    return lax.dot_general(a, b, (((1,), (0,)), ((), ())), preferred_element_type=F32)


def nt(a, b):
    return lax.dot_general(a, b, (((1,), (1,)), ((), ())), preferred_element_type=F32)


def tn(a, b):
    return lax.dot_general(a, b, (((0,), (0,)), ((), ())), preferred_element_type=F32)


def params(**more):
    return pltpu.CompilerParams(vmem_limit_bytes=VMEM_BYTES, **more)


def resident(shape):
    return pl.BlockSpec(shape, lambda *_: (0,) * len(shape), pipeline_mode=pl.Buffered(1))


def shape_of(shape, dtype):
    return jax.ShapeDtypeStruct(shape, dtype)


def head_mask(quad):
    head = quad // QUAD
    at = lambda axis: lax.broadcasted_iota(jnp.int32, (quad, quad), axis) // head
    return (at(0) == at(1)).astype(F32).astype(BF)


def line(ref):
    return ref[...].reshape(1, ref.shape[0])


def blocked(rows, mask):
    return jnp.concatenate([rows] * QUAD, axis=0) * mask


def diagonal(full, seq):
    half = full.shape[1] // 2
    lane = lax.broadcasted_iota(jnp.int32, (seq, half), 1) < half // 2
    left = jnp.where(lane, full[:seq, :half], full[seq : 2 * seq, :half])
    right = jnp.where(lane, full[2 * seq : 3 * seq, half:], full[3 * seq :, half:])
    return jnp.concatenate([left, right], axis=1)


def paired(left, right, seq):
    half = left.shape[1] // 2
    lane = lax.broadcasted_iota(jnp.int32, (seq, half), 1) < half // 2
    parts = []
    for at in (slice(0, half), slice(half, 2 * half)):
        full = tn(left[:, at], right[:, at])
        parts.append(jnp.where(lane, full[:seq], full[seq:]))
    return jnp.concatenate(parts, axis=1)


def attend_kernel(x_ref, w_ref, qb_ref, vb_ref, qkv_ref, p_ref, ctx_ref):
    sents, seq, width = x_ref.shape
    rows = x_ref[...].reshape(sents * seq, width)
    quad = width // QUADS
    for part, bias in ((0, qb_ref), (1, None), (2, vb_ref)):
        cols = slice(part * width, (part + 1) * width)
        y = nn(rows, w_ref[:, cols])
        if bias is not None:
            y = y + line(bias)
        qkv_ref[:, cols] = y.astype(BF)
    mask = head_mask(quad)
    scale = (width // HEADS) ** -0.5
    for s in range(sents):
        at = slice(s * seq, (s + 1) * seq)
        for g in range(width // quad):
            q = qkv_ref[at, g * quad : (g + 1) * quad]
            k = qkv_ref[at, width + g * quad : width + (g + 1) * quad]
            v = qkv_ref[at, 2 * width + g * quad : 2 * width + (g + 1) * quad]
            scores = nt(k, blocked(q, mask)) * scale
            e = jnp.exp(scores - jnp.max(scores, axis=0, keepdims=True))
            p = (e * (1.0 / jnp.sum(e, axis=0, keepdims=True))).astype(BF)
            p_ref[s, :, g * quad : (g + 1) * quad] = p
            ctx_ref[at, g * quad : (g + 1) * quad] = diagonal(tn(p, v), seq).astype(BF)


def attend(tokens, qkv_weight, query_bias, value_bias):
    sents, seq, width = tokens.shape
    rows = sents * seq
    side = SIDE * seq
    return pl.pallas_call(
        attend_kernel,
        grid=(sents // SIDE,),
        in_specs=[
            pl.BlockSpec((SIDE, seq, width), lambda i: (i, 0, 0)),
            resident((width, 3 * width)),
            resident((width,)),
            resident((width,)),
        ],
        out_specs=[
            pl.BlockSpec((side, 3 * width), lambda i: (i, 0)),
            pl.BlockSpec((SIDE, seq, width), lambda i: (i, 0, 0)),
            pl.BlockSpec((side, width), lambda i: (i, 0)),
        ],
        out_shape=[
            shape_of((rows, 3 * width), BF),
            shape_of((sents, seq, width), BF),
            shape_of((rows, width), BF),
        ],
        compiler_params=params(),
        name="attend",
    )(tokens, qkv_weight, query_bias, value_bias)


def norm(values):
    mean = jnp.mean(values, -1, keepdims=True)
    centred = values - mean
    root = lax.rsqrt(jnp.mean(centred * centred, -1, keepdims=True) + EPS)
    return centred * root, root


def place():
    wide, narrow = lax.axis_index("wide"), lax.axis_index("narrow")
    return wide, narrow, wide // 4, (wide // 2) % 2, wide % 2


def forward_kernel(
    x_ref, ctx_ref, ow_ref, ob_ref, g1_ref, s1_ref, uw_hbm, ub_ref, dw_hbm, db_ref, g2_ref, s2_ref,
    out_ref, low_ref, xh1_ref, rs1_ref, hid_ref, slope_ref, xh2_ref, rs2_ref, cls_ref, all_ref,
    rows_ref, uw_ref, dw_ref, w_sems, buf, zs, zr, ys, yr, xs, xr, cs, cr, done,
):
    sents, part, width = x_ref.shape
    depth = uw_ref.shape[1]
    rows = sents * part
    step = pl.program_id(0)
    wide, narrow, z, y, core = place()
    nz, nx = buf.shape[0], buf.shape[3]
    wide_of = lambda a, b, c: (a * 2 + b) * 2 + c

    z_peers = [(lax.rem(z + k, nz), k) for k in range(1, nz)]
    x_peers = [(lax.rem(narrow + k, nx), k) for k in range(1, nx)]
    z_copies = [
        pltpu.make_async_remote_copy(
            src_ref=buf.at[z, y, core, narrow], dst_ref=buf.at[z, y, core, narrow],
            send_sem=zs.at[k - 1], recv_sem=zr.at[k - 1],
            device_id=(wide_of(to, y, core), narrow), device_id_type=MESH,
        )
        for to, k in z_peers
    ]
    y_copy = pltpu.make_async_remote_copy(
        src_ref=buf.at[:, y, core, narrow], dst_ref=buf.at[:, y, core, narrow],
        send_sem=ys, recv_sem=yr,
        device_id=(wide_of(z, 1 - y, core), narrow), device_id_type=MESH,
    )
    x_copies = [
        pltpu.make_async_remote_copy(
            src_ref=buf.at[:, :, core, narrow], dst_ref=buf.at[:, :, core, narrow],
            send_sem=xs.at[k - 1], recv_sem=xr.at[k - 1],
            device_id=(wide, to), device_id_type=MESH,
        )
        for to, k in x_peers
    ]
    core_copy = pltpu.make_async_remote_copy(
        src_ref=buf.at[:, :, core], dst_ref=buf.at[:, :, core],
        send_sem=cs, recv_sem=cr,
        device_id=(wide_of(z, y, 1 - core), narrow), device_id_type=MESH,
    )

    barrier = pltpu.get_barrier_semaphore()
    weights = [
        pltpu.make_async_copy(uw_hbm, uw_ref, w_sems.at[0]), pltpu.make_async_copy(dw_hbm, dw_ref, w_sems.at[1])
    ]

    @pl.when(step == 0)
    def _():
        for copy in weights:
            copy.start()
        for to, _ in z_peers:
            pl.semaphore_signal(barrier, inc=1, device_id=(wide_of(to, y, core), narrow), device_id_type=MESH)
        pl.semaphore_signal(barrier, inc=1, device_id=(wide_of(z, 1 - y, core), narrow), device_id_type=MESH)
        for to, _ in x_peers:
            pl.semaphore_signal(barrier, inc=1, device_id=(wide, to), device_id_type=MESH)
        pl.semaphore_signal(barrier, inc=1, device_id=(wide_of(z, y, 1 - core), narrow), device_id_type=MESH)
        pl.semaphore_wait(barrier, nz + nx)

    block = lambda ref: ref[...].reshape(rows, ref.shape[2])

    def put(ref, value):
        ref[...] = value.astype(ref.dtype).reshape(ref.shape)

    pre_one = block(x_ref).astype(F32) + nn(block(ctx_ref), ow_ref[...]) + line(ob_ref)
    xh1, rs1 = norm(pre_one)
    normed = xh1 * line(g1_ref) + line(s1_ref)
    low = normed.astype(BF)
    put(low_ref, low)
    put(xh1_ref, xh1)
    put(rs1_ref, jnp.broadcast_to(rs1, (rows, 128)))
    total = normed + line(db_ref)

    @pl.when(step == 0)
    def _():
        for copy in weights:
            copy.wait()

    for c in range(depth // width):
        cols = slice(c * width, (c + 1) * width)
        up = nn(low, uw_ref[:, cols]) + ub_ref[cols].reshape(1, width)
        cdf = 0.5 * (lax.erf(up * 0.7071067811865476) + 1.0)
        slope = cdf + up * (0.3989422804014327 * jnp.exp(-0.5 * up * up))
        hidden = (up * cdf).astype(BF)
        hid_ref[:, :, cols] = hidden.reshape(sents, part, width)
        slope_ref[:, :, cols] = slope.astype(BF).reshape(sents, part, width)
        total = total + nn(hidden, dw_ref[cols, :])
    xh2, rs2 = norm(total)
    final = xh2 * line(g2_ref) + line(s2_ref)
    put(out_ref, final)
    put(xh2_ref, xh2)
    put(rs2_ref, jnp.broadcast_to(rs2, (rows, 128)))

    @pl.when(step == 0)
    def _():
        for s in range(sents):
            cls_ref[s : s + 1, :] = final[s * part : s * part + 1, :]
        cls = cls_ref[...]
        pooled = cls * lax.rsqrt(jnp.sum(cls * cls, -1, keepdims=True) + EPS)
        for s in range(sents):
            half = slice(s % 2 * width, (s % 2 + 1) * width)
            rows_ref[s // 2 : s // 2 + 1, half] = pooled[s : s + 1, :]
        buf[z, y, core, narrow] = rows_ref[...].astype(BF)
        for copy in z_copies:
            copy.start()

    @pl.when(step == 1)
    def _():
        for copy in z_copies:
            copy.wait()
        y_copy.start()

    @pl.when(step == 2)
    def _():
        y_copy.wait()
        for copy in x_copies:
            copy.start()

    @pl.when(step == 3)
    def _():
        for copy in x_copies:
            copy.wait()
        core_copy.start()
        core_copy.wait()
        out = pltpu.make_async_copy(buf, all_ref, done)
        out.start()
        out.wait()


def forward(tokens, ctx, ow, ob, g1, s1, uw, ub, dw, db, g2, s2, sizes):
    sents, seq, width = tokens.shape
    depth = uw.shape[1]
    part = seq // 4
    nz, nx = sizes[0] // 4, sizes[1]
    tile = lambda lanes: pl.BlockSpec((sents, part, lanes), lambda i: (0, i, 0))
    whole = lambda lanes, dtype: shape_of((sents, seq, lanes), dtype)
    slots = (nz, 2, 2, nx, sents // 2, 2 * width)
    dma = pltpu.SemaphoreType.DMA
    return pl.pallas_call(
        forward_kernel,
        grid=(4,),
        in_specs=[
            tile(width), tile(width), resident(ow.shape), resident(ob.shape), resident(g1.shape),
            resident(s1.shape), pl.BlockSpec(memory_space=pl.ANY), resident(ub.shape),
            pl.BlockSpec(memory_space=pl.ANY),
            resident(db.shape), resident(g2.shape), resident(s2.shape),
        ],
        out_specs=[
            tile(width), tile(width), tile(width), tile(128), tile(depth), tile(depth), tile(width),
            tile(128), pl.BlockSpec((sents, width), lambda i: (0, 0)), pl.BlockSpec(memory_space=pl.ANY),
        ],
        out_shape=[
            whole(width, BF), whole(width, BF), whole(width, BF), whole(128, F32), whole(depth, BF),
            whole(depth, BF), whole(width, BF), whole(128, F32), shape_of((sents, width), F32),
            shape_of(slots, BF),
        ],
        scratch_shapes=[
            pltpu.VMEM((sents // 2, 2 * width), F32), pltpu.VMEM(uw.shape, BF), pltpu.VMEM(dw.shape, BF), dma((2,)),
            pltpu.VMEM(slots, BF),
            dma((nz - 1,)), dma((nz - 1,)), dma, dma, dma((nx - 1,)), dma((nx - 1,)), dma, dma, dma,
        ],
        compiler_params=params(collective_id=0, has_side_effects=True),
        name="forward",
    )(tokens, ctx.reshape(sents, seq, width), ow, ob, g1, s1, uw, ub, dw, db, g2, s2)


def ranking_kernel(
    all_ref, group_ref, cls_ref, cot_ref, xh2_ref, rs2_ref, g2_ref,
    loss_ref, down_ref, sums_ref, dcls, gcol_ref,
):
    pairs, width = all_ref.shape[0], all_ref.shape[1] // 2
    own = cls_ref.shape[0] // 2
    step = pl.program_id(0)

    @pl.when(step == 0)
    def _():
        first = (lax.axis_index("wide") * lax.axis_size("narrow") + lax.axis_index("narrow")) * own
        strip = min(256, pairs)
        groups = line(group_ref)
        gcol_ref[...] = jnp.transpose(jnp.broadcast_to(groups, (128, pairs)))
        own_rows = pl.ds(pl.multiple_of(first, own), own)

        def logits_of(left, right, start):
            count = left.shape[0]
            same_at = lax.broadcasted_iota(jnp.int32, (count, pairs), 0) + start
            pair_at = lax.broadcasted_iota(jnp.int32, (count, pairs), 1)
            hit = same_at == pair_at
            return nt(left, right) * SCALE - jnp.where(hit, SCALE * MARGIN, 0.0), hit

        def column_lse(left_at, right_at):
            right = all_ref[:, right_at * width : (right_at + 1) * width]

            def strip_step(at, carry):
                top, total, diag = carry
                start = pl.multiple_of(at * strip, strip)
                left = all_ref[pl.ds(start, strip), left_at * width : (left_at + 1) * width]
                logits, hit = logits_of(left, right, start)
                masked = jnp.where(gcol_ref[pl.ds(start, strip), :1] == groups, logits, -1e30)
                peak = jnp.maximum(top, jnp.max(masked, axis=0, keepdims=True))
                total = total * jnp.exp(top - peak) + jnp.sum(jnp.exp(masked - peak), axis=0, keepdims=True)
                diag = diag + jnp.sum(jnp.where(hit, logits, 0.0), axis=0, keepdims=True)
                return peak, total, diag

            start = (jnp.full((1, pairs), -1e30, F32), jnp.zeros((1, pairs), F32), jnp.zeros((1, pairs), F32))
            top, total, diag = lax.fori_loop(0, pairs // strip, strip_step, start)
            return top + jnp.log(total), diag

        col_lse, diag = column_lse(0, 1)
        row_lse, diag_again = column_lse(1, 0)
        loss_ref[...] = jnp.sum(col_lse - diag + row_lse - diag_again, axis=1, keepdims=True) / pairs

        same = gcol_ref[own_rows, :1] == groups

        def side(my_at, other_at, other_lse):
            other = all_ref[:, other_at * width : (other_at + 1) * width]
            mine = all_ref[own_rows, my_at * width : (my_at + 1) * width]
            logits, hit = logits_of(mine, other, first)
            eye = hit.astype(F32)
            masked = jnp.where(same, logits, -1e30)
            e = jnp.exp(masked - jnp.max(masked, axis=1, keepdims=True))
            d_mine = (e / jnp.sum(e, axis=1, keepdims=True) - eye).astype(BF)
            d_other = (jnp.where(same, jnp.exp(masked - other_lse), 0.0) - eye).astype(BF)
            return (nn(d_mine, other) + nn(d_other, other)) * SCALE

        for at, (other, lse) in enumerate(((1, col_lse), (0, row_lse))):
            terms = side(at, other, lse)
            for p in range(own):
                dcls[2 * p + at : 2 * p + at + 1, :] = terms[p : p + 1, :]
        d = dcls[...]
        c = cls_ref[...]
        root = lax.rsqrt(jnp.sum(c * c, -1, keepdims=True) + EPS)
        dcls[...] = root * d - root * root * root * c * jnp.sum(c * d, -1, keepdims=True)
        sums_ref[...] = jnp.zeros_like(sums_ref)

    side_sents, seq, _ = cot_ref.shape
    rows = side_sents * seq
    start = pl.multiple_of(step * side_sents, side_sents)
    extra = dcls[pl.ds(start, side_sents), :]
    at_zero = lax.broadcasted_iota(jnp.int32, (side_sents, seq, width), 1) == 0
    d_final = cot_ref[...].astype(F32) + jnp.where(at_zero, extra[:, None, :], 0.0)
    d_final = d_final.reshape(rows, width)
    xhat = xh2_ref[...].reshape(rows, width).astype(F32)
    root = rs2_ref[...].reshape(rows, 128)[:, :1]
    e = d_final * line(g2_ref)
    d_pre = (e - jnp.mean(e, -1, keepdims=True) - xhat * jnp.mean(e * xhat, -1, keepdims=True)) * root
    d_down = d_pre.astype(BF)
    down_ref[...] = d_down
    sums_ref[0:1, :] += jnp.sum(d_final * xhat, axis=0, keepdims=True)
    sums_ref[1:2, :] += jnp.sum(d_final, axis=0, keepdims=True)
    sums_ref[2:3, :] += jnp.sum(d_down.astype(F32), axis=0, keepdims=True)


def ranking(gathered, groups, cls, cotangent, xh2, rs2, g2):
    sents, seq, width = cotangent.shape
    pairs = gathered.shape[0]
    tile = lambda lanes: pl.BlockSpec((SIDE, seq, lanes), lambda i: (i, 0, 0))
    return pl.pallas_call(
        ranking_kernel,
        grid=(sents // SIDE,),
        in_specs=[
            resident(gathered.shape), resident(groups.shape), resident(cls.shape), tile(width), tile(width), tile(128),
            resident(g2.shape),
        ],
        out_specs=[
            pl.BlockSpec((1, 1), lambda i: (0, 0)),
            pl.BlockSpec((SIDE * seq, width), lambda i: (i, 0)),
            pl.BlockSpec((8, width), lambda i: (0, 0)),
        ],
        out_shape=[shape_of((1, 1), F32), shape_of((sents * seq, width), BF), shape_of((8, width), F32)],
        scratch_shapes=[pltpu.VMEM((sents, width), F32), pltpu.VMEM((pairs, 128), jnp.int32)],
        compiler_params=params(),
        name="ranking",
    )(gathered, groups, cls, cotangent, xh2, rs2, g2)


def copy_to(src, dst, sends, recvs, at, device):
    return pltpu.make_async_remote_copy(
        src_ref=src, dst_ref=dst, send_sem=sends.at[at], recv_sem=recvs.at[at], device_id=device,
        device_id_type=MESH,
    )


def plus(*terms):
    return sum(t.astype(F32) for t in terms).astype(BF)


class Peers:
    def __init__(self, nz):
        self.nz = nz
        wide, self.x, self.z, self.y, self.core = place()
        self.sibling = (wide + 1 - 2 * self.core, self.x)
        self.over_x = (wide, 1 - self.x)
        self.over_y = (wide + 2 - 4 * self.y, self.x)
        self.zs = [lax.rem(self.z + k, nz) for k in range(1, nz)]
        self.over_z = [(lax.rem(wide + 4 * k, 4 * nz), self.x) for k in range(1, nz)]

    def greet(self, devices):
        barrier = pltpu.get_barrier_semaphore()
        for device in devices:
            pl.semaphore_signal(barrier, inc=1, device_id=device, device_id_type=MESH)
        pl.semaphore_wait(barrier, len(devices))


class Stages:
    SEMS = 9

    def __init__(self, peers, terms, got, sends, recvs):
        self.peers, self.terms, self.got, self.sends, self.recvs = peers, terms, got, sends, recvs
        self.third = got["xa"].shape[2]

    @staticmethod
    def scratch(nz, rows, cols):
        third = rows // 3
        return {
            "xa": (nz, 2, third, cols), "yb": (2, nz, rows - third, cols),
            "ya": (nz, third, cols), "xb": (nz, rows - third, cols),
        }

    def first(self):
        p, t = self.peers, self.third
        return [
            copy_to(self.terms.at[1 - p.x, :, :, :t], self.got["xa"], self.sends, self.recvs, 1, p.over_x),
            copy_to(self.terms.at[:, :, 1 - p.y, t:], self.got["yb"], self.sends, self.recvs, 2, p.over_y),
        ]

    def second(self):
        p, t = self.peers, self.third
        return [
            copy_to(self.terms.at[p.x, :, 1 - p.y, :t], self.got["ya"], self.sends, self.recvs, 3, p.over_y),
            copy_to(self.terms.at[1 - p.x, :, p.y, t:], self.got["xb"], self.sends, self.recvs, 4, p.over_x),
        ]

    def add_first(self):
        p, t = self.peers, self.third
        for copy in self.first():
            copy.wait()
        self.terms[p.x, :, :, :t] = plus(self.terms[p.x, :, :, :t], self.got["xa"][...])
        for h in range(2):
            self.terms[h, :, p.y, t:] = plus(self.terms[h, :, p.y, t:], self.got["yb"][h])

    def add_second(self):
        p, t = self.peers, self.third
        for copy in self.second():
            copy.wait()
        self.terms[p.x, :, p.y, :t] = plus(self.terms[p.x, :, p.y, :t], self.got["ya"][...])
        self.terms[p.x, :, p.y, t:] = plus(self.terms[p.x, :, p.y, t:], self.got["xb"][...])


class Finish:
    def __init__(self, peers, shard, got_z, mine, other, sends, recvs):
        self.peers, self.shard, self.got_z, self.mine, self.other = peers, shard, got_z, mine, other
        self.sends, self.recvs = sends, recvs

    def along_z(self):
        p = self.peers
        return [
            copy_to(self.shard(to), self.got_z.at[k], self.sends, self.recvs, 5 + k, device)
            for k, (to, device) in enumerate(zip(p.zs, p.over_z, strict=True))
        ]

    def along_x(self):
        return copy_to(self.mine, self.other, self.sends, self.recvs, 8, self.peers.over_x)

    def add(self):
        for copy in self.along_z():
            copy.wait()
        got = [self.got_z[k] for k in range(self.peers.nz - 1)]
        self.mine[...] = plus(self.shard(self.peers.z)[...], *got)


def hand_out(value, keep, send):
    halves, nz, ny, rows, cols = keep.shape
    core = lax.axis_index("wide") % 2
    for z in range(nz):
        for y in range(ny):
            first = (z * ny + y) * 2 * rows
            for ref, side in ((keep, core), (send, 1 - core)):
                part = value[pl.ds(pl.multiple_of(first + side * rows, rows), rows), :].astype(BF)
                for h in range(halves):
                    ref[h, z, y] = part[:, h * cols : (h + 1) * cols]


def backward_kernel(fused, nz, *refs):
    (down_ref, hid_ref, slope_ref, dw_hbm, uw_hbm, xh1_ref, rs1_ref, g1_ref, ow_ref, actx_ref) = refs[:10]
    (up_ref, attn_ref, ctx_ref, sums_ref, upsum_ref, owg_ref, dwg_ref) = refs[10:17]
    dw_ref, uw_ref, w_sems, owg, *comm = refs[17:]
    blocks = 4
    width = down_ref.shape[1]
    rows, depth = slope_ref.shape
    step = pl.program_id(0)
    weights = [
        pltpu.make_async_copy(dw_hbm, dw_ref, w_sems.at[0]), pltpu.make_async_copy(uw_hbm, uw_ref, w_sems.at[1])
    ]

    if fused:
        terms, send, got, xa, yb, ya, xb, c_send, c_recv, s_send, s_recv = comm
        peers = Peers(nz)
        stages = Stages(peers, terms, {"xa": xa, "yb": yb, "ya": ya, "xb": xb}, s_send, s_recv)

        def exchange(i):
            return copy_to(send.at[i % 2], got.at[i % 2], c_send, c_recv, i, peers.sibling)

    @pl.when(step == 0)
    def _():
        for copy in weights:
            copy.start()
        sums_ref[...] = jnp.zeros_like(sums_ref)
        upsum_ref[...] = jnp.zeros_like(upsum_ref)
        if fused:
            peers.greet([peers.sibling, peers.over_x, peers.over_y])

    def settle(i):
        exchange(i).wait()
        for h in range(2):
            terms[h, i] = plus(terms[h, i], got[i % 2, h, 0])

    @pl.when(step < blocks)
    def _():
        value = tn(hid_ref[...], down_ref[...])
        if fused:

            @pl.when(step > 0)
            def _():
                settle(step - 1)

            owg[...] = value
            hand_out(owg, terms.at[:, pl.ds(step, 1)], send.at[step % 2])
            exchange(step).start()

        else:
            dwg_ref[...] = value.astype(BF)

    @pl.when(step == blocks)
    def _():
        for copy in weights:
            copy.wait()

    @pl.when(step >= blocks)
    def _():
        d_down = down_ref[pl.ds(pl.multiple_of((step - blocks) * rows, rows), rows), :]
        total = d_down.astype(F32)
        for c in range(depth // width):
            cols = slice(c * width, (c + 1) * width)
            d_up = (nt(d_down, dw_ref[cols, :]) * slope_ref[:, cols].astype(F32)).astype(BF)
            up_ref[:, cols] = d_up
            upsum_ref[:, cols] += jnp.sum(d_up.astype(F32), axis=0, keepdims=True)
            total = total + nt(d_up, uw_ref[:, cols])
        xhat = xh1_ref[...].astype(F32)
        root = rs1_ref[:, :1]
        e = total * g1_ref[...].reshape(1, width)
        d_pre = (e - jnp.mean(e, -1, keepdims=True) - xhat * jnp.mean(e * xhat, -1, keepdims=True)) * root
        d_attn = d_pre.astype(BF)
        attn_ref[...] = d_attn
        ctx_ref[...] = nt(d_attn, ow_ref[...]).astype(BF)
        sums_ref[0:1, :] += jnp.sum(total * xhat, axis=0, keepdims=True)
        sums_ref[1:2, :] += jnp.sum(total, axis=0, keepdims=True)
        sums_ref[2:3, :] += jnp.sum(d_attn.astype(F32), axis=0, keepdims=True)
        part = tn(actx_ref[...], d_attn)

        @pl.when(step == blocks)
        def _():
            owg[...] = part

        @pl.when(step > blocks)
        def _():
            owg[...] += part

    if fused:

        @pl.when(step == blocks)
        def _():
            settle(blocks - 1)
            for copy in stages.first():
                copy.start()

        @pl.when(step == blocks + 2)
        def _():
            stages.add_first()
            for copy in stages.second():
                copy.start()

    @pl.when(step == pl.num_programs(0) - 1)
    def _():
        if fused:
            hand_out(owg, owg_ref.at[0], owg_ref.at[1])
            stages.add_second()
            dwg_ref[...] = terms[peers.x, :, peers.y]
        else:
            owg_ref[...] = owg[...].astype(BF)


def backward(d_down, hidden, slope, dw, uw, xh1, rs1, g1, ow, ctx, sizes):
    fused = sizes == (16, 2)
    nz = sizes[0] // 4
    rows, width = d_down.shape
    depth = uw.shape[1]
    side = rows // 4
    tile = lambda lanes: pl.BlockSpec((side, lanes), lambda i: (jnp.maximum(i - 4, 0), 0))
    once = lambda *shape: pl.BlockSpec(shape, lambda i: (0,) * len(shape))
    shard = depth // sizes[0]
    half = width // 2
    dma = pltpu.SemaphoreType.DMA
    scratch = [
        pltpu.VMEM(dw.shape, BF), pltpu.VMEM(uw.shape, BF), dma((2,)), pltpu.VMEM((width, width), F32)
    ]
    if fused:
        scratch += [
            pltpu.VMEM((2, nz, 2, shard, half), BF), pltpu.VMEM((2, 2, 1, 2, shard, half), BF),
            pltpu.VMEM((2, 2, 1, 2, shard, half), BF),
        ]
        scratch += [pltpu.VMEM(s, BF) for s in Stages.scratch(nz, shard, half).values()]
        scratch += [dma((4,)), dma((4,)), dma((Stages.SEMS,)), dma((Stages.SEMS,))]
        dwg_spec, dwg_shape = once(nz, shard, half), (nz, shard, half)
        owg_shape = (2, 2, nz, 2, width // sizes[0], half)
        extra = dict(collective_id=1, has_side_effects=True)
    else:
        dwg_spec, dwg_shape = pl.BlockSpec((width, width), lambda i: (jnp.minimum(i, 3), 0)), (depth, width)
        owg_shape = (width, width)
        extra = {}
    return pl.pallas_call(
        functools.partial(backward_kernel, fused, nz),
        grid=(8,),
        in_specs=[
            resident((rows, width)), pl.BlockSpec((rows, width), lambda i: (0, jnp.minimum(i, 3))), tile(depth),
            pl.BlockSpec(memory_space=pl.ANY), pl.BlockSpec(memory_space=pl.ANY), tile(width), tile(128),
            resident(g1.shape), resident(ow.shape), tile(width),
        ],
        out_specs=[
            tile(depth), tile(width), tile(width), once(8, width), once(1, depth), once(*owg_shape), dwg_spec
        ],
        out_shape=[
            shape_of((rows, depth), BF), shape_of((rows, width), BF), shape_of((rows, width), BF),
            shape_of((8, width), F32), shape_of((1, depth), F32), shape_of(owg_shape, BF),
            shape_of(dwg_shape, BF),
        ],
        scratch_shapes=scratch,
        compiler_params=params(**extra),
        name="backward",
    )(d_down, hidden, slope, dw, uw, xh1, rs1, g1, ow, ctx)


UPS, QUADS, TILES = 4, 3, 4
FIRST_QUAD = UPS
FIRST_INPUT = UPS + QUADS * TILES
STEPS = FIRST_INPUT + TILES
OUT_PIECE, UP_PIECE, QUAD_PIECE = 0, 1, 1 + UPS
PIECES = UPS + 1 + QUADS
VECTORS = 16


def tail_kernel(fused, nz, *refs):
    (low_ref, up_ref, q_ref, k_ref, v_ref, dctx_ref, p_ref, x_ref, w_hbm, owg_ref, dsum_ref,
     one_ref, two_ref, upsum_ref) = refs[:14]
    out_ref, vec_out = refs[14:16]
    if fused:
        outs = refs[16:20]
        w_ref, w_sem, dqkv, acc, vec, *comm = refs[20:]
    else:
        upg_ref, qkvg_ref = refs[16:18]
        w_ref, w_sem, dqkv, acc, vec = refs[18:]
    rows, quad = q_ref.shape
    sents, seq, _ = p_ref.shape
    width = acc.shape[0]
    step = pl.program_id(0)
    weight = pltpu.make_async_copy(w_hbm, w_ref, w_sem)
    at_quad = jnp.clip(step - FIRST_QUAD, 0, QUADS * TILES - 1)
    g, tile = at_quad // TILES, at_quad % TILES

    if fused:
        (mine, other, dmine, dother, terms, send, got, xa, yb, ya, xb, gz, dz, vlow, vgot, sends, recvs, d_sends, d_recvs,
         v_sends, v_recvs) = comm
        peers = Peers(nz)
        down = Finish(peers, lambda at: dsum_ref.at[at], dz, dmine, dother, d_sends, d_recvs)

        def stages_of(n):
            return Stages(
                peers, terms.at[n], {"xa": xa.at[n], "yb": yb.at[n], "ya": ya.at[n], "xb": xb.at[n]}, sends.at[n],
                recvs.at[n],
            )

        def finish_of(n):
            return Finish(
                peers, lambda at: terms.at[n, peers.x, at, peers.y], gz.at[n], mine.at[n], other.at[n],
                sends.at[n], recvs.at[n],
            )

        def chip(n):
            return copy_to(send.at[n % 2], got.at[n % 2], sends.at[n], recvs.at[n], 0, peers.sibling)

        def add_chip(n):
            chip(n).wait()
            for h in range(2):
                terms[n, h] = plus(terms[n, h], got[n % 2, h])
            for copy in stages_of(n).first():
                copy.start()

        def add_first(n):
            stages_of(n).add_first()
            for copy in stages_of(n).second():
                copy.start()

        def add_second(n):
            stages_of(n).add_second()
            for copy in finish_of(n).along_z():
                copy.start()

        def add_z(n):
            finish_of(n).add()
            finish_of(n).along_x().start()

        def last(n):
            finish_of(n).along_x().wait()

        usual, hurried = (1, 3, 5, 7, 8), (1, 2, 3, 4, STEPS)
        ready = [*range(-1, UPS)] + [FIRST_QUAD + TILES * (q + 1) - 1 for q in range(QUADS)]

        def settle():
            for stage, action in enumerate((add_chip, add_first, add_second, add_z, last)):
                at = [t + (hurried if n == PIECES - 1 else usual)[stage] for n, t in enumerate(ready)]
                due, piece = step == at[0], jnp.int32(0)
                for n in range(1, PIECES):
                    due = due | (step == at[n])
                    piece = jnp.where(step == at[n], n, piece)
                pl.when(due)(functools.partial(action, piece))

        def vector_copy(n, device):
            return copy_to(vlow, vgot.at[n], v_sends, v_recvs, n, device)

        routes = [[peers.sibling], [peers.over_x], [peers.over_y], peers.over_z]

        def vector_copies(hop):
            return [vector_copy(hop + k, device) for k, device in enumerate(routes[hop])]

        @pl.when(step == 0)
        def _():
            peers.greet([peers.sibling, peers.over_x, peers.over_y, *peers.over_z])
            for copy in down.along_z():
                copy.start()
            for h in range(2):
                terms[OUT_PIECE, h] = owg_ref[0, h]
                send[OUT_PIECE, h] = owg_ref[1, h]
            chip(OUT_PIECE).start()

    @pl.when(step == 0)
    def _():
        weight.start()
        vec[...] = jnp.zeros_like(vec)
        vec[2:3, :] = one_ref[2:3, :]
        vec[3:5, :] = one_ref[0:2, :]
        vec[5:6, :] = two_ref[2:3, :]
        vec[6:8, :] = two_ref[0:2, :]
        for c in range(UPS):
            vec[8 + c : 9 + c, :] = upsum_ref[:, c * width : (c + 1) * width]

    @pl.when(step < UPS)
    def _():
        value = tn(low_ref[...], up_ref[...])
        if fused:
            acc[...] = value
        else:
            upg_ref[...] = value.astype(BF)

    @pl.when((step >= FIRST_QUAD) & (step < FIRST_INPUT))
    def _():
        mask = head_mask(quad)
        scale = (quad // QUAD) ** -0.5
        here = lambda size, s=0: pl.ds(pl.multiple_of(tile * rows + s * seq, seq), size)
        for s in range(sents):
            at = slice(s * seq, (s + 1) * seq)
            k = k_ref[at, :]
            p_low = p_ref[s]
            p = p_low.astype(F32)
            dctx = blocked(dctx_ref[at, :], mask)
            d_probs = nt(v_ref[at, :], dctx)
            d_scores = (p * (d_probs - jnp.sum(p * d_probs, axis=0, keepdims=True))).astype(BF)
            dqkv[g, here(seq, s), :quad] = (paired(d_scores, k, seq) * scale).astype(BF)
            dqkv[g, here(seq, s), quad : 2 * quad] = (nn(d_scores, blocked(q_ref[at, :], mask)) * scale).astype(BF)
            dqkv[g, here(seq, s), 2 * quad :] = nn(p_low, dctx).astype(BF)
        grads = dqkv[g, here(rows), :]
        part = tn(x_ref[...], grads)
        q_sum = jnp.sum(grads[:, :quad].astype(F32), axis=0, keepdims=True)
        v_sum = jnp.sum(grads[:, 2 * quad :].astype(F32), axis=0, keepdims=True)
        for q in range(QUADS):

            @pl.when(g == q)
            def _(q=q):
                vec[0:1, q * quad : (q + 1) * quad] += q_sum
                vec[1:2, q * quad : (q + 1) * quad] += v_sum

        @pl.when(tile == 0)
        def _():
            acc[...] = part

        @pl.when(tile > 0)
        def _():
            acc[...] += part

    if fused:
        settle()
        done_quad = (step >= FIRST_QUAD) & (step < FIRST_INPUT) & (tile == TILES - 1)

        @pl.when((step < UPS) | done_quad)
        def _():
            n = jnp.where(step < UPS, UP_PIECE + step, QUAD_PIECE + g)
            hand_out(acc, terms.at[n], send.at[n % 2])
            chip(n).start()

        @pl.when(step == FIRST_INPUT - 1)
        def _():
            vlow[...] = vec[...].astype(BF)
            for copy in vector_copies(0):
                copy.start()

        for hop in range(4):

            @pl.when(step == FIRST_INPUT + hop)
            def _(hop=hop):
                for copy in vector_copies(hop):
                    copy.wait()
                vec[...] = vlow[...].astype(F32) + sum(vgot[hop + k].astype(F32) for k in range(len(routes[hop])))
                if hop < 3:
                    vlow[...] = vec[...].astype(BF)
                    for copy in vector_copies(hop + 1):
                        copy.start()

        @pl.when(step == 4)
        def _():
            down.add()
            down.along_x().start()

        @pl.when(step == 7)
        def _():
            down.along_x().wait()

    else:

        @pl.when((step >= FIRST_QUAD) & (step < FIRST_INPUT) & (tile == TILES - 1))
        def _():
            qkvg_ref[...] = acc[...].astype(BF)

    @pl.when(step == FIRST_INPUT)
    def _():
        weight.wait()

    @pl.when(step >= FIRST_INPUT)
    def _():
        here = pl.ds(pl.multiple_of((step - FIRST_INPUT) * rows, rows), rows)
        grads = jnp.concatenate(
            [dqkv[q, here, part * quad : (part + 1) * quad] for part in range(3) for q in range(QUADS)], axis=1
        )
        out_ref[...] = nt(grads, w_ref[...]).astype(BF)

    @pl.when(step == STEPS - 1)
    def _():
        if fused:
            last(PIECES - 1)
        vec_out[...] = vec[...]
        if fused:
            for ref, value in zip(outs, (mine, other, dmine, dother), strict=True):
                ref[...] = value[...]


def tail(low, d_up, qkv, d_ctx, probs, token_rows, qkv_weight, owg, dsum, one, two, upsum, sizes):
    fused = sizes == (16, 2)
    nz = sizes[0] // 4
    sents, seq, width = probs.shape
    rows = sents * seq
    side = rows // TILES
    quad = width // QUADS
    shard, half = width // sizes[0], width // 2
    at = lambda i: jnp.clip(i - FIRST_QUAD, 0, QUADS * TILES - 1)
    cols = lambda part: pl.BlockSpec((side, quad), lambda i: (at(i) % TILES, part * QUADS + at(i) // TILES))
    once = lambda *shape: pl.BlockSpec(shape, lambda i: (0,) * len(shape))
    finish = lambda lanes: pl.BlockSpec((side, lanes), lambda i: (jnp.maximum(i - FIRST_INPUT, 0), 0))
    dma = pltpu.SemaphoreType.DMA
    scratch = [
        pltpu.VMEM(qkv_weight.shape, BF), dma, pltpu.VMEM((QUADS, rows, width), BF),
        pltpu.VMEM((width, width), F32), pltpu.VMEM((VECTORS, width), F32),
    ]
    out_specs = [finish(width), once(VECTORS, width)]
    out_shape = [shape_of((rows, width), BF), shape_of((VECTORS, width), F32)]
    if fused:
        piece = (2, nz, 2, shard, half)
        scratch += [pltpu.VMEM((PIECES, shard, half), BF)] * 2 + [pltpu.VMEM(dsum.shape[1:], BF)] * 2
        scratch += [pltpu.VMEM((PIECES, *piece), BF), pltpu.VMEM((2, *piece), BF), pltpu.VMEM((2, *piece), BF)]
        scratch += [pltpu.VMEM((PIECES, *s), BF) for s in Stages.scratch(nz, shard, half).values()]
        scratch += [
            pltpu.VMEM((PIECES, nz - 1, shard, half), BF), pltpu.VMEM((nz - 1, *dsum.shape[1:]), BF),
            pltpu.VMEM((VECTORS, width), BF), pltpu.VMEM((2 + nz, VECTORS, width), BF),
        ]
        scratch += [dma((PIECES, Stages.SEMS))] * 2 + [dma((Stages.SEMS,))] * 2 + [dma((2 + nz,))] * 2
        out_specs += [once(PIECES, shard, half)] * 2 + [once(*dsum.shape[1:])] * 2
        out_shape += [shape_of((PIECES, shard, half), BF)] * 2 + [shape_of(dsum.shape[1:], BF)] * 2
        extra = dict(collective_id=2, has_side_effects=True)
    else:
        out_specs += [
            pl.BlockSpec((width, width), lambda i: (0, jnp.minimum(i, UPS - 1))),
            pl.BlockSpec((width, width), lambda i: (0, at(i) // TILES)),
        ]
        out_shape += [shape_of((width, UPS * width), BF), shape_of((width, QUADS * width), BF)]
        extra = {}
    return pl.pallas_call(
        functools.partial(tail_kernel, fused, nz),
        grid=(STEPS,),
        in_specs=[
            resident((rows, width)), pl.BlockSpec((rows, width), lambda i: (0, jnp.minimum(i, UPS - 1))),
            cols(0), cols(1), cols(2), cols(0),
            pl.BlockSpec((SIDE, seq, quad), lambda i: (at(i) % TILES, 0, at(i) // TILES)),
            pl.BlockSpec((side, width), lambda i: (at(i) % TILES, 0)),
            pl.BlockSpec(memory_space=pl.ANY), resident(owg.shape), resident(dsum.shape), resident(one.shape),
            resident(two.shape), resident(upsum.shape),
        ],
        out_specs=out_specs,
        out_shape=out_shape,
        scratch_shapes=scratch,
        compiler_params=params(**extra),
        name="tail",
    )(low, d_up, qkv, qkv, qkv, d_ctx, probs, token_rows, qkv_weight, owg, dsum, one, two, upsum)


def finish_kernel(fused, part_ref, attn_ref, *refs):
    if not fused:
        (input_ref,) = refs
    else:
        (mine_ref, other_ref, dmine_ref, dother_ref, vec_ref, input_ref, qkv_ref, qb_ref, vb_ref, out_ref, ob_ref,
         g1_ref, s1_ref, up_ref, ub_ref, down_ref, db_ref, g2_ref, s2_ref) = refs
    input_ref[...] = part_ref[...].astype(F32) + attn_ref[...].astype(F32)
    if not fused:
        return

    @pl.when(pl.program_id(0) == 0)
    def _():
        wide, narrow, z, _, _ = place()
        width = vec_ref.shape[1]
        shard = qb_ref.shape[0]

        def whole(mine, other):
            mine, other = mine.astype(F32), other.astype(F32)
            return jnp.concatenate([jnp.where(narrow == 0, mine, other), jnp.where(narrow == 0, other, mine)], axis=-1)

        for n in range(UPS):
            up_ref[:, n * width : (n + 1) * width] = whole(mine_ref[UP_PIECE + n], other_ref[UP_PIECE + n])
        out_ref[...] = whole(mine_ref[OUT_PIECE], other_ref[OUT_PIECE])
        quad = width // QUADS
        for q in range(QUADS):
            block = whole(mine_ref[QUAD_PIECE + q], other_ref[QUAD_PIECE + q])
            for part in range(3):
                to = part * width + q * quad
                qkv_ref[:, to : to + quad] = block[:, part * quad : (part + 1) * quad]
        down_ref[...] = whole(dmine_ref[...], dother_ref[...])
        rolled = pltpu.roll(vec_ref[...], lax.rem(width - wide * shard, width), 1)
        for n, ref in enumerate((qb_ref, vb_ref, ob_ref, g1_ref, s1_ref, db_ref, g2_ref, s2_ref)):
            ref[...] = rolled[n, :shard]
        depth = ub_ref.shape[0]
        ups = jnp.concatenate([vec_ref[pl.ds(8 + z, 1), :]] * 8, axis=0)
        ub_ref[...] = pltpu.roll(ups, lax.rem(width - lax.rem(wide, 4) * depth, width), 1)[0, :depth]


def finish(part, d_attn, sums, sizes, depth):
    fused = bool(sums)
    rows, width = part.shape
    side = rows // TILES
    shard = width // sizes[0]
    tile = pl.BlockSpec((side, width), lambda i: (i, 0))
    shapes = [(rows, width)]
    if fused:
        up = depth // sizes[0]
        vector = (shard,)
        shapes += [
            (shard, 3 * width), vector, vector, (shard, width), vector, vector, vector, (shard, depth), (up,),
            (up, width), vector, vector, vector,
        ]
    return pl.pallas_call(
        functools.partial(finish_kernel, fused),
        grid=(TILES,),
        in_specs=[tile, tile] + [resident(a.shape) for a in sums],
        out_specs=[tile] + [pl.BlockSpec(s, lambda i, n=len(s): (0,) * n) for s in shapes[1:]],
        out_shape=[shape_of(s, F32) for s in shapes],
        compiler_params=params(),
        name="finish",
    )(part, d_attn, *sums)


def per_device(
    sizes, tokens, cotangent, groups, qkv_weight, query_bias, value_bias, out_weight, out_bias, gain_one,
    shift_one, up_weight, up_bias, down_weight, down_bias, gain_two, shift_two,
):
    n_wide, n_narrow = sizes
    sents, seq, width = tokens.shape
    depth = up_weight.shape[1]
    rows = sents * seq
    flat = lambda v: v.reshape(rows, v.shape[-1])

    qkv, probs, ctx = attend(tokens, qkv_weight, query_bias, value_bias)
    block_out, low, xh1, rs1, hidden, slope, xh2, rs2, cls, slots = forward(
        tokens, ctx, out_weight, out_bias, gain_one, shift_one, up_weight, up_bias, down_weight, down_bias,
        gain_two, shift_two, sizes,
    )
    gathered = slots.reshape(n_wide * n_narrow * (sents // 2), 2 * width)
    loss, d_down, sums_two = ranking(gathered, groups, cls, cotangent, xh2, rs2, gain_two)
    d_up, d_attn, d_ctx, sums_one, up_sum, out_terms, down_terms = backward(
        d_down, flat(hidden), flat(slope), down_weight, up_weight, flat(xh1), flat(rs1), gain_one, out_weight,
        ctx, sizes,
    )
    part, vectors, *sums = tail(
        flat(low), d_up, qkv, d_ctx, probs, flat(tokens), qkv_weight, out_terms, down_terms, sums_one, sums_two,
        up_sum, sizes,
    )
    if sizes == (16, 2):
        input_grad, *grads = finish(part, d_attn, [*sums, vectors], sizes, depth)
    else:
        (input_grad,) = finish(part, d_attn, [], sizes, depth)
        up_terms, qkv_terms = sums
        quad = width // QUADS
        qkv_terms = qkv_terms.reshape(width, QUADS, 3, quad).transpose(0, 2, 1, 3).reshape(width, 3 * width)
        total = lambda v: lax.psum(
            lax.psum_scatter(v, "wide", scatter_dimension=0, tiled=True).astype(F32), "narrow"
        )
        vector = lambda n: total(vectors[n])
        grads = (
            total(qkv_terms), vector(0), vector(1), total(out_terms), vector(2), vector(3), vector(4),
            total(up_terms), total(vectors[8 : 8 + UPS].reshape(-1)), total(down_terms), vector(5), vector(6),
            vector(7),
        )
    return (loss.reshape(()), block_out, input_grad.reshape(sents, seq, width), *grads)


def solution(mesh):
    sizes = (mesh.shape["wide"], mesh.shape["narrow"])
    split = P(("wide", "narrow"), None, None)
    matrix, vector = P("wide", None), P("wide")
    return jax.shard_map(
        functools.partial(per_device, sizes),
        mesh=mesh,
        in_specs=(split, split) + (P(),) * 14,
        out_specs=(
            P(), split, split, matrix, vector, vector, matrix, vector, vector, vector, matrix, vector,
            matrix, vector, vector, vector,
        ),
        check_vma=False,
    )
```

```python
import functools

import jax
import jax.numpy as jnp
from jax import lax
from jax.experimental import pallas as pl
from jax.experimental.pallas import tpu as pltpu
from jax.sharding import PartitionSpec as P

BF = jnp.bfloat16
F32 = jnp.float32
MESH = pl.DeviceIdType.MESH

HEADS = 12
QUAD = 4
SCALE = 40.0
MARGIN = 0.3
EPS = 1e-06
SIDE = 8
VMEM_BYTES = 60 * 2**20


def nn(a, b):
    return lax.dot_general(a, b, (((1,), (0,)), ((), ())), preferred_element_type=F32)


def nt(a, b):
    return lax.dot_general(a, b, (((1,), (1,)), ((), ())), preferred_element_type=F32)


def tn(a, b):
    return lax.dot_general(a, b, (((0,), (0,)), ((), ())), preferred_element_type=F32)


def params(**more):
    return pltpu.CompilerParams(vmem_limit_bytes=VMEM_BYTES, **more)


def resident(shape):
    return pl.BlockSpec(shape, lambda *_: (0,) * len(shape), pipeline_mode=pl.Buffered(1))


def shape_of(shape, dtype):
    return jax.ShapeDtypeStruct(shape, dtype)


def head_mask(quad):
    head = quad // QUAD
    at = lambda axis: lax.broadcasted_iota(jnp.int32, (quad, quad), axis) // head
    return (at(0) == at(1)).astype(F32).astype(BF)


def line(ref):
    return ref[...].reshape(1, ref.shape[0])


def blocked(rows, mask):
    return jnp.concatenate([rows] * QUAD, axis=0) * mask


def diagonal(full, seq):
    half = full.shape[1] // 2
    lane = lax.broadcasted_iota(jnp.int32, (seq, half), 1) < half // 2
    left = jnp.where(lane, full[:seq, :half], full[seq : 2 * seq, :half])
    right = jnp.where(lane, full[2 * seq : 3 * seq, half:], full[3 * seq :, half:])
    return jnp.concatenate([left, right], axis=1)


def paired(left, right, seq):
    half = left.shape[1] // 2
    lane = lax.broadcasted_iota(jnp.int32, (seq, half), 1) < half // 2
    parts = []
    for at in (slice(0, half), slice(half, 2 * half)):
        full = tn(left[:, at], right[:, at])
        parts.append(jnp.where(lane, full[:seq], full[seq:]))
    return jnp.concatenate(parts, axis=1)


def attend_kernel(x_ref, w_ref, qb_ref, vb_ref, qkv_ref, p_ref, ctx_ref):
    sents, seq, width = x_ref.shape
    rows = x_ref[...].reshape(sents * seq, width)
    quad = width // QUADS
    for part, bias in ((0, qb_ref), (1, None), (2, vb_ref)):
        cols = slice(part * width, (part + 1) * width)
        y = nn(rows, w_ref[:, cols])
        if bias is not None:
            y = y + line(bias)
        qkv_ref[:, cols] = y.astype(BF)
    mask = head_mask(quad)
    scale = (width // HEADS) ** -0.5
    for s in range(sents):
        at = slice(s * seq, (s + 1) * seq)
        for g in range(width // quad):
            q = qkv_ref[at, g * quad : (g + 1) * quad]
            k = qkv_ref[at, width + g * quad : width + (g + 1) * quad]
            v = qkv_ref[at, 2 * width + g * quad : 2 * width + (g + 1) * quad]
            scores = nt(k, blocked(q, mask)) * scale
            e = jnp.exp(scores - jnp.max(scores, axis=0, keepdims=True))
            p = (e * (1.0 / jnp.sum(e, axis=0, keepdims=True))).astype(BF)
            p_ref[s, :, g * quad : (g + 1) * quad] = p
            ctx_ref[at, g * quad : (g + 1) * quad] = diagonal(tn(p, v), seq).astype(BF)


def attend(tokens, qkv_weight, query_bias, value_bias):
    sents, seq, width = tokens.shape
    rows = sents * seq
    side = SIDE * seq
    return pl.pallas_call(
        attend_kernel,
        grid=(sents // SIDE,),
        in_specs=[
            pl.BlockSpec((SIDE, seq, width), lambda i: (i, 0, 0)),
            resident((width, 3 * width)),
            resident((width,)),
            resident((width,)),
        ],
        out_specs=[
            pl.BlockSpec((side, 3 * width), lambda i: (i, 0)),
            pl.BlockSpec((SIDE, seq, width), lambda i: (i, 0, 0)),
            pl.BlockSpec((side, width), lambda i: (i, 0)),
        ],
        out_shape=[
            shape_of((rows, 3 * width), BF),
            shape_of((sents, seq, width), BF),
            shape_of((rows, width), BF),
        ],
        compiler_params=params(),
        name="attend",
    )(tokens, qkv_weight, query_bias, value_bias)


def norm(values):
    mean = jnp.mean(values, -1, keepdims=True)
    centred = values - mean
    root = lax.rsqrt(jnp.mean(centred * centred, -1, keepdims=True) + EPS)
    return centred * root, root


def place():
    wide, narrow = lax.axis_index("wide"), lax.axis_index("narrow")
    return wide, narrow, wide // 4, (wide // 2) % 2, wide % 2


def forward_kernel(
    x_ref, ctx_ref, ow_ref, ob_ref, g1_ref, s1_ref, uw_hbm, ub_ref, dw_hbm, db_ref, g2_ref, s2_ref,
    low_ref, xh1_ref, rs1_ref, hid_ref, slope_ref, xh2_ref, rs2_ref, cls_ref, all_ref,
    rows_ref, uw_ref, dw_ref, w_sems, buf, zs, zr, ys, yr, xs, xr, cs, cr, done,
):
    sents, part, width = x_ref.shape
    depth = uw_ref.shape[1]
    rows = sents * part
    step = pl.program_id(0)
    wide, narrow, z, y, core = place()
    nz, nx = buf.shape[1], buf.shape[4]
    wide_of = lambda a, b, c: (a * 2 + b) * 2 + c
    z_peers = [(lax.rem(z + k, nz), k) for k in range(1, nz)]
    x_peers = [(lax.rem(narrow + k, nx), k) for k in range(1, nx)]

    def gather_copy(slots, sems, at, device):
        return pltpu.make_async_remote_copy(
            src_ref=buf.at[slots], dst_ref=buf.at[slots], send_sem=sems[0].at[at], recv_sem=sems[1].at[at],
            device_id=device, device_id_type=MESH,
        )

    every = slice(None)
    z_copies = [
        gather_copy((every, z, y, core, narrow), (zs, zr), k - 1, (wide_of(to, y, core), narrow))
        for to, k in z_peers
    ]

    def over_y(half, xs_held, at):
        return gather_copy((half, every, y, core, xs_held), (ys, yr), at, (wide_of(z, 1 - y, core), narrow))

    def over_x(half, ys_held, first):
        return [
            gather_copy((half, every, ys_held, core, narrow), (xs, xr), first + k - 1, (wide, to)) for to, k in x_peers
        ]

    second = [over_y(0, narrow, 0), *over_x(1, y, 0)]
    third = [*over_x(0, every, nx - 1), over_y(1, every, 1)]
    core_copy = gather_copy((every, every, every, core), (cs, cr), 0, (wide_of(z, y, 1 - core), narrow))

    barrier = pltpu.get_barrier_semaphore()
    weights = [
        pltpu.make_async_copy(uw_hbm, uw_ref, w_sems.at[0]), pltpu.make_async_copy(dw_hbm, dw_ref, w_sems.at[1])
    ]

    @pl.when(step == 0)
    def _():
        for copy in weights:
            copy.start()
        for to, _ in z_peers:
            pl.semaphore_signal(barrier, inc=1, device_id=(wide_of(to, y, core), narrow), device_id_type=MESH)
        pl.semaphore_signal(barrier, inc=1, device_id=(wide_of(z, 1 - y, core), narrow), device_id_type=MESH)
        for to, _ in x_peers:
            pl.semaphore_signal(barrier, inc=1, device_id=(wide, to), device_id_type=MESH)
        pl.semaphore_signal(barrier, inc=1, device_id=(wide_of(z, y, 1 - core), narrow), device_id_type=MESH)

    block = lambda ref: ref[...].reshape(rows, ref.shape[2])

    def put(ref, value):
        ref[...] = value.astype(ref.dtype).reshape(ref.shape)

    pre_one = block(x_ref).astype(F32) + nn(block(ctx_ref), ow_ref[...]) + line(ob_ref)
    xh1, rs1 = norm(pre_one)
    normed = xh1 * line(g1_ref) + line(s1_ref)
    low = normed.astype(BF)
    put(low_ref, low)
    put(xh1_ref, xh1)
    put(rs1_ref, jnp.broadcast_to(rs1, (rows, 128)))
    total = normed + line(db_ref)

    @pl.when(step == 0)
    def _():
        for copy in weights:
            copy.wait()

    for c in range(depth // width):
        if c == 2:

            @pl.when(step == 0)
            def _():
                pl.semaphore_wait(barrier, nz + nx)

            @pl.when(step == 2)
            def _():
                for copy in second:
                    copy.wait()
                for copy in third:
                    copy.start()

            @pl.when(step == 3)
            def _():
                for copy in third:
                    copy.wait()
                core_copy.start()

        cols = slice(c * width, (c + 1) * width)
        up = nn(low, uw_ref[:, cols]) + ub_ref[cols].reshape(1, width)
        cdf = 0.5 * (lax.erf(up * 0.7071067811865476) + 1.0)
        slope = cdf + up * (0.3989422804014327 * jnp.exp(-0.5 * up * up))
        hidden = (up * cdf).astype(BF)
        hid_ref[:, :, cols] = hidden.reshape(sents, part, width)
        slope_ref[:, :, cols] = slope.astype(BF).reshape(sents, part, width)
        total = total + nn(hidden, dw_ref[cols, :])
    xh2, rs2 = norm(total)
    final = xh2 * line(g2_ref) + line(s2_ref)
    put(xh2_ref, xh2)
    put(rs2_ref, jnp.broadcast_to(rs2, (rows, 128)))

    @pl.when(step == 0)
    def _():
        for s in range(sents):
            cls_ref[s : s + 1, :] = final[s * part : s * part + 1, :]
        cls = cls_ref[...]
        pooled = cls * lax.rsqrt(jnp.sum(cls * cls, -1, keepdims=True) + EPS)
        for s in range(sents):
            rows_ref[s % 2, s // 2 : s // 2 + 1, :] = pooled[s : s + 1, :]
        for half in range(2):
            buf[half, z, y, core, narrow] = rows_ref[half].astype(BF)
        for copy in z_copies:
            copy.start()

    @pl.when(step == 1)
    def _():
        for copy in z_copies:
            copy.wait()
        for copy in second:
            copy.start()

    @pl.when(step == 3)
    def _():
        core_copy.wait()
        out = pltpu.make_async_copy(buf, all_ref, done)
        out.start()
        out.wait()


def forward(tokens, ctx, ow, ob, g1, s1, uw, ub, dw, db, g2, s2, sizes):
    sents, seq, width = tokens.shape
    depth = uw.shape[1]
    part = seq // 4
    nz, nx = sizes[0] // 4, sizes[1]
    tile = lambda lanes: pl.BlockSpec((sents, part, lanes), lambda i: (0, i, 0))
    whole = lambda lanes, dtype: shape_of((sents, seq, lanes), dtype)
    slots = (2, nz, 2, 2, nx, sents // 2, width)
    dma = pltpu.SemaphoreType.DMA
    return pl.pallas_call(
        forward_kernel,
        grid=(4,),
        in_specs=[
            tile(width), tile(width), resident(ow.shape), resident(ob.shape), resident(g1.shape),
            resident(s1.shape), pl.BlockSpec(memory_space=pl.ANY), resident(ub.shape),
            pl.BlockSpec(memory_space=pl.ANY),
            resident(db.shape), resident(g2.shape), resident(s2.shape),
        ],
        out_specs=[
            tile(width), tile(width), tile(128), tile(depth), tile(depth), tile(width),
            tile(128), pl.BlockSpec((sents, width), lambda i: (0, 0)), pl.BlockSpec(memory_space=pl.ANY),
        ],
        out_shape=[
            whole(width, BF), whole(width, BF), whole(128, F32), whole(depth, BF),
            whole(depth, BF), whole(width, BF), whole(128, F32), shape_of((sents, width), F32),
            shape_of(slots, BF),
        ],
        scratch_shapes=[
            pltpu.VMEM((2, sents // 2, width), F32), pltpu.VMEM(uw.shape, BF), pltpu.VMEM(dw.shape, BF), dma((2,)),
            pltpu.VMEM(slots, BF),
            dma((nz - 1,)), dma((nz - 1,)), dma((2,)), dma((2,)), dma((2 * nx - 2,)), dma((2 * nx - 2,)), dma((1,)),
            dma((1,)), dma,
        ],
        compiler_params=params(collective_id=0, has_side_effects=True),
        name="forward",
    )(tokens, ctx.reshape(sents, seq, width), ow, ob, g1, s1, uw, ub, dw, db, g2, s2)


def ranking_kernel(
    all_ref, group_ref, cls_ref, cot_ref, xh2_ref, rs2_ref, g2_ref, s2_ref,
    loss_ref, out_ref, down_ref, sums_ref, dcls, gcol_ref,
):
    _, pairs, width = all_ref.shape
    own = cls_ref.shape[0] // 2
    step = pl.program_id(0)

    @pl.when(step == 0)
    def _():
        first = (lax.axis_index("wide") * lax.axis_size("narrow") + lax.axis_index("narrow")) * own
        strip = min(256, pairs)
        groups = line(group_ref)
        gcol_ref[...] = jnp.transpose(jnp.broadcast_to(groups, (128, pairs)))
        own_rows = pl.ds(pl.multiple_of(first, own), own)

        def logits_of(left, right, start):
            count = left.shape[0]
            same_at = lax.broadcasted_iota(jnp.int32, (count, pairs), 0) + start
            pair_at = lax.broadcasted_iota(jnp.int32, (count, pairs), 1)
            hit = same_at == pair_at
            return nt(left, right) * SCALE - jnp.where(hit, SCALE * MARGIN, 0.0), hit

        def column_lse(left_at, right_at):
            right = all_ref[right_at]

            def strip_step(at, carry):
                top, total, diag = carry
                start = pl.multiple_of(at * strip, strip)
                left = all_ref[left_at, pl.ds(start, strip), :]
                logits, hit = logits_of(left, right, start)
                masked = jnp.where(gcol_ref[pl.ds(start, strip), :1] == groups, logits, -1e30)
                peak = jnp.maximum(top, jnp.max(masked, axis=0, keepdims=True))
                total = total * jnp.exp(top - peak) + jnp.sum(jnp.exp(masked - peak), axis=0, keepdims=True)
                diag = diag + jnp.sum(jnp.where(hit, logits, 0.0), axis=0, keepdims=True)
                return peak, total, diag

            start = (jnp.full((1, pairs), -1e30, F32), jnp.zeros((1, pairs), F32), jnp.zeros((1, pairs), F32))
            top, total, diag = lax.fori_loop(0, pairs // strip, strip_step, start)
            return top + jnp.log(total), diag

        col_lse, diag = column_lse(0, 1)
        row_lse, diag_again = column_lse(1, 0)
        loss_ref[...] = jnp.sum(col_lse - diag + row_lse - diag_again, axis=1, keepdims=True) / pairs

        same = gcol_ref[own_rows, :1] == groups

        def side(my_at, other_at, other_lse):
            other = all_ref[other_at]
            mine = all_ref[my_at, own_rows, :]
            logits, hit = logits_of(mine, other, first)
            eye = hit.astype(F32)
            masked = jnp.where(same, logits, -1e30)
            e = jnp.exp(masked - jnp.max(masked, axis=1, keepdims=True))
            d_mine = (e / jnp.sum(e, axis=1, keepdims=True) - eye).astype(BF)
            d_other = (jnp.where(same, jnp.exp(masked - other_lse), 0.0) - eye).astype(BF)
            return (nn(d_mine, other) + nn(d_other, other)) * SCALE

        for at, (other, lse) in enumerate(((1, col_lse), (0, row_lse))):
            terms = side(at, other, lse)
            for p in range(own):
                dcls[2 * p + at : 2 * p + at + 1, :] = terms[p : p + 1, :]
        d = dcls[...]
        c = cls_ref[...]
        root = lax.rsqrt(jnp.sum(c * c, -1, keepdims=True) + EPS)
        dcls[...] = root * d - root * root * root * c * jnp.sum(c * d, -1, keepdims=True)
        sums_ref[...] = jnp.zeros_like(sums_ref)

    side_sents, seq, _ = cot_ref.shape
    rows = side_sents * seq
    start = pl.multiple_of(step * side_sents, side_sents)
    extra = dcls[pl.ds(start, side_sents), :]
    at_zero = lax.broadcasted_iota(jnp.int32, (side_sents, seq, width), 1) == 0
    d_final = cot_ref[...].astype(F32) + jnp.where(at_zero, extra[:, None, :], 0.0)
    d_final = d_final.reshape(rows, width)
    xhat = xh2_ref[...].reshape(rows, width).astype(F32)
    root = rs2_ref[...].reshape(rows, 128)[:, :1]
    out_ref[...] = (xhat * line(g2_ref) + line(s2_ref)).astype(BF).reshape(out_ref.shape)
    e = d_final * line(g2_ref)
    d_pre = (e - jnp.mean(e, -1, keepdims=True) - xhat * jnp.mean(e * xhat, -1, keepdims=True)) * root
    d_down = d_pre.astype(BF)
    down_ref[...] = d_down
    sums_ref[0:1, :] += jnp.sum(d_final * xhat, axis=0, keepdims=True)
    sums_ref[1:2, :] += jnp.sum(d_final, axis=0, keepdims=True)
    sums_ref[2:3, :] += jnp.sum(d_down.astype(F32), axis=0, keepdims=True)


def ranking(gathered, groups, cls, cotangent, xh2, rs2, g2, s2):
    sents, seq, width = cotangent.shape
    pairs = gathered.shape[1]
    tile = lambda lanes: pl.BlockSpec((SIDE, seq, lanes), lambda i: (i, 0, 0))
    return pl.pallas_call(
        ranking_kernel,
        grid=(sents // SIDE,),
        in_specs=[
            resident(gathered.shape), resident(groups.shape), resident(cls.shape), tile(width), tile(width), tile(128),
            resident(g2.shape), resident(s2.shape),
        ],
        out_specs=[
            pl.BlockSpec((1, 1), lambda i: (0, 0)), tile(width),
            pl.BlockSpec((SIDE * seq, width), lambda i: (i, 0)),
            pl.BlockSpec((8, width), lambda i: (0, 0)),
        ],
        out_shape=[shape_of((1, 1), F32), shape_of(cotangent.shape, BF), shape_of((sents * seq, width), BF), shape_of((8, width), F32)],
        scratch_shapes=[pltpu.VMEM((sents, width), F32), pltpu.VMEM((pairs, 128), jnp.int32)],
        compiler_params=params(),
        name="ranking",
    )(gathered, groups, cls, cotangent, xh2, rs2, g2, s2)


def copy_to(src, dst, sends, recvs, at, device):
    return pltpu.make_async_remote_copy(
        src_ref=src, dst_ref=dst, send_sem=sends.at[at], recv_sem=recvs.at[at], device_id=device,
        device_id_type=MESH,
    )


def plus(*terms):
    if len(terms) == 2:
        return terms[0] + terms[1]
    return sum(t.astype(F32) for t in terms).astype(BF)


class Peers:
    def __init__(self, nz):
        self.nz = nz
        wide, self.x, self.z, self.y, self.core = place()
        self.sibling = (wide + 1 - 2 * self.core, self.x)
        self.over_x = (wide, 1 - self.x)
        self.over_y = (wide + 2 - 4 * self.y, self.x)
        self.zs = [lax.rem(self.z + k, nz) for k in range(1, nz)]
        self.over_z = [(lax.rem(wide + 4 * k, 4 * nz), self.x) for k in range(1, nz)]

    def greet(self, devices):
        barrier = pltpu.get_barrier_semaphore()
        for device in devices:
            pl.semaphore_signal(barrier, inc=1, device_id=device, device_id_type=MESH)

    def met(self, count):
        pl.semaphore_wait(pltpu.get_barrier_semaphore(), count)


class Stages:
    SEMS = 9

    def __init__(self, peers, terms, got, sends, recvs):
        self.peers, self.terms, self.got, self.sends, self.recvs = peers, terms, got, sends, recvs
        self.half = peers.nz // 2

    @staticmethod
    def scratch(nz, rows, cols):
        half = nz // 2
        return {
            "xa": (half, 2, rows, cols), "yb": (2, nz - half, rows, cols), "ya": (half, rows, cols),
            "xb": (nz - half, rows, cols),
        }

    def first_of(self, z, at):
        p = self.peers
        if z < self.half:
            return copy_to(self.terms.at[1 - p.x, z], self.got["xa"].at[z], self.sends, self.recvs, at, p.over_x)
        return copy_to(
            self.terms.at[:, z, 1 - p.y], self.got["yb"].at[:, z - self.half], self.sends, self.recvs, at, p.over_y
        )

    def first(self):
        p, h = self.peers, self.half
        return [
            copy_to(self.terms.at[1 - p.x, :h], self.got["xa"], self.sends, self.recvs, 1, p.over_x),
            copy_to(self.terms.at[:, h:, 1 - p.y], self.got["yb"], self.sends, self.recvs, 2, p.over_y),
        ]

    def second(self):
        p, h = self.peers, self.half
        return [
            copy_to(self.terms.at[p.x, :h, 1 - p.y], self.got["ya"], self.sends, self.recvs, 3, p.over_y),
            copy_to(self.terms.at[1 - p.x, h:, p.y], self.got["xb"], self.sends, self.recvs, 4, p.over_x),
        ]

    def add_first(self, copies=None):
        p, h = self.peers, self.half
        for copy in copies or self.first():
            copy.wait()
        self.terms[p.x, :h] = plus(self.terms[p.x, :h], self.got["xa"][...])
        for x in range(2):
            self.terms[x, h:, p.y] = plus(self.terms[x, h:, p.y], self.got["yb"][x])

    def add_second(self):
        p, h = self.peers, self.half
        for copy in self.second():
            copy.wait()
        self.terms[p.x, :h, p.y] = plus(self.terms[p.x, :h, p.y], self.got["ya"][...])
        self.terms[p.x, h:, p.y] = plus(self.terms[p.x, h:, p.y], self.got["xb"][...])


class Finish:
    def __init__(self, peers, shard, got_z, mine, other, sends, recvs):
        self.peers, self.shard, self.got_z, self.mine, self.other = peers, shard, got_z, mine, other
        self.sends, self.recvs = sends, recvs

    def along_z(self):
        p = self.peers
        return [
            copy_to(self.shard(to), self.got_z.at[k], self.sends, self.recvs, 5 + k, device)
            for k, (to, device) in enumerate(zip(p.zs, p.over_z, strict=True))
        ]

    def along_x(self):
        return copy_to(self.mine, self.other, self.sends, self.recvs, 8, self.peers.over_x)

    def add(self):
        for copy in self.along_z():
            copy.wait()
        got = [self.got_z[k] for k in range(self.peers.nz - 1)]
        self.mine[...] = plus(self.shard(self.peers.z)[...], *got)


def hand_out(value, keep, send):
    halves, nz, ny, rows, cols = keep.shape
    core = lax.axis_index("wide") % 2
    for z in range(nz):
        for y in range(ny):
            first = (z * ny + y) * 2 * rows
            for ref, side in ((keep, core), (send, 1 - core)):
                part = value[pl.ds(pl.multiple_of(first + side * rows, rows), rows), :].astype(BF)
                for h in range(halves):
                    ref[h, z, y] = part[:, h * cols : (h + 1) * cols]


def backward_kernel(fused, nz, *refs):
    (down_ref, hid_ref, slope_ref, dw_hbm, uw_hbm, xh1_ref, rs1_ref, g1_ref, ow_ref, actx_ref) = refs[:10]
    (up_ref, attn_ref, ctx_ref, sums_ref, upsum_ref, owg_ref, dwg_ref) = refs[10:17]
    dw_ref, uw_ref, w_sems, owg, *comm = refs[17:]
    blocks = 4
    width = down_ref.shape[1]
    rows, depth = slope_ref.shape
    step = pl.program_id(0)
    weights = [
        pltpu.make_async_copy(dw_hbm, dw_ref, w_sems.at[0]), pltpu.make_async_copy(uw_hbm, uw_ref, w_sems.at[1])
    ]

    if fused:
        terms, send, got, xa, yb, ya, xb, c_send, c_recv, s_send, s_recv = comm
        peers = Peers(nz)
        stages = Stages(peers, terms, {"xa": xa, "yb": yb, "ya": ya, "xb": xb}, s_send, s_recv)

        def exchange(i):
            return copy_to(send.at[i % 2], got.at[i % 2], c_send, c_recv, i, peers.sibling)

    @pl.when(step == 0)
    def _():
        for copy in weights:
            copy.start()
        sums_ref[...] = jnp.zeros_like(sums_ref)
        upsum_ref[...] = jnp.zeros_like(upsum_ref)
        if fused:
            peers.greet([peers.sibling, peers.over_x, peers.over_y])

    def settle(i):
        exchange(i).wait()
        for h in range(2):
            terms[h, i] = plus(terms[h, i], got[i % 2, h, 0])
        for z in range(blocks):
            if isinstance(i, int) and z != i:
                continue

            @pl.when(i == z)
            def _(z=z):
                stages.first_of(z, Stages.SEMS + z).start()

    @pl.when(step < blocks)
    def _():
        value = tn(hid_ref[...], down_ref[...])
        if fused:

            @pl.when(step == 0)
            def _():
                peers.met(3)

            @pl.when(step > 0)
            def _():
                settle(step - 1)

            owg[...] = value
            hand_out(owg, terms.at[:, pl.ds(step, 1)], send.at[step % 2])
            exchange(step).start()

        else:
            dwg_ref[...] = value.astype(BF)

    @pl.when(step == blocks)
    def _():
        for copy in weights:
            copy.wait()

    @pl.when(step >= blocks)
    def _():
        d_down = down_ref[pl.ds(pl.multiple_of((step - blocks) * rows, rows), rows), :]
        total = d_down.astype(F32)
        for c in range(depth // width):
            cols = slice(c * width, (c + 1) * width)
            d_up = (nt(d_down, dw_ref[cols, :]) * slope_ref[:, cols].astype(F32)).astype(BF)
            up_ref[:, cols] = d_up
            upsum_ref[:, cols] += jnp.sum(d_up.astype(F32), axis=0, keepdims=True)
            total = total + nt(d_up, uw_ref[:, cols])
        xhat = xh1_ref[...].astype(F32)
        root = rs1_ref[:, :1]
        e = total * g1_ref[...].reshape(1, width)
        d_pre = (e - jnp.mean(e, -1, keepdims=True) - xhat * jnp.mean(e * xhat, -1, keepdims=True)) * root
        d_attn = d_pre.astype(BF)
        attn_ref[...] = d_attn
        ctx_ref[...] = nt(d_attn, ow_ref[...]).astype(BF)
        sums_ref[0:1, :] += jnp.sum(total * xhat, axis=0, keepdims=True)
        sums_ref[1:2, :] += jnp.sum(total, axis=0, keepdims=True)
        sums_ref[2:3, :] += jnp.sum(d_attn.astype(F32), axis=0, keepdims=True)
        part = tn(actx_ref[...], d_attn)

        @pl.when(step == blocks)
        def _():
            owg[...] = part

        @pl.when(step > blocks)
        def _():
            owg[...] += part

    if fused:

        @pl.when(step == blocks)
        def _():
            settle(blocks - 1)

        @pl.when(step == blocks + 1)
        def _():
            stages.add_first([stages.first_of(z, Stages.SEMS + z) for z in range(blocks)])
            for copy in stages.second():
                copy.start()

    @pl.when(step == pl.num_programs(0) - 1)
    def _():
        if fused:
            hand_out(owg, owg_ref.at[0], owg_ref.at[1])
            stages.add_second()
            dwg_ref[...] = terms[peers.x, :, peers.y]
        else:
            owg_ref[...] = owg[...].astype(BF)


def backward(d_down, hidden, slope, dw, uw, xh1, rs1, g1, ow, ctx, sizes):
    fused = sizes == (16, 2)
    nz = sizes[0] // 4
    rows, width = d_down.shape
    depth = uw.shape[1]
    side = rows // 4
    tile = lambda lanes: pl.BlockSpec((side, lanes), lambda i: (jnp.maximum(i - 4, 0), 0))
    once = lambda *shape: pl.BlockSpec(shape, lambda i: (0,) * len(shape))
    shard = depth // sizes[0]
    half = width // 2
    dma = pltpu.SemaphoreType.DMA
    scratch = [
        pltpu.VMEM(dw.shape, BF), pltpu.VMEM(uw.shape, BF), dma((2,)), pltpu.VMEM((width, width), F32)
    ]
    if fused:
        scratch += [
            pltpu.VMEM((2, nz, 2, shard, half), BF), pltpu.VMEM((2, 2, 1, 2, shard, half), BF),
            pltpu.VMEM((2, 2, 1, 2, shard, half), BF),
        ]
        scratch += [pltpu.VMEM(s, BF) for s in Stages.scratch(nz, shard, half).values()]
        scratch += [dma((4,)), dma((4,)), dma((Stages.SEMS + 4,)), dma((Stages.SEMS + 4,))]
        dwg_spec, dwg_shape = once(nz, shard, half), (nz, shard, half)
        owg_shape = (2, 2, nz, 2, width // sizes[0], half)
        extra = dict(collective_id=1, has_side_effects=True)
    else:
        dwg_spec, dwg_shape = pl.BlockSpec((width, width), lambda i: (jnp.minimum(i, 3), 0)), (depth, width)
        owg_shape = (width, width)
        extra = {}
    return pl.pallas_call(
        functools.partial(backward_kernel, fused, nz),
        grid=(8,),
        in_specs=[
            resident((rows, width)), pl.BlockSpec((rows, width), lambda i: (0, jnp.minimum(i, 3))), tile(depth),
            pl.BlockSpec(memory_space=pl.ANY), pl.BlockSpec(memory_space=pl.ANY), tile(width), tile(128),
            resident(g1.shape), resident(ow.shape), tile(width),
        ],
        out_specs=[
            tile(depth), tile(width), tile(width), once(8, width), once(1, depth), once(*owg_shape), dwg_spec
        ],
        out_shape=[
            shape_of((rows, depth), BF), shape_of((rows, width), BF), shape_of((rows, width), BF),
            shape_of((8, width), F32), shape_of((1, depth), F32), shape_of(owg_shape, BF),
            shape_of(dwg_shape, BF),
        ],
        scratch_shapes=scratch,
        compiler_params=params(**extra),
        name="backward",
    )(d_down, hidden, slope, dw, uw, xh1, rs1, g1, ow, ctx)


UPS, QUADS, TILES = 4, 3, 4
FIRST_QUAD = UPS
FIRST_INPUT = UPS + QUADS * TILES
STEPS = FIRST_INPUT + TILES
UP_PIECE, OUT_PIECE, QUAD_PIECE = 0, UPS, 1 + UPS
PIECES = UPS + 1 + QUADS
VECTORS = 16


def tail_kernel(fused, nz, *refs):
    (low_ref, up_ref, q_ref, k_ref, v_ref, dctx_ref, p_ref, x_ref, w_hbm, owg_ref, dsum_ref,
     one_ref, two_ref, upsum_ref) = refs[:14]
    out_ref, vec_out = refs[14:16]
    if fused:
        outs = refs[16:20]
        w_ref, w_sem, dqkv, acc, vec, *comm = refs[20:]
    else:
        upg_ref, qkvg_ref = refs[16:18]
        w_ref, w_sem, dqkv, acc, vec = refs[18:]
    rows, quad = q_ref.shape
    sents, seq, _ = p_ref.shape
    width = acc.shape[0]
    step = pl.program_id(0)
    weight = pltpu.make_async_copy(w_hbm, w_ref, w_sem)
    at_quad = jnp.clip(step - FIRST_QUAD, 0, QUADS * TILES - 1)
    g, tile = at_quad // TILES, at_quad % TILES

    if fused:
        (mine, other, dmine, dother, terms, send, got, xa, yb, ya, xb, gz, dz, vlow, vgot, sends, recvs, d_sends, d_recvs,
         v_sends, v_recvs) = comm
        peers = Peers(nz)
        down = Finish(peers, lambda at: dsum_ref.at[at], dz, dmine, dother, d_sends, d_recvs)

        def stages_of(n):
            return Stages(
                peers, terms.at[n], {"xa": xa.at[n], "yb": yb.at[n], "ya": ya.at[n], "xb": xb.at[n]}, sends.at[n],
                recvs.at[n],
            )

        def finish_of(n):
            return Finish(
                peers, lambda at: terms.at[n, peers.x, at, peers.y], gz.at[n], mine.at[n], other.at[n],
                sends.at[n], recvs.at[n],
            )

        def chip(n):
            return copy_to(send.at[n % 2], got.at[n % 2], sends.at[n], recvs.at[n], 0, peers.sibling)

        def add_chip(n):
            chip(n).wait()
            for h in range(2):
                terms[n, h] = plus(terms[n, h], got[n % 2, h])
            for copy in stages_of(n).first():
                copy.start()

        def add_first(n):
            stages_of(n).add_first()
            for copy in stages_of(n).second():
                copy.start()

        def add_second(n):
            stages_of(n).add_second()
            for copy in finish_of(n).along_z():
                copy.start()

        def add_z(n):
            finish_of(n).add()
            finish_of(n).along_x().start()

        def last(n):
            finish_of(n).along_x().wait()

        usual, hurried = (1, 3, 5, 7, 8), (1, 2, 3, 4, STEPS)
        ready = [*range(UPS + 1)] + [FIRST_QUAD + TILES * (q + 1) - 1 for q in range(QUADS)]

        def settle():
            for stage, action in enumerate((add_chip, add_first, add_second, add_z, last)):
                at = [t + (hurried if n == PIECES - 1 else usual)[stage] for n, t in enumerate(ready)]
                due, piece = step == at[0], jnp.int32(0)
                for n in range(1, PIECES):
                    due = due | (step == at[n])
                    piece = jnp.where(step == at[n], n, piece)
                pl.when(due)(functools.partial(action, piece))

        def vector_copy(n, device):
            return copy_to(vlow, vgot.at[n], v_sends, v_recvs, n, device)

        routes = [[peers.sibling], [peers.over_x], [peers.over_y], peers.over_z]

        def vector_copies(hop):
            return [vector_copy(hop + k, device) for k, device in enumerate(routes[hop])]

        @pl.when(step == 0)
        def _():
            peers.greet([peers.sibling, peers.over_x, peers.over_y, *peers.over_z])

    @pl.when(step == 0)
    def _():
        weight.start()
        vec[...] = jnp.zeros_like(vec)
        vec[2:3, :] = one_ref[2:3, :]
        vec[3:5, :] = one_ref[0:2, :]
        vec[5:6, :] = two_ref[2:3, :]
        vec[6:8, :] = two_ref[0:2, :]
        for c in range(UPS):
            vec[8 + c : 9 + c, :] = upsum_ref[:, c * width : (c + 1) * width]

    @pl.when(step < UPS)
    def _():
        value = tn(low_ref[...], up_ref[...])
        if fused:
            acc[...] = value
        else:
            upg_ref[...] = value.astype(BF)

    @pl.when((step >= FIRST_QUAD) & (step < FIRST_INPUT))
    def _():
        mask = head_mask(quad)
        scale = (quad // QUAD) ** -0.5
        here = lambda size, s=0: pl.ds(pl.multiple_of(tile * rows + s * seq, seq), size)
        for s in range(sents):
            at = slice(s * seq, (s + 1) * seq)
            k = k_ref[at, :]
            p_low = p_ref[s]
            p = p_low.astype(F32)
            dctx = blocked(dctx_ref[at, :], mask)
            d_probs = nt(v_ref[at, :], dctx)
            d_scores = (p * (d_probs - jnp.sum(p * d_probs, axis=0, keepdims=True))).astype(BF)
            dqkv[g, here(seq, s), :quad] = (paired(d_scores, k, seq) * scale).astype(BF)
            dqkv[g, here(seq, s), quad : 2 * quad] = (nn(d_scores, blocked(q_ref[at, :], mask)) * scale).astype(BF)
            dqkv[g, here(seq, s), 2 * quad :] = nn(p_low, dctx).astype(BF)
        grads = dqkv[g, here(rows), :]
        part = tn(x_ref[...], grads)
        q_sum = jnp.sum(grads[:, :quad].astype(F32), axis=0, keepdims=True)
        v_sum = jnp.sum(grads[:, 2 * quad :].astype(F32), axis=0, keepdims=True)
        for q in range(QUADS):

            @pl.when(g == q)
            def _(q=q):
                vec[0:1, q * quad : (q + 1) * quad] += q_sum
                vec[1:2, q * quad : (q + 1) * quad] += v_sum

        @pl.when(tile == 0)
        def _():
            acc[...] = part

        @pl.when(tile > 0)
        def _():
            acc[...] += part

    if fused:

        @pl.when(step == 0)
        def _():
            peers.met(2 + nz)
            for copy in down.along_z():
                copy.start()

        settle()

        @pl.when(step == UPS)
        def _():
            for h in range(2):
                terms[OUT_PIECE, h] = owg_ref[0, h]
                send[OUT_PIECE % 2, h] = owg_ref[1, h]
            chip(OUT_PIECE).start()

        done_quad = (step >= FIRST_QUAD) & (step < FIRST_INPUT) & (tile == TILES - 1)

        @pl.when((step < UPS) | done_quad)
        def _():
            n = jnp.where(step < UPS, UP_PIECE + step, QUAD_PIECE + g)
            hand_out(acc, terms.at[n], send.at[n % 2])
            chip(n).start()

        @pl.when(step == FIRST_INPUT - 1)
        def _():
            vlow[...] = vec[...].astype(BF)
            for copy in vector_copies(0):
                copy.start()

        for hop in range(4):

            @pl.when(step == FIRST_INPUT + hop)
            def _(hop=hop):
                for copy in vector_copies(hop):
                    copy.wait()
                vec[...] = vlow[...].astype(F32) + sum(vgot[hop + k].astype(F32) for k in range(len(routes[hop])))
                if hop < 3:
                    vlow[...] = vec[...].astype(BF)
                    for copy in vector_copies(hop + 1):
                        copy.start()

        @pl.when(step == 4)
        def _():
            down.add()
            down.along_x().start()

        @pl.when(step == 7)
        def _():
            down.along_x().wait()

    else:

        @pl.when((step >= FIRST_QUAD) & (step < FIRST_INPUT) & (tile == TILES - 1))
        def _():
            qkvg_ref[...] = acc[...].astype(BF)

    @pl.when(step == FIRST_INPUT)
    def _():
        weight.wait()

    @pl.when(step >= FIRST_INPUT)
    def _():
        here = pl.ds(pl.multiple_of((step - FIRST_INPUT) * rows, rows), rows)
        grads = jnp.concatenate(
            [dqkv[q, here, part * quad : (part + 1) * quad] for part in range(3) for q in range(QUADS)], axis=1
        )
        out_ref[...] = nt(grads, w_ref[...]).astype(BF)

    @pl.when(step == STEPS - 1)
    def _():
        if fused:
            last(PIECES - 1)
        vec_out[...] = vec[...]
        if fused:
            for ref, value in zip(outs, (mine, other, dmine, dother), strict=True):
                ref[...] = value[...]


def tail(low, d_up, qkv, d_ctx, probs, token_rows, qkv_weight, owg, dsum, one, two, upsum, sizes):
    fused = sizes == (16, 2)
    nz = sizes[0] // 4
    sents, seq, width = probs.shape
    rows = sents * seq
    side = rows // TILES
    quad = width // QUADS
    shard, half = width // sizes[0], width // 2
    at = lambda i: jnp.clip(i - FIRST_QUAD, 0, QUADS * TILES - 1)
    cols = lambda part: pl.BlockSpec((side, quad), lambda i: (at(i) % TILES, part * QUADS + at(i) // TILES))
    once = lambda *shape: pl.BlockSpec(shape, lambda i: (0,) * len(shape))
    finish = lambda lanes: pl.BlockSpec((side, lanes), lambda i: (jnp.maximum(i - FIRST_INPUT, 0), 0))
    dma = pltpu.SemaphoreType.DMA
    scratch = [
        pltpu.VMEM(qkv_weight.shape, BF), dma, pltpu.VMEM((QUADS, rows, width), BF),
        pltpu.VMEM((width, width), F32), pltpu.VMEM((VECTORS, width), F32),
    ]
    out_specs = [finish(width), once(VECTORS, width)]
    out_shape = [shape_of((rows, width), BF), shape_of((VECTORS, width), F32)]
    if fused:
        piece = (2, nz, 2, shard, half)
        scratch += [pltpu.VMEM((PIECES, shard, half), BF)] * 2 + [pltpu.VMEM(dsum.shape[1:], BF)] * 2
        scratch += [pltpu.VMEM((PIECES, *piece), BF), pltpu.VMEM((2, *piece), BF), pltpu.VMEM((2, *piece), BF)]
        scratch += [pltpu.VMEM((PIECES, *s), BF) for s in Stages.scratch(nz, shard, half).values()]
        scratch += [
            pltpu.VMEM((PIECES, nz - 1, shard, half), BF), pltpu.VMEM((nz - 1, *dsum.shape[1:]), BF),
            pltpu.VMEM((VECTORS, width), BF), pltpu.VMEM((2 + nz, VECTORS, width), BF),
        ]
        scratch += [dma((PIECES, Stages.SEMS))] * 2 + [dma((Stages.SEMS,))] * 2 + [dma((2 + nz,))] * 2
        out_specs += [once(PIECES, shard, half)] * 2 + [once(*dsum.shape[1:])] * 2
        out_shape += [shape_of((PIECES, shard, half), BF)] * 2 + [shape_of(dsum.shape[1:], BF)] * 2
        extra = dict(collective_id=2, has_side_effects=True)
    else:
        out_specs += [
            pl.BlockSpec((width, width), lambda i: (0, jnp.minimum(i, UPS - 1))),
            pl.BlockSpec((width, width), lambda i: (0, at(i) // TILES)),
        ]
        out_shape += [shape_of((width, UPS * width), BF), shape_of((width, QUADS * width), BF)]
        extra = {}
    return pl.pallas_call(
        functools.partial(tail_kernel, fused, nz),
        grid=(STEPS,),
        in_specs=[
            resident((rows, width)), pl.BlockSpec((rows, width), lambda i: (0, jnp.minimum(i, UPS - 1))),
            cols(0), cols(1), cols(2), cols(0),
            pl.BlockSpec((SIDE, seq, quad), lambda i: (at(i) % TILES, 0, at(i) // TILES)),
            pl.BlockSpec((side, width), lambda i: (at(i) % TILES, 0)),
            pl.BlockSpec(memory_space=pl.ANY), resident(owg.shape), resident(dsum.shape), resident(one.shape),
            resident(two.shape), resident(upsum.shape),
        ],
        out_specs=out_specs,
        out_shape=out_shape,
        scratch_shapes=scratch,
        compiler_params=params(**extra),
        name="tail",
    )(low, d_up, qkv, qkv, qkv, d_ctx, probs, token_rows, qkv_weight, owg, dsum, one, two, upsum)


def finish_kernel(fused, part_ref, attn_ref, *refs):
    if not fused:
        (input_ref,) = refs
    else:
        (mine_ref, other_ref, dmine_ref, dother_ref, vec_ref, input_ref, qkv_ref, qb_ref, vb_ref, out_ref, ob_ref,
         g1_ref, s1_ref, up_ref, ub_ref, down_ref, db_ref, g2_ref, s2_ref) = refs
    input_ref[...] = part_ref[...].astype(F32) + attn_ref[...].astype(F32)
    if not fused:
        return

    @pl.when(pl.program_id(0) == 0)
    def _():
        wide, narrow, z, _, _ = place()
        width = vec_ref.shape[1]
        shard = qb_ref.shape[0]

        def whole(mine, other):
            mine, other = mine.astype(F32), other.astype(F32)
            return jnp.concatenate([jnp.where(narrow == 0, mine, other), jnp.where(narrow == 0, other, mine)], axis=-1)

        for n in range(UPS):
            up_ref[:, n * width : (n + 1) * width] = whole(mine_ref[UP_PIECE + n], other_ref[UP_PIECE + n])
        out_ref[...] = whole(mine_ref[OUT_PIECE], other_ref[OUT_PIECE])
        quad = width // QUADS
        for q in range(QUADS):
            block = whole(mine_ref[QUAD_PIECE + q], other_ref[QUAD_PIECE + q])
            for part in range(3):
                to = part * width + q * quad
                qkv_ref[:, to : to + quad] = block[:, part * quad : (part + 1) * quad]
        down_ref[...] = whole(dmine_ref[...], dother_ref[...])
        rolled = pltpu.roll(vec_ref[...], lax.rem(width - wide * shard, width), 1)
        for n, ref in enumerate((qb_ref, vb_ref, ob_ref, g1_ref, s1_ref, db_ref, g2_ref, s2_ref)):
            ref[...] = rolled[n, :shard]
        depth = ub_ref.shape[0]
        ups = jnp.concatenate([vec_ref[pl.ds(8 + z, 1), :]] * 8, axis=0)
        ub_ref[...] = pltpu.roll(ups, lax.rem(width - lax.rem(wide, 4) * depth, width), 1)[0, :depth]


def finish(part, d_attn, sums, sizes, depth):
    fused = bool(sums)
    rows, width = part.shape
    side = rows // TILES
    shard = width // sizes[0]
    tile = pl.BlockSpec((side, width), lambda i: (i, 0))
    shapes = [(rows, width)]
    if fused:
        up = depth // sizes[0]
        vector = (shard,)
        shapes += [
            (shard, 3 * width), vector, vector, (shard, width), vector, vector, vector, (shard, depth), (up,),
            (up, width), vector, vector, vector,
        ]
    return pl.pallas_call(
        functools.partial(finish_kernel, fused),
        grid=(TILES,),
        in_specs=[tile, tile] + [resident(a.shape) for a in sums],
        out_specs=[tile] + [pl.BlockSpec(s, lambda i, n=len(s): (0,) * n) for s in shapes[1:]],
        out_shape=[shape_of(s, F32) for s in shapes],
        compiler_params=params(),
        name="finish",
    )(part, d_attn, *sums)


def per_device(
    sizes, tokens, cotangent, groups, qkv_weight, query_bias, value_bias, out_weight, out_bias, gain_one,
    shift_one, up_weight, up_bias, down_weight, down_bias, gain_two, shift_two,
):
    n_wide, n_narrow = sizes
    sents, seq, width = tokens.shape
    depth = up_weight.shape[1]
    rows = sents * seq
    flat = lambda v: v.reshape(rows, v.shape[-1])

    qkv, probs, ctx = attend(tokens, qkv_weight, query_bias, value_bias)
    low, xh1, rs1, hidden, slope, xh2, rs2, cls, slots = forward(
        tokens, ctx, out_weight, out_bias, gain_one, shift_one, up_weight, up_bias, down_weight, down_bias,
        gain_two, shift_two, sizes,
    )
    gathered = slots.reshape(2, n_wide * n_narrow * (sents // 2), width)
    loss, block_out, d_down, sums_two = ranking(
        gathered, groups, cls, cotangent, xh2, rs2, gain_two, shift_two
    )
    d_up, d_attn, d_ctx, sums_one, up_sum, out_terms, down_terms = backward(
        d_down, flat(hidden), flat(slope), down_weight, up_weight, flat(xh1), flat(rs1), gain_one, out_weight,
        ctx, sizes,
    )
    part, vectors, *sums = tail(
        flat(low), d_up, qkv, d_ctx, probs, flat(tokens), qkv_weight, out_terms, down_terms, sums_one, sums_two,
        up_sum, sizes,
    )
    if sizes == (16, 2):
        input_grad, *grads = finish(part, d_attn, [*sums, vectors], sizes, depth)
    else:
        (input_grad,) = finish(part, d_attn, [], sizes, depth)
        up_terms, qkv_terms = sums
        quad = width // QUADS
        qkv_terms = qkv_terms.reshape(width, QUADS, 3, quad).transpose(0, 2, 1, 3).reshape(width, 3 * width)
        total = lambda v: lax.psum(
            lax.psum_scatter(v, "wide", scatter_dimension=0, tiled=True).astype(F32), "narrow"
        )
        vector = lambda n: total(vectors[n])
        grads = (
            total(qkv_terms), vector(0), vector(1), total(out_terms), vector(2), vector(3), vector(4),
            total(up_terms), total(vectors[8 : 8 + UPS].reshape(-1)), total(down_terms), vector(5), vector(6),
            vector(7),
        )
    return (loss.reshape(()), block_out, input_grad.reshape(sents, seq, width), *grads)


def solution(mesh):
    sizes = (mesh.shape["wide"], mesh.shape["narrow"])
    split = P(("wide", "narrow"), None, None)
    matrix, vector = P("wide", None), P("wide")
    return jax.shard_map(
        functools.partial(per_device, sizes),
        mesh=mesh,
        in_specs=(split, split) + (P(),) * 14,
        out_specs=(
            P(), split, split, matrix, vector, vector, matrix, vector, vector, vector, matrix, vector,
            matrix, vector, vector, vector,
        ),
        check_vma=False,
    )
```

```python
import functools

import jax
import jax.numpy as jnp
from jax import lax
from jax.experimental import pallas as pl
from jax.experimental.pallas import tpu as pltpu
from jax.sharding import PartitionSpec as P

BF = jnp.bfloat16
F32 = jnp.float32
MESH = pl.DeviceIdType.MESH

HEADS = 12
QUAD = 4
SCALE = 40.0
MARGIN = 0.3
EPS = 1e-06
SIDE = 8
VMEM_BYTES = 60 * 2**20


def nn(a, b):
    return lax.dot_general(a, b, (((1,), (0,)), ((), ())), preferred_element_type=F32)


def nt(a, b):
    return lax.dot_general(a, b, (((1,), (1,)), ((), ())), preferred_element_type=F32)


def tn(a, b):
    return lax.dot_general(a, b, (((0,), (0,)), ((), ())), preferred_element_type=F32)


def params(**more):
    return pltpu.CompilerParams(vmem_limit_bytes=VMEM_BYTES, **more)


def resident(shape):
    return pl.BlockSpec(shape, lambda *_: (0,) * len(shape), pipeline_mode=pl.Buffered(1))


def shape_of(shape, dtype):
    return jax.ShapeDtypeStruct(shape, dtype)


def head_mask(quad):
    head = quad // QUAD
    at = lambda axis: lax.broadcasted_iota(jnp.int32, (quad, quad), axis) // head
    return (at(0) == at(1)).astype(F32).astype(BF)


def line(ref):
    return ref[...].reshape(1, ref.shape[0])


def blocked(rows, mask):
    return jnp.concatenate([rows] * QUAD, axis=0) * mask


def diagonal(full, seq):
    half = full.shape[1] // 2
    lane = lax.broadcasted_iota(jnp.int32, (seq, half), 1) < half // 2
    left = jnp.where(lane, full[:seq, :half], full[seq : 2 * seq, :half])
    right = jnp.where(lane, full[2 * seq : 3 * seq, half:], full[3 * seq :, half:])
    return jnp.concatenate([left, right], axis=1)


def paired(left, right, seq):
    half = left.shape[1] // 2
    lane = lax.broadcasted_iota(jnp.int32, (seq, half), 1) < half // 2
    parts = []
    for at in (slice(0, half), slice(half, 2 * half)):
        full = tn(left[:, at], right[:, at])
        parts.append(jnp.where(lane, full[:seq], full[seq:]))
    return jnp.concatenate(parts, axis=1)


def attend_kernel(x_ref, w_ref, qb_ref, vb_ref, qkv_ref, p_ref, ctx_ref):
    sents, seq, width = x_ref.shape
    rows = x_ref[...].reshape(sents * seq, width)
    quad = width // QUADS
    for part, bias in ((0, qb_ref), (1, None), (2, vb_ref)):
        cols = slice(part * width, (part + 1) * width)
        y = nn(rows, w_ref[:, cols])
        if bias is not None:
            y = y + line(bias)
        qkv_ref[:, cols] = y.astype(BF)
    mask = head_mask(quad)
    scale = (width // HEADS) ** -0.5
    units = [(s, g) for s in range(sents) for g in range(width // quad)]
    for first in range(0, len(units), 12):
        some = units[first : first + 12]
        rows_of = lambda s: slice(s * seq, (s + 1) * seq)
        cols_of = lambda g, part: slice(part * width + g * quad, part * width + (g + 1) * quad)
        scores = [
            nt(qkv_ref[rows_of(s), cols_of(g, 1)], blocked(qkv_ref[rows_of(s), cols_of(g, 0)], mask)) * scale
            for s, g in some
        ]
        e = [jnp.exp(v - jnp.max(v, axis=0, keepdims=True)) for v in scores]
        p = [(v * (1.0 / jnp.sum(v, axis=0, keepdims=True))).astype(BF) for v in e]
        for (s, g), low in zip(some, p, strict=True):
            p_ref[s, :, cols_of(g, 0)] = low
            v = qkv_ref[rows_of(s), cols_of(g, 2)]
            ctx_ref[rows_of(s), cols_of(g, 0)] = diagonal(tn(low, v), seq).astype(BF)


def attend(tokens, qkv_weight, query_bias, value_bias):
    sents, seq, width = tokens.shape
    rows = sents * seq
    side = SIDE * seq
    return pl.pallas_call(
        attend_kernel,
        grid=(sents // SIDE,),
        in_specs=[
            pl.BlockSpec((SIDE, seq, width), lambda i: (i, 0, 0)),
            resident((width, 3 * width)),
            resident((width,)),
            resident((width,)),
        ],
        out_specs=[
            pl.BlockSpec((side, 3 * width), lambda i: (i, 0)),
            pl.BlockSpec((SIDE, seq, width), lambda i: (i, 0, 0)),
            pl.BlockSpec((side, width), lambda i: (i, 0)),
        ],
        out_shape=[
            shape_of((rows, 3 * width), BF),
            shape_of((sents, seq, width), BF),
            shape_of((rows, width), BF),
        ],
        compiler_params=params(),
        name="attend",
    )(tokens, qkv_weight, query_bias, value_bias)


def norm(values):
    mean = jnp.mean(values, -1, keepdims=True)
    centred = values - mean
    root = lax.rsqrt(jnp.mean(centred * centred, -1, keepdims=True) + EPS)
    return centred * root, root


def place():
    wide, narrow = lax.axis_index("wide"), lax.axis_index("narrow")
    return wide, narrow, wide // 4, (wide // 2) % 2, wide % 2


def forward_kernel(
    x_ref, ctx_ref, ow_ref, ob_ref, g1_ref, s1_ref, uw_hbm, ub_ref, dw_hbm, db_ref, g2_ref, s2_ref,
    low_ref, xh1_ref, rs1_ref, hid_ref, slope_ref, xh2_ref, rs2_ref, cls_ref, all_ref,
    rows_ref, uw_ref, dw_ref, w_sems, buf, zs, zr, ys, yr, xs, xr, cs, cr, done,
):
    sents, part, width = x_ref.shape
    depth = uw_ref.shape[1]
    rows = sents * part
    step = pl.program_id(0)
    wide, narrow, z, y, core = place()
    nz, nx = buf.shape[1], buf.shape[4]
    wide_of = lambda a, b, c: (a * 2 + b) * 2 + c
    z_peers = [(lax.rem(z + k, nz), k) for k in range(1, nz)]
    x_peers = [(lax.rem(narrow + k, nx), k) for k in range(1, nx)]

    def gather_copy(slots, sems, at, device):
        return pltpu.make_async_remote_copy(
            src_ref=buf.at[slots], dst_ref=buf.at[slots], send_sem=sems[0].at[at], recv_sem=sems[1].at[at],
            device_id=device, device_id_type=MESH,
        )

    every = slice(None)
    z_copies = [
        gather_copy((every, z, y, core, narrow), (zs, zr), k - 1, (wide_of(to, y, core), narrow))
        for to, k in z_peers
    ]

    def over_y(half, xs_held, at):
        return gather_copy((half, every, y, core, xs_held), (ys, yr), at, (wide_of(z, 1 - y, core), narrow))

    def over_x(half, ys_held, first):
        return [
            gather_copy((half, every, ys_held, core, narrow), (xs, xr), first + k - 1, (wide, to)) for to, k in x_peers
        ]

    second = [over_y(0, narrow, 0), *over_x(1, y, 0)]
    third = [*over_x(0, every, nx - 1), over_y(1, every, 1)]
    core_copy = gather_copy((every, every, every, core), (cs, cr), 0, (wide_of(z, y, 1 - core), narrow))

    barrier = pltpu.get_barrier_semaphore()
    weights = [
        pltpu.make_async_copy(uw_hbm, uw_ref, w_sems.at[0]), pltpu.make_async_copy(dw_hbm, dw_ref, w_sems.at[1])
    ]

    @pl.when(step == 0)
    def _():
        for copy in weights:
            copy.start()
        for to, _ in z_peers:
            pl.semaphore_signal(barrier, inc=1, device_id=(wide_of(to, y, core), narrow), device_id_type=MESH)
        pl.semaphore_signal(barrier, inc=1, device_id=(wide_of(z, 1 - y, core), narrow), device_id_type=MESH)
        for to, _ in x_peers:
            pl.semaphore_signal(barrier, inc=1, device_id=(wide, to), device_id_type=MESH)
        pl.semaphore_signal(barrier, inc=1, device_id=(wide_of(z, y, 1 - core), narrow), device_id_type=MESH)

    block = lambda ref: ref[...].reshape(rows, ref.shape[2])

    def put(ref, value):
        ref[...] = value.astype(ref.dtype).reshape(ref.shape)

    pre_one = block(x_ref).astype(F32) + nn(block(ctx_ref), ow_ref[...]) + line(ob_ref)
    xh1, rs1 = norm(pre_one)
    normed = xh1 * line(g1_ref) + line(s1_ref)
    low = normed.astype(BF)
    put(low_ref, low)
    put(xh1_ref, xh1)
    put(rs1_ref, jnp.broadcast_to(rs1, (rows, 128)))
    total = normed + line(db_ref)

    @pl.when(step == 0)
    def _():
        for copy in weights:
            copy.wait()

    for c in range(depth // width):
        if c == 2:

            @pl.when(step == 0)
            def _():
                pl.semaphore_wait(barrier, nz + nx)

            @pl.when(step == 2)
            def _():
                for copy in second:
                    copy.wait()
                for copy in third:
                    copy.start()

            @pl.when(step == 3)
            def _():
                for copy in third:
                    copy.wait()
                core_copy.start()

        cols = slice(c * width, (c + 1) * width)
        up = nn(low, uw_ref[:, cols]) + ub_ref[cols].reshape(1, width)
        cdf = 0.5 * (lax.erf(up * 0.7071067811865476) + 1.0)
        slope = cdf + up * (0.3989422804014327 * jnp.exp(-0.5 * up * up))
        hidden = (up * cdf).astype(BF)
        hid_ref[:, :, cols] = hidden.reshape(sents, part, width)
        slope_ref[:, :, cols] = slope.astype(BF).reshape(sents, part, width)
        total = total + nn(hidden, dw_ref[cols, :])
    xh2, rs2 = norm(total)
    final = xh2 * line(g2_ref) + line(s2_ref)
    put(xh2_ref, xh2)
    put(rs2_ref, jnp.broadcast_to(rs2, (rows, 128)))

    @pl.when(step == 0)
    def _():
        for s in range(sents):
            cls_ref[s : s + 1, :] = final[s * part : s * part + 1, :]
        cls = cls_ref[...]
        pooled = cls * lax.rsqrt(jnp.sum(cls * cls, -1, keepdims=True) + EPS)
        for s in range(sents):
            rows_ref[s % 2, s // 2 : s // 2 + 1, :] = pooled[s : s + 1, :]
        for half in range(2):
            buf[half, z, y, core, narrow] = rows_ref[half].astype(BF)
        for copy in z_copies:
            copy.start()

    @pl.when(step == 1)
    def _():
        for copy in z_copies:
            copy.wait()
        for copy in second:
            copy.start()

    @pl.when(step == 3)
    def _():
        core_copy.wait()
        out = pltpu.make_async_copy(buf, all_ref, done)
        out.start()
        out.wait()


def forward(tokens, ctx, ow, ob, g1, s1, uw, ub, dw, db, g2, s2, sizes):
    sents, seq, width = tokens.shape
    depth = uw.shape[1]
    part = seq // 4
    nz, nx = sizes[0] // 4, sizes[1]
    tile = lambda lanes: pl.BlockSpec((sents, part, lanes), lambda i: (0, i, 0))
    whole = lambda lanes, dtype: shape_of((sents, seq, lanes), dtype)
    slots = (2, nz, 2, 2, nx, sents // 2, width)
    dma = pltpu.SemaphoreType.DMA
    return pl.pallas_call(
        forward_kernel,
        grid=(4,),
        in_specs=[
            tile(width), tile(width), resident(ow.shape), resident(ob.shape), resident(g1.shape),
            resident(s1.shape), pl.BlockSpec(memory_space=pl.ANY), resident(ub.shape),
            pl.BlockSpec(memory_space=pl.ANY),
            resident(db.shape), resident(g2.shape), resident(s2.shape),
        ],
        out_specs=[
            tile(width), tile(width), tile(128), tile(depth), tile(depth), tile(width),
            tile(128), pl.BlockSpec((sents, width), lambda i: (0, 0)), pl.BlockSpec(memory_space=pl.ANY),
        ],
        out_shape=[
            whole(width, BF), whole(width, BF), whole(128, F32), whole(depth, BF),
            whole(depth, BF), whole(width, BF), whole(128, F32), shape_of((sents, width), F32),
            shape_of(slots, BF),
        ],
        scratch_shapes=[
            pltpu.VMEM((2, sents // 2, width), F32), pltpu.VMEM(uw.shape, BF), pltpu.VMEM(dw.shape, BF), dma((2,)),
            pltpu.VMEM(slots, BF),
            dma((nz - 1,)), dma((nz - 1,)), dma((2,)), dma((2,)), dma((2 * nx - 2,)), dma((2 * nx - 2,)), dma((1,)),
            dma((1,)), dma,
        ],
        compiler_params=params(collective_id=0, has_side_effects=True),
        name="forward",
    )(tokens, ctx.reshape(sents, seq, width), ow, ob, g1, s1, uw, ub, dw, db, g2, s2)


def ranking_kernel(
    all_ref, group_ref, cls_ref, cot_ref, xh2_ref, rs2_ref, g2_ref, s2_ref,
    loss_ref, out_ref, down_ref, sums_ref, dcls, gcol_ref,
):
    _, pairs, width = all_ref.shape
    own = cls_ref.shape[0] // 2
    step = pl.program_id(0)

    @pl.when(step == 0)
    def _():
        first = (lax.axis_index("wide") * lax.axis_size("narrow") + lax.axis_index("narrow")) * own
        strip = min(256, pairs)
        groups = line(group_ref)
        gcol_ref[...] = jnp.transpose(jnp.broadcast_to(groups, (128, pairs)))
        own_rows = pl.ds(pl.multiple_of(first, own), own)

        def logits_of(left, right, start):
            count = left.shape[0]
            same_at = lax.broadcasted_iota(jnp.int32, (count, pairs), 0) + start
            pair_at = lax.broadcasted_iota(jnp.int32, (count, pairs), 1)
            hit = same_at == pair_at
            return nt(left, right) * SCALE - jnp.where(hit, SCALE * MARGIN, 0.0), hit

        def column_lse(left_at, right_at):
            right = all_ref[right_at]

            def strip_step(at, carry):
                top, total, diag = carry
                start = pl.multiple_of(at * strip, strip)
                left = all_ref[left_at, pl.ds(start, strip), :]
                logits, hit = logits_of(left, right, start)
                masked = jnp.where(gcol_ref[pl.ds(start, strip), :1] == groups, logits, -1e30)
                peak = jnp.maximum(top, jnp.max(masked, axis=0, keepdims=True))
                total = total * jnp.exp(top - peak) + jnp.sum(jnp.exp(masked - peak), axis=0, keepdims=True)
                diag = diag + jnp.sum(jnp.where(hit, logits, 0.0), axis=0, keepdims=True)
                return peak, total, diag

            start = (jnp.full((1, pairs), -1e30, F32), jnp.zeros((1, pairs), F32), jnp.zeros((1, pairs), F32))
            top, total, diag = lax.fori_loop(0, pairs // strip, strip_step, start)
            return top + jnp.log(total), diag

        col_lse, diag = column_lse(0, 1)
        row_lse, diag_again = column_lse(1, 0)
        loss_ref[...] = jnp.sum(col_lse - diag + row_lse - diag_again, axis=1, keepdims=True) / pairs

        same = gcol_ref[own_rows, :1] == groups

        def side(my_at, other_at, other_lse):
            other = all_ref[other_at]
            mine = all_ref[my_at, own_rows, :]
            logits, hit = logits_of(mine, other, first)
            eye = hit.astype(F32)
            masked = jnp.where(same, logits, -1e30)
            e = jnp.exp(masked - jnp.max(masked, axis=1, keepdims=True))
            d_mine = (e / jnp.sum(e, axis=1, keepdims=True) - eye).astype(BF)
            d_other = (jnp.where(same, jnp.exp(masked - other_lse), 0.0) - eye).astype(BF)
            return (nn(d_mine, other) + nn(d_other, other)) * SCALE

        for at, (other, lse) in enumerate(((1, col_lse), (0, row_lse))):
            terms = side(at, other, lse)
            for p in range(own):
                dcls[2 * p + at : 2 * p + at + 1, :] = terms[p : p + 1, :]
        d = dcls[...]
        c = cls_ref[...]
        root = lax.rsqrt(jnp.sum(c * c, -1, keepdims=True) + EPS)
        dcls[...] = root * d - root * root * root * c * jnp.sum(c * d, -1, keepdims=True)
        sums_ref[...] = jnp.zeros_like(sums_ref)

    side_sents, seq, _ = cot_ref.shape
    rows = side_sents * seq
    start = pl.multiple_of(step * side_sents, side_sents)
    extra = dcls[pl.ds(start, side_sents), :]
    at_zero = lax.broadcasted_iota(jnp.int32, (side_sents, seq, width), 1) == 0
    d_final = cot_ref[...].astype(F32) + jnp.where(at_zero, extra[:, None, :], 0.0)
    d_final = d_final.reshape(rows, width)
    xhat = xh2_ref[...].reshape(rows, width).astype(F32)
    root = rs2_ref[...].reshape(rows, 128)[:, :1]
    out_ref[...] = (xhat * line(g2_ref) + line(s2_ref)).astype(BF).reshape(out_ref.shape)
    e = d_final * line(g2_ref)
    d_pre = (e - jnp.mean(e, -1, keepdims=True) - xhat * jnp.mean(e * xhat, -1, keepdims=True)) * root
    d_down = d_pre.astype(BF)
    down_ref[...] = d_down
    sums_ref[0:1, :] += jnp.sum(d_final * xhat, axis=0, keepdims=True)
    sums_ref[1:2, :] += jnp.sum(d_final, axis=0, keepdims=True)
    sums_ref[2:3, :] += jnp.sum(d_down.astype(F32), axis=0, keepdims=True)


def ranking(gathered, groups, cls, cotangent, xh2, rs2, g2, s2):
    sents, seq, width = cotangent.shape
    pairs = gathered.shape[1]
    tile = lambda lanes: pl.BlockSpec((SIDE, seq, lanes), lambda i: (i, 0, 0))
    return pl.pallas_call(
        ranking_kernel,
        grid=(sents // SIDE,),
        in_specs=[
            resident(gathered.shape), resident(groups.shape), resident(cls.shape), tile(width), tile(width), tile(128),
            resident(g2.shape), resident(s2.shape),
        ],
        out_specs=[
            pl.BlockSpec((1, 1), lambda i: (0, 0)), tile(width),
            pl.BlockSpec((SIDE * seq, width), lambda i: (i, 0)),
            pl.BlockSpec((8, width), lambda i: (0, 0)),
        ],
        out_shape=[shape_of((1, 1), F32), shape_of(cotangent.shape, BF), shape_of((sents * seq, width), BF), shape_of((8, width), F32)],
        scratch_shapes=[pltpu.VMEM((sents, width), F32), pltpu.VMEM((pairs, 128), jnp.int32)],
        compiler_params=params(),
        name="ranking",
    )(gathered, groups, cls, cotangent, xh2, rs2, g2, s2)


def copy_to(src, dst, sends, recvs, at, device):
    return pltpu.make_async_remote_copy(
        src_ref=src, dst_ref=dst, send_sem=sends.at[at], recv_sem=recvs.at[at], device_id=device,
        device_id_type=MESH,
    )


def plus(*terms):
    if len(terms) == 2:
        return terms[0] + terms[1]
    return sum(t.astype(F32) for t in terms).astype(BF)


class Peers:
    def __init__(self, nz):
        self.nz = nz
        wide, self.x, self.z, self.y, self.core = place()
        self.sibling = (wide + 1 - 2 * self.core, self.x)
        self.over_x = (wide, 1 - self.x)
        self.over_y = (wide + 2 - 4 * self.y, self.x)
        self.zs = [lax.rem(self.z + k, nz) for k in range(1, nz)]
        self.over_z = [(lax.rem(wide + 4 * k, 4 * nz), self.x) for k in range(1, nz)]

    def greet(self, devices):
        barrier = pltpu.get_barrier_semaphore()
        for device in devices:
            pl.semaphore_signal(barrier, inc=1, device_id=device, device_id_type=MESH)

    def met(self, count):
        pl.semaphore_wait(pltpu.get_barrier_semaphore(), count)


class Stages:
    SEMS = 9

    def __init__(self, peers, terms, got, sends, recvs):
        self.peers, self.terms, self.got, self.sends, self.recvs = peers, terms, got, sends, recvs
        self.half = peers.nz // 2

    @staticmethod
    def scratch(nz, rows, cols):
        half = nz // 2
        return {
            "xa": (half, 2, rows, cols), "yb": (2, nz - half, rows, cols), "ya": (half, rows, cols),
            "xb": (nz - half, rows, cols),
        }

    def first_of(self, z, at):
        p = self.peers
        if z < self.half:
            return copy_to(self.terms.at[1 - p.x, z], self.got["xa"].at[z], self.sends, self.recvs, at, p.over_x)
        return copy_to(
            self.terms.at[:, z, 1 - p.y], self.got["yb"].at[:, z - self.half], self.sends, self.recvs, at, p.over_y
        )

    def first(self):
        p, h = self.peers, self.half
        return [
            copy_to(self.terms.at[1 - p.x, :h], self.got["xa"], self.sends, self.recvs, 1, p.over_x),
            copy_to(self.terms.at[:, h:, 1 - p.y], self.got["yb"], self.sends, self.recvs, 2, p.over_y),
        ]

    def second(self):
        p, h = self.peers, self.half
        return [
            copy_to(self.terms.at[p.x, :h, 1 - p.y], self.got["ya"], self.sends, self.recvs, 3, p.over_y),
            copy_to(self.terms.at[1 - p.x, h:, p.y], self.got["xb"], self.sends, self.recvs, 4, p.over_x),
        ]

    def add_first(self, copies=None):
        p, h = self.peers, self.half
        for copy in copies or self.first():
            copy.wait()
        self.terms[p.x, :h] = plus(self.terms[p.x, :h], self.got["xa"][...])
        for x in range(2):
            self.terms[x, h:, p.y] = plus(self.terms[x, h:, p.y], self.got["yb"][x])

    def add_second(self):
        p, h = self.peers, self.half
        for copy in self.second():
            copy.wait()
        self.terms[p.x, :h, p.y] = plus(self.terms[p.x, :h, p.y], self.got["ya"][...])
        self.terms[p.x, h:, p.y] = plus(self.terms[p.x, h:, p.y], self.got["xb"][...])


class Finish:
    def __init__(self, peers, shard, got_z, mine, other, sends, recvs):
        self.peers, self.shard, self.got_z, self.mine, self.other = peers, shard, got_z, mine, other
        self.sends, self.recvs = sends, recvs

    def along_z(self):
        p = self.peers
        return [
            copy_to(self.shard(to), self.got_z.at[k], self.sends, self.recvs, 5 + k, device)
            for k, (to, device) in enumerate(zip(p.zs, p.over_z, strict=True))
        ]

    def along_x(self):
        return copy_to(self.mine, self.other, self.sends, self.recvs, 8, self.peers.over_x)

    def add(self):
        for copy in self.along_z():
            copy.wait()
        got = [self.got_z[k] for k in range(self.peers.nz - 1)]
        self.mine[...] = plus(self.shard(self.peers.z)[...], *got)


def hand_out(value, keep, send):
    halves, nz, ny, rows, cols = keep.shape
    core = lax.axis_index("wide") % 2
    for z in range(nz):
        for y in range(ny):
            first = (z * ny + y) * 2 * rows
            for ref, side in ((keep, core), (send, 1 - core)):
                part = value[pl.ds(pl.multiple_of(first + side * rows, rows), rows), :].astype(BF)
                for h in range(halves):
                    ref[h, z, y] = part[:, h * cols : (h + 1) * cols]


def backward_kernel(fused, nz, *refs):
    (down_ref, hid_ref, slope_ref, dw_hbm, uw_hbm, xh1_ref, rs1_ref, g1_ref, ow_ref, actx_ref) = refs[:10]
    (up_ref, attn_ref, ctx_ref, sums_ref, upsum_ref, owg_ref, dwg_ref) = refs[10:17]
    dw_ref, uw_ref, w_sems, owg, *comm = refs[17:]
    blocks = 4
    width = down_ref.shape[1]
    rows, depth = slope_ref.shape
    step = pl.program_id(0)
    weights = [
        pltpu.make_async_copy(dw_hbm, dw_ref, w_sems.at[0]), pltpu.make_async_copy(uw_hbm, uw_ref, w_sems.at[1])
    ]

    if fused:
        terms, send, got, xa, yb, ya, xb, c_send, c_recv, s_send, s_recv = comm
        peers = Peers(nz)
        stages = Stages(peers, terms, {"xa": xa, "yb": yb, "ya": ya, "xb": xb}, s_send, s_recv)

        def exchange(i):
            return copy_to(send.at[i % 2], got.at[i % 2], c_send, c_recv, i, peers.sibling)

    @pl.when(step == 0)
    def _():
        for copy in weights:
            copy.start()
        sums_ref[...] = jnp.zeros_like(sums_ref)
        upsum_ref[...] = jnp.zeros_like(upsum_ref)
        if fused:
            peers.greet([peers.sibling, peers.over_x, peers.over_y])

    def settle(i):
        exchange(i).wait()
        for h in range(2):
            terms[h, i] = plus(terms[h, i], got[i % 2, h, 0])
        for z in range(blocks):
            if isinstance(i, int) and z != i:
                continue

            @pl.when(i == z)
            def _(z=z):
                stages.first_of(z, Stages.SEMS + z).start()

    @pl.when(step < blocks)
    def _():
        value = tn(hid_ref[...], down_ref[...])
        if fused:

            @pl.when(step == 0)
            def _():
                peers.met(3)

            @pl.when(step > 0)
            def _():
                settle(step - 1)

            owg[...] = value
            hand_out(owg, terms.at[:, pl.ds(step, 1)], send.at[step % 2])
            exchange(step).start()

        else:
            dwg_ref[...] = value.astype(BF)

    @pl.when(step == blocks)
    def _():
        for copy in weights:
            copy.wait()

    @pl.when(step >= blocks)
    def _():
        d_down = down_ref[pl.ds(pl.multiple_of((step - blocks) * rows, rows), rows), :]
        total = d_down.astype(F32)
        for c in range(depth // width):
            cols = slice(c * width, (c + 1) * width)
            d_up = (nt(d_down, dw_ref[cols, :]) * slope_ref[:, cols].astype(F32)).astype(BF)
            up_ref[:, cols] = d_up
            upsum_ref[:, cols] += jnp.sum(d_up.astype(F32), axis=0, keepdims=True)
            total = total + nt(d_up, uw_ref[:, cols])
        xhat = xh1_ref[...].astype(F32)
        root = rs1_ref[:, :1]
        e = total * g1_ref[...].reshape(1, width)
        d_pre = (e - jnp.mean(e, -1, keepdims=True) - xhat * jnp.mean(e * xhat, -1, keepdims=True)) * root
        d_attn = d_pre.astype(BF)
        attn_ref[...] = d_attn
        ctx_ref[...] = nt(d_attn, ow_ref[...]).astype(BF)
        sums_ref[0:1, :] += jnp.sum(total * xhat, axis=0, keepdims=True)
        sums_ref[1:2, :] += jnp.sum(total, axis=0, keepdims=True)
        sums_ref[2:3, :] += jnp.sum(d_attn.astype(F32), axis=0, keepdims=True)
        part = tn(actx_ref[...], d_attn)

        @pl.when(step == blocks)
        def _():
            owg[...] = part

        @pl.when(step > blocks)
        def _():
            owg[...] += part

    if fused:

        @pl.when(step == blocks)
        def _():
            settle(blocks - 1)

        @pl.when(step == blocks + 1)
        def _():
            stages.add_first([stages.first_of(z, Stages.SEMS + z) for z in range(blocks)])
            for copy in stages.second():
                copy.start()

    @pl.when(step == pl.num_programs(0) - 1)
    def _():
        if fused:
            hand_out(owg, owg_ref.at[0], owg_ref.at[1])
            stages.add_second()
            dwg_ref[...] = terms[peers.x, :, peers.y]
        else:
            owg_ref[...] = owg[...].astype(BF)


def backward(d_down, hidden, slope, dw, uw, xh1, rs1, g1, ow, ctx, sizes):
    fused = sizes == (16, 2)
    nz = sizes[0] // 4
    rows, width = d_down.shape
    depth = uw.shape[1]
    side = rows // 4
    tile = lambda lanes: pl.BlockSpec((side, lanes), lambda i: (jnp.maximum(i - 4, 0), 0))
    once = lambda *shape: pl.BlockSpec(shape, lambda i: (0,) * len(shape))
    shard = depth // sizes[0]
    half = width // 2
    dma = pltpu.SemaphoreType.DMA
    scratch = [
        pltpu.VMEM(dw.shape, BF), pltpu.VMEM(uw.shape, BF), dma((2,)), pltpu.VMEM((width, width), F32)
    ]
    if fused:
        scratch += [
            pltpu.VMEM((2, nz, 2, shard, half), BF), pltpu.VMEM((2, 2, 1, 2, shard, half), BF),
            pltpu.VMEM((2, 2, 1, 2, shard, half), BF),
        ]
        scratch += [pltpu.VMEM(s, BF) for s in Stages.scratch(nz, shard, half).values()]
        scratch += [dma((4,)), dma((4,)), dma((Stages.SEMS + 4,)), dma((Stages.SEMS + 4,))]
        dwg_spec, dwg_shape = once(nz, shard, half), (nz, shard, half)
        owg_shape = (2, 2, nz, 2, width // sizes[0], half)
        extra = dict(collective_id=1, has_side_effects=True)
    else:
        dwg_spec, dwg_shape = pl.BlockSpec((width, width), lambda i: (jnp.minimum(i, 3), 0)), (depth, width)
        owg_shape = (width, width)
        extra = {}
    return pl.pallas_call(
        functools.partial(backward_kernel, fused, nz),
        grid=(8,),
        in_specs=[
            resident((rows, width)), pl.BlockSpec((rows, width), lambda i: (0, jnp.minimum(i, 3))), tile(depth),
            pl.BlockSpec(memory_space=pl.ANY), pl.BlockSpec(memory_space=pl.ANY), tile(width), tile(128),
            resident(g1.shape), resident(ow.shape), tile(width),
        ],
        out_specs=[
            tile(depth), tile(width), tile(width), once(8, width), once(1, depth), once(*owg_shape), dwg_spec
        ],
        out_shape=[
            shape_of((rows, depth), BF), shape_of((rows, width), BF), shape_of((rows, width), BF),
            shape_of((8, width), F32), shape_of((1, depth), F32), shape_of(owg_shape, BF),
            shape_of(dwg_shape, BF),
        ],
        scratch_shapes=scratch,
        compiler_params=params(**extra),
        name="backward",
    )(d_down, hidden, slope, dw, uw, xh1, rs1, g1, ow, ctx)


UPS, QUADS, TILES = 4, 3, 4
FIRST_QUAD = UPS
FIRST_INPUT = UPS + QUADS * TILES
STEPS = FIRST_INPUT + TILES
UP_PIECE, OUT_PIECE, QUAD_PIECE = 0, UPS, 1 + UPS
PIECES = UPS + 1 + QUADS
VECTORS = 16


def tail_kernel(fused, nz, *refs):
    (low_ref, up_ref, q_ref, k_ref, v_ref, dctx_ref, p_ref, x_ref, w_hbm, owg_ref, dsum_ref,
     one_ref, two_ref, upsum_ref) = refs[:14]
    out_ref, vec_out = refs[14:16]
    if fused:
        outs = refs[16:20]
        w_ref, w_sem, dqkv, acc, vec, *comm = refs[20:]
    else:
        upg_ref, qkvg_ref = refs[16:18]
        w_ref, w_sem, dqkv, acc, vec = refs[18:]
    rows, quad = q_ref.shape
    sents, seq, _ = p_ref.shape
    width = acc.shape[0]
    step = pl.program_id(0)
    weight = pltpu.make_async_copy(w_hbm, w_ref, w_sem)
    at_quad = jnp.clip(step - FIRST_QUAD, 0, QUADS * TILES - 1)
    g, tile = at_quad // TILES, at_quad % TILES

    if fused:
        (mine, other, dmine, dother, terms, send, got, xa, yb, ya, xb, gz, dz, vlow, vgot, sends, recvs, d_sends, d_recvs,
         v_sends, v_recvs) = comm
        peers = Peers(nz)
        down = Finish(peers, lambda at: dsum_ref.at[at], dz, dmine, dother, d_sends, d_recvs)

        def stages_of(n):
            return Stages(
                peers, terms.at[n], {"xa": xa.at[n], "yb": yb.at[n], "ya": ya.at[n], "xb": xb.at[n]}, sends.at[n],
                recvs.at[n],
            )

        def finish_of(n):
            return Finish(
                peers, lambda at: terms.at[n, peers.x, at, peers.y], gz.at[n], mine.at[n], other.at[n],
                sends.at[n], recvs.at[n],
            )

        def chip(n):
            return copy_to(send.at[n % 2], got.at[n % 2], sends.at[n], recvs.at[n], 0, peers.sibling)

        def add_chip(n):
            chip(n).wait()
            for h in range(2):
                terms[n, h] = plus(terms[n, h], got[n % 2, h])
            for copy in stages_of(n).first():
                copy.start()

        def add_first(n):
            stages_of(n).add_first()
            for copy in stages_of(n).second():
                copy.start()

        def add_second(n):
            stages_of(n).add_second()
            for copy in finish_of(n).along_z():
                copy.start()

        def add_z(n):
            finish_of(n).add()
            finish_of(n).along_x().start()

        def last(n):
            finish_of(n).along_x().wait()

        usual, hurried = (1, 3, 5, 7, 8), (1, 2, 3, 4, STEPS)
        ready = [*range(UPS + 1)] + [FIRST_QUAD + TILES * (q + 1) - 1 for q in range(QUADS)]

        def settle():
            for stage, action in enumerate((add_chip, add_first, add_second, add_z, last)):
                at = [t + (hurried if n == PIECES - 1 else usual)[stage] for n, t in enumerate(ready)]
                due, piece = step == at[0], jnp.int32(0)
                for n in range(1, PIECES):
                    due = due | (step == at[n])
                    piece = jnp.where(step == at[n], n, piece)
                pl.when(due)(functools.partial(action, piece))

        def vector_copy(n, device):
            return copy_to(vlow, vgot.at[n], v_sends, v_recvs, n, device)

        routes = [[peers.sibling], [peers.over_x], [peers.over_y], peers.over_z]

        def vector_copies(hop):
            return [vector_copy(hop + k, device) for k, device in enumerate(routes[hop])]

        @pl.when(step == 0)
        def _():
            peers.greet([peers.sibling, peers.over_x, peers.over_y, *peers.over_z])

    @pl.when(step == 0)
    def _():
        weight.start()
        vec[...] = jnp.zeros_like(vec)
        vec[2:3, :] = one_ref[2:3, :]
        vec[3:5, :] = one_ref[0:2, :]
        vec[5:6, :] = two_ref[2:3, :]
        vec[6:8, :] = two_ref[0:2, :]
        for c in range(UPS):
            vec[8 + c : 9 + c, :] = upsum_ref[:, c * width : (c + 1) * width]

    @pl.when(step < UPS)
    def _():
        value = tn(low_ref[...], up_ref[...])
        if fused:
            acc[...] = value
        else:
            upg_ref[...] = value.astype(BF)

    @pl.when((step >= FIRST_QUAD) & (step < FIRST_INPUT))
    def _():
        mask = head_mask(quad)
        scale = (quad // QUAD) ** -0.5
        here = lambda size, s=0: pl.ds(pl.multiple_of(tile * rows + s * seq, seq), size)
        def sentences(which):
            k = [k_ref[s * seq : (s + 1) * seq, :] for s in which]
            low = [p_ref[s] for s in which]
            p = [v.astype(F32) for v in low]
            dctx = [blocked(dctx_ref[s * seq : (s + 1) * seq, :], mask) for s in which]
            d_probs = [nt(v_ref[s * seq : (s + 1) * seq, :], c) for s, c in zip(which, dctx, strict=True)]
            d_scores = [
                (a * (b - jnp.sum(a * b, axis=0, keepdims=True))).astype(BF) for a, b in zip(p, d_probs, strict=True)
            ]
            d_value = [nn(a, b).astype(BF) for a, b in zip(low, dctx, strict=True)]
            d_query = [(paired(a, b, seq) * scale).astype(BF) for a, b in zip(d_scores, k, strict=True)]
            d_key = [
                (nn(a, blocked(q_ref[s * seq : (s + 1) * seq, :], mask)) * scale).astype(BF)
                for s, a in zip(which, d_scores, strict=True)
            ]
            out = []
            for s, *three in zip(which, d_query, d_key, d_value, strict=True):
                out.append(jnp.concatenate(three, axis=1))
                dqkv[g, here(seq, s), :] = out[-1]
            return out

        grads = jnp.concatenate(sentences(range(sents)), axis=0)
        part = tn(x_ref[...], grads)
        q_sum = jnp.sum(grads[:, :quad].astype(F32), axis=0, keepdims=True)
        v_sum = jnp.sum(grads[:, 2 * quad :].astype(F32), axis=0, keepdims=True)
        for q in range(QUADS):

            @pl.when(g == q)
            def _(q=q):
                vec[0:1, q * quad : (q + 1) * quad] += q_sum
                vec[1:2, q * quad : (q + 1) * quad] += v_sum

        @pl.when(tile == 0)
        def _():
            acc[...] = part

        @pl.when(tile > 0)
        def _():
            acc[...] += part

    if fused:

        @pl.when(step == 0)
        def _():
            peers.met(2 + nz)
            for copy in down.along_z():
                copy.start()

        settle()

        @pl.when(step == UPS)
        def _():
            for h in range(2):
                terms[OUT_PIECE, h] = owg_ref[0, h]
                send[OUT_PIECE % 2, h] = owg_ref[1, h]
            chip(OUT_PIECE).start()

        done_quad = (step >= FIRST_QUAD) & (step < FIRST_INPUT) & (tile == TILES - 1)

        @pl.when((step < UPS) | done_quad)
        def _():
            n = jnp.where(step < UPS, UP_PIECE + step, QUAD_PIECE + g)
            hand_out(acc, terms.at[n], send.at[n % 2])
            chip(n).start()

        @pl.when(step == FIRST_INPUT - 1)
        def _():
            vlow[...] = vec[...].astype(BF)
            for copy in vector_copies(0):
                copy.start()

        for hop in range(4):

            @pl.when(step == FIRST_INPUT + hop)
            def _(hop=hop):
                for copy in vector_copies(hop):
                    copy.wait()
                vec[...] = vlow[...].astype(F32) + sum(vgot[hop + k].astype(F32) for k in range(len(routes[hop])))
                if hop < 3:
                    vlow[...] = vec[...].astype(BF)
                    for copy in vector_copies(hop + 1):
                        copy.start()

        @pl.when(step == 4)
        def _():
            down.add()
            down.along_x().start()

        @pl.when(step == 7)
        def _():
            down.along_x().wait()

    else:

        @pl.when((step >= FIRST_QUAD) & (step < FIRST_INPUT) & (tile == TILES - 1))
        def _():
            qkvg_ref[...] = acc[...].astype(BF)

    @pl.when(step == FIRST_INPUT)
    def _():
        weight.wait()

    @pl.when(step >= FIRST_INPUT)
    def _():
        here = pl.ds(pl.multiple_of((step - FIRST_INPUT) * rows, rows), rows)
        grads = jnp.concatenate(
            [dqkv[q, here, part * quad : (part + 1) * quad] for part in range(3) for q in range(QUADS)], axis=1
        )
        out_ref[...] = nt(grads, w_ref[...]).astype(BF)

    @pl.when(step == STEPS - 1)
    def _():
        if fused:
            last(PIECES - 1)
        vec_out[...] = vec[...]
        if fused:
            for ref, value in zip(outs, (mine, other, dmine, dother), strict=True):
                ref[...] = value[...]


def tail(low, d_up, qkv, d_ctx, probs, token_rows, qkv_weight, owg, dsum, one, two, upsum, sizes):
    fused = sizes == (16, 2)
    nz = sizes[0] // 4
    sents, seq, width = probs.shape
    rows = sents * seq
    side = rows // TILES
    quad = width // QUADS
    shard, half = width // sizes[0], width // 2
    at = lambda i: jnp.clip(i - FIRST_QUAD, 0, QUADS * TILES - 1)
    cols = lambda part: pl.BlockSpec((side, quad), lambda i: (at(i) % TILES, part * QUADS + at(i) // TILES))
    once = lambda *shape: pl.BlockSpec(shape, lambda i: (0,) * len(shape))
    finish = lambda lanes: pl.BlockSpec((side, lanes), lambda i: (jnp.maximum(i - FIRST_INPUT, 0), 0))
    dma = pltpu.SemaphoreType.DMA
    scratch = [
        pltpu.VMEM(qkv_weight.shape, BF), dma, pltpu.VMEM((QUADS, rows, width), BF),
        pltpu.VMEM((width, width), F32), pltpu.VMEM((VECTORS, width), F32),
    ]
    out_specs = [finish(width), once(VECTORS, width)]
    out_shape = [shape_of((rows, width), BF), shape_of((VECTORS, width), F32)]
    if fused:
        piece = (2, nz, 2, shard, half)
        scratch += [pltpu.VMEM((PIECES, shard, half), BF)] * 2 + [pltpu.VMEM(dsum.shape[1:], BF)] * 2
        scratch += [pltpu.VMEM((PIECES, *piece), BF), pltpu.VMEM((2, *piece), BF), pltpu.VMEM((2, *piece), BF)]
        scratch += [pltpu.VMEM((PIECES, *s), BF) for s in Stages.scratch(nz, shard, half).values()]
        scratch += [
            pltpu.VMEM((PIECES, nz - 1, shard, half), BF), pltpu.VMEM((nz - 1, *dsum.shape[1:]), BF),
            pltpu.VMEM((VECTORS, width), BF), pltpu.VMEM((2 + nz, VECTORS, width), BF),
        ]
        scratch += [dma((PIECES, Stages.SEMS))] * 2 + [dma((Stages.SEMS,))] * 2 + [dma((2 + nz,))] * 2
        out_specs += [once(PIECES, shard, half)] * 2 + [once(*dsum.shape[1:])] * 2
        out_shape += [shape_of((PIECES, shard, half), BF)] * 2 + [shape_of(dsum.shape[1:], BF)] * 2
        extra = dict(collective_id=2, has_side_effects=True)
    else:
        out_specs += [
            pl.BlockSpec((width, width), lambda i: (0, jnp.minimum(i, UPS - 1))),
            pl.BlockSpec((width, width), lambda i: (0, at(i) // TILES)),
        ]
        out_shape += [shape_of((width, UPS * width), BF), shape_of((width, QUADS * width), BF)]
        extra = {}
    return pl.pallas_call(
        functools.partial(tail_kernel, fused, nz),
        grid=(STEPS,),
        in_specs=[
            resident((rows, width)), pl.BlockSpec((rows, width), lambda i: (0, jnp.minimum(i, UPS - 1))),
            cols(0), cols(1), cols(2), cols(0),
            pl.BlockSpec((SIDE, seq, quad), lambda i: (at(i) % TILES, 0, at(i) // TILES)),
            pl.BlockSpec((side, width), lambda i: (at(i) % TILES, 0)),
            pl.BlockSpec(memory_space=pl.ANY), resident(owg.shape), resident(dsum.shape), resident(one.shape),
            resident(two.shape), resident(upsum.shape),
        ],
        out_specs=out_specs,
        out_shape=out_shape,
        scratch_shapes=scratch,
        compiler_params=params(**extra),
        name="tail",
    )(low, d_up, qkv, qkv, qkv, d_ctx, probs, token_rows, qkv_weight, owg, dsum, one, two, upsum)


def finish_kernel(fused, part_ref, attn_ref, *refs):
    if not fused:
        (input_ref,) = refs
    else:
        (mine_ref, other_ref, dmine_ref, dother_ref, vec_ref, input_ref, qkv_ref, qb_ref, vb_ref, out_ref, ob_ref,
         g1_ref, s1_ref, up_ref, ub_ref, down_ref, db_ref, g2_ref, s2_ref) = refs
    input_ref[...] = part_ref[...].astype(F32) + attn_ref[...].astype(F32)
    if not fused:
        return

    @pl.when(pl.program_id(0) == 0)
    def _():
        wide, narrow, z, _, _ = place()
        width = vec_ref.shape[1]
        shard = qb_ref.shape[0]

        def whole(mine, other):
            mine, other = mine.astype(F32), other.astype(F32)
            return jnp.concatenate([jnp.where(narrow == 0, mine, other), jnp.where(narrow == 0, other, mine)], axis=-1)

        for n in range(UPS):
            up_ref[:, n * width : (n + 1) * width] = whole(mine_ref[UP_PIECE + n], other_ref[UP_PIECE + n])
        out_ref[...] = whole(mine_ref[OUT_PIECE], other_ref[OUT_PIECE])
        quad = width // QUADS
        for q in range(QUADS):
            block = whole(mine_ref[QUAD_PIECE + q], other_ref[QUAD_PIECE + q])
            for part in range(3):
                to = part * width + q * quad
                qkv_ref[:, to : to + quad] = block[:, part * quad : (part + 1) * quad]
        down_ref[...] = whole(dmine_ref[...], dother_ref[...])
        rolled = pltpu.roll(vec_ref[...], lax.rem(width - wide * shard, width), 1)
        for n, ref in enumerate((qb_ref, vb_ref, ob_ref, g1_ref, s1_ref, db_ref, g2_ref, s2_ref)):
            ref[...] = rolled[n, :shard]
        depth = ub_ref.shape[0]
        ups = jnp.concatenate([vec_ref[pl.ds(8 + z, 1), :]] * 8, axis=0)
        ub_ref[...] = pltpu.roll(ups, lax.rem(width - lax.rem(wide, 4) * depth, width), 1)[0, :depth]


def finish(part, d_attn, sums, sizes, depth):
    fused = bool(sums)
    rows, width = part.shape
    side = rows // TILES
    shard = width // sizes[0]
    tile = pl.BlockSpec((side, width), lambda i: (i, 0))
    shapes = [(rows, width)]
    if fused:
        up = depth // sizes[0]
        vector = (shard,)
        shapes += [
            (shard, 3 * width), vector, vector, (shard, width), vector, vector, vector, (shard, depth), (up,),
            (up, width), vector, vector, vector,
        ]
    return pl.pallas_call(
        functools.partial(finish_kernel, fused),
        grid=(TILES,),
        in_specs=[tile, tile] + [resident(a.shape) for a in sums],
        out_specs=[tile] + [pl.BlockSpec(s, lambda i, n=len(s): (0,) * n) for s in shapes[1:]],
        out_shape=[shape_of(s, F32) for s in shapes],
        compiler_params=params(),
        name="finish",
    )(part, d_attn, *sums)


def per_device(
    sizes, tokens, cotangent, groups, qkv_weight, query_bias, value_bias, out_weight, out_bias, gain_one,
    shift_one, up_weight, up_bias, down_weight, down_bias, gain_two, shift_two,
):
    n_wide, n_narrow = sizes
    sents, seq, width = tokens.shape
    depth = up_weight.shape[1]
    rows = sents * seq
    flat = lambda v: v.reshape(rows, v.shape[-1])

    qkv, probs, ctx = attend(tokens, qkv_weight, query_bias, value_bias)
    low, xh1, rs1, hidden, slope, xh2, rs2, cls, slots = forward(
        tokens, ctx, out_weight, out_bias, gain_one, shift_one, up_weight, up_bias, down_weight, down_bias,
        gain_two, shift_two, sizes,
    )
    gathered = slots.reshape(2, n_wide * n_narrow * (sents // 2), width)
    loss, block_out, d_down, sums_two = ranking(
        gathered, groups, cls, cotangent, xh2, rs2, gain_two, shift_two
    )
    d_up, d_attn, d_ctx, sums_one, up_sum, out_terms, down_terms = backward(
        d_down, flat(hidden), flat(slope), down_weight, up_weight, flat(xh1), flat(rs1), gain_one, out_weight,
        ctx, sizes,
    )
    part, vectors, *sums = tail(
        flat(low), d_up, qkv, d_ctx, probs, flat(tokens), qkv_weight, out_terms, down_terms, sums_one, sums_two,
        up_sum, sizes,
    )
    if sizes == (16, 2):
        input_grad, *grads = finish(part, d_attn, [*sums, vectors], sizes, depth)
    else:
        (input_grad,) = finish(part, d_attn, [], sizes, depth)
        up_terms, qkv_terms = sums
        quad = width // QUADS
        qkv_terms = qkv_terms.reshape(width, QUADS, 3, quad).transpose(0, 2, 1, 3).reshape(width, 3 * width)
        total = lambda v: lax.psum(
            lax.psum_scatter(v, "wide", scatter_dimension=0, tiled=True).astype(F32), "narrow"
        )
        vector = lambda n: total(vectors[n])
        grads = (
            total(qkv_terms), vector(0), vector(1), total(out_terms), vector(2), vector(3), vector(4),
            total(up_terms), total(vectors[8 : 8 + UPS].reshape(-1)), total(down_terms), vector(5), vector(6),
            vector(7),
        )
    return (loss.reshape(()), block_out, input_grad.reshape(sents, seq, width), *grads)


def solution(mesh):
    sizes = (mesh.shape["wide"], mesh.shape["narrow"])
    split = P(("wide", "narrow"), None, None)
    matrix, vector = P("wide", None), P("wide")
    return jax.shard_map(
        functools.partial(per_device, sizes),
        mesh=mesh,
        in_specs=(split, split) + (P(),) * 14,
        out_specs=(
            P(), split, split, matrix, vector, vector, matrix, vector, vector, vector, matrix, vector,
            matrix, vector, vector, vector,
        ),
        check_vma=False,
    )
```

```python
import functools

import jax
import jax.numpy as jnp
from jax import lax
from jax.experimental import pallas as pl
from jax.experimental.pallas import tpu as pltpu
from jax.sharding import PartitionSpec as P

BF = jnp.bfloat16
F32 = jnp.float32
MESH = pl.DeviceIdType.MESH

HEADS = 12
QUAD = 4
SCALE = 40.0
MARGIN = 0.3
EPS = 1e-06
SIDE = 8
VMEM_BYTES = 60 * 2**20


def nn(a, b):
    return lax.dot_general(a, b, (((1,), (0,)), ((), ())), preferred_element_type=F32)


def nt(a, b):
    return lax.dot_general(a, b, (((1,), (1,)), ((), ())), preferred_element_type=F32)


def tn(a, b):
    return lax.dot_general(a, b, (((0,), (0,)), ((), ())), preferred_element_type=F32)


def params(**more):
    return pltpu.CompilerParams(vmem_limit_bytes=VMEM_BYTES, **more)


def resident(shape):
    return pl.BlockSpec(shape, lambda *_: (0,) * len(shape), pipeline_mode=pl.Buffered(1))


def shape_of(shape, dtype):
    return jax.ShapeDtypeStruct(shape, dtype)


def head_mask(quad):
    head = quad // QUAD
    at = lambda axis: lax.broadcasted_iota(jnp.int32, (quad, quad), axis) // head
    return (at(0) == at(1)).astype(F32).astype(BF)


def line(ref):
    return ref[...].reshape(1, ref.shape[0])


def blocked(rows, mask):
    return jnp.concatenate([rows] * QUAD, axis=0) * mask


def diagonal(full, seq):
    half = full.shape[1] // 2
    lane = lax.broadcasted_iota(jnp.int32, (seq, half), 1) < half // 2
    left = jnp.where(lane, full[:seq, :half], full[seq : 2 * seq, :half])
    right = jnp.where(lane, full[2 * seq : 3 * seq, half:], full[3 * seq :, half:])
    return jnp.concatenate([left, right], axis=1)


def paired(left, right, seq):
    half = left.shape[1] // 2
    lane = lax.broadcasted_iota(jnp.int32, (seq, half), 1) < half // 2
    parts = []
    for at in (slice(0, half), slice(half, 2 * half)):
        full = tn(left[:, at], right[:, at])
        parts.append(jnp.where(lane, full[:seq], full[seq:]))
    return jnp.concatenate(parts, axis=1)


def attend_kernel(x_ref, w_ref, qb_ref, vb_ref, qkv_ref, p_ref, ctx_ref):
    sents, seq, width = x_ref.shape
    rows = x_ref[...].reshape(sents * seq, width)
    quad = width // QUADS
    for part, bias in ((0, qb_ref), (1, None), (2, vb_ref)):
        cols = slice(part * width, (part + 1) * width)
        y = nn(rows, w_ref[:, cols])
        if bias is not None:
            y = y + line(bias)
        qkv_ref[:, cols] = y.astype(BF)
    mask = head_mask(quad)
    scale = (width // HEADS) ** -0.5
    units = [(s, g) for s in range(sents) for g in range(width // quad)]
    for first in range(0, len(units), 12):
        some = units[first : first + 12]
        rows_of = lambda s: slice(s * seq, (s + 1) * seq)
        cols_of = lambda g, part: slice(part * width + g * quad, part * width + (g + 1) * quad)
        scores = [
            nt(qkv_ref[rows_of(s), cols_of(g, 1)], blocked(qkv_ref[rows_of(s), cols_of(g, 0)], mask)) * scale
            for s, g in some
        ]
        e = [jnp.exp(v - jnp.max(v, axis=0, keepdims=True)) for v in scores]
        p = [(v * (1.0 / jnp.sum(v, axis=0, keepdims=True))).astype(BF) for v in e]
        for (s, g), low in zip(some, p, strict=True):
            p_ref[s, :, cols_of(g, 0)] = low
            v = qkv_ref[rows_of(s), cols_of(g, 2)]
            ctx_ref[rows_of(s), cols_of(g, 0)] = diagonal(tn(low, v), seq).astype(BF)


def attend(tokens, qkv_weight, query_bias, value_bias):
    sents, seq, width = tokens.shape
    rows = sents * seq
    side = SIDE * seq
    return pl.pallas_call(
        attend_kernel,
        grid=(sents // SIDE,),
        in_specs=[
            pl.BlockSpec((SIDE, seq, width), lambda i: (i, 0, 0)),
            resident((width, 3 * width)),
            resident((width,)),
            resident((width,)),
        ],
        out_specs=[
            pl.BlockSpec((side, 3 * width), lambda i: (i, 0)),
            pl.BlockSpec((SIDE, seq, width), lambda i: (i, 0, 0)),
            pl.BlockSpec((side, width), lambda i: (i, 0)),
        ],
        out_shape=[
            shape_of((rows, 3 * width), BF),
            shape_of((sents, seq, width), BF),
            shape_of((rows, width), BF),
        ],
        compiler_params=params(),
        name="attend",
    )(tokens, qkv_weight, query_bias, value_bias)


def norm(values):
    mean = jnp.mean(values, -1, keepdims=True)
    centred = values - mean
    root = lax.rsqrt(jnp.mean(centred * centred, -1, keepdims=True) + EPS)
    return centred * root, root


def place():
    wide, narrow = lax.axis_index("wide"), lax.axis_index("narrow")
    return wide, narrow, wide // 4, (wide // 2) % 2, wide % 2


def forward_kernel(
    x_ref, ctx_ref, ow_ref, ob_ref, g1_ref, s1_ref, uw_hbm, ub_ref, dw_hbm, db_ref, g2_ref, s2_ref,
    low_ref, xh1_ref, rs1_ref, hid_ref, slope_ref, xh2_ref, rs2_ref, cls_ref, all_ref,
    rows_ref, uw_ref, dw_ref, w_sems, buf, zs, zr, ys, yr, xs, xr, cs, cr, done,
):
    sents, part, width = x_ref.shape
    depth = uw_ref.shape[1]
    rows = sents * part
    step = pl.program_id(0)
    wide, narrow, z, y, core = place()
    nz, nx = buf.shape[1], buf.shape[4]
    wide_of = lambda a, b, c: (a * 2 + b) * 2 + c
    z_peers = [(lax.rem(z + k, nz), k) for k in range(1, nz)]
    x_peers = [(lax.rem(narrow + k, nx), k) for k in range(1, nx)]

    def gather_copy(slots, sems, at, device):
        return pltpu.make_async_remote_copy(
            src_ref=buf.at[slots], dst_ref=buf.at[slots], send_sem=sems[0].at[at], recv_sem=sems[1].at[at],
            device_id=device, device_id_type=MESH,
        )

    every = slice(None)
    z_copies = [
        gather_copy((every, z, y, core, narrow), (zs, zr), k - 1, (wide_of(to, y, core), narrow))
        for to, k in z_peers
    ]

    def over_y(half, xs_held, at):
        return gather_copy((half, every, y, core, xs_held), (ys, yr), at, (wide_of(z, 1 - y, core), narrow))

    def over_x(half, ys_held, first):
        return [
            gather_copy((half, every, ys_held, core, narrow), (xs, xr), first + k - 1, (wide, to)) for to, k in x_peers
        ]

    second = [over_y(0, narrow, 0), *over_x(1, y, 0)]
    third = [*over_x(0, every, nx - 1), over_y(1, every, 1)]
    core_copy = gather_copy((every, every, every, core), (cs, cr), 0, (wide_of(z, y, 1 - core), narrow))

    barrier = pltpu.get_barrier_semaphore()
    weights = [
        pltpu.make_async_copy(uw_hbm, uw_ref, w_sems.at[0]), pltpu.make_async_copy(dw_hbm, dw_ref, w_sems.at[1])
    ]

    @pl.when(step == 0)
    def _():
        for copy in weights:
            copy.start()
        for to, _ in z_peers:
            pl.semaphore_signal(barrier, inc=1, device_id=(wide_of(to, y, core), narrow), device_id_type=MESH)
        pl.semaphore_signal(barrier, inc=1, device_id=(wide_of(z, 1 - y, core), narrow), device_id_type=MESH)
        for to, _ in x_peers:
            pl.semaphore_signal(barrier, inc=1, device_id=(wide, to), device_id_type=MESH)
        pl.semaphore_signal(barrier, inc=1, device_id=(wide_of(z, y, 1 - core), narrow), device_id_type=MESH)

    block = lambda ref: ref[...].reshape(rows, ref.shape[2])

    def put(ref, value):
        ref[...] = value.astype(ref.dtype).reshape(ref.shape)

    x, ctx = block(x_ref), block(ctx_ref)
    some = rows // 4
    cuts = [slice(i * some, (i + 1) * some) for i in range(4)]
    pre, normals = [], []
    for i, at in enumerate(cuts):
        pre.append(x[at].astype(F32) + nn(ctx[at], ow_ref[...]) + line(ob_ref))
        if i:
            normals.append(norm(pre[i - 1]))
    normals.append(norm(pre[-1]))
    xh1 = jnp.concatenate([a for a, _ in normals], axis=0)
    rs1 = jnp.concatenate([b for _, b in normals], axis=0)
    normed = xh1 * line(g1_ref) + line(s1_ref)
    low = normed.astype(BF)
    put(low_ref, low)
    put(xh1_ref, xh1)
    put(rs1_ref, jnp.broadcast_to(rs1, (rows, 128)))
    total = normed + line(db_ref)

    @pl.when(step == 0)
    def _():
        for copy in weights:
            copy.wait()

    def up_of(c):
        cols = slice(c * width, (c + 1) * width)
        return nn(low, uw_ref[:, cols]) + ub_ref[cols].reshape(1, width)

    chunks = depth // width
    ahead = up_of(0)
    for c in range(chunks):
        if c == 2:

            @pl.when(step == 0)
            def _():
                pl.semaphore_wait(barrier, nz + nx)

            @pl.when(step == 2)
            def _():
                for copy in second:
                    copy.wait()
                for copy in third:
                    copy.start()

            @pl.when(step == 3)
            def _():
                for copy in third:
                    copy.wait()
                core_copy.start()

        cols = slice(c * width, (c + 1) * width)
        up = ahead
        if c + 1 < chunks:
            ahead = up_of(c + 1)
        cdf = 0.5 * (lax.erf(up * 0.7071067811865476) + 1.0)
        slope = cdf + up * (0.3989422804014327 * jnp.exp(-0.5 * up * up))
        hidden = (up * cdf).astype(BF)
        hid_ref[:, :, cols] = hidden.reshape(sents, part, width)
        slope_ref[:, :, cols] = slope.astype(BF).reshape(sents, part, width)
        total = total + nn(hidden, dw_ref[cols, :])
    xh2, rs2 = norm(total)
    final = xh2 * line(g2_ref) + line(s2_ref)
    put(xh2_ref, xh2)
    put(rs2_ref, jnp.broadcast_to(rs2, (rows, 128)))

    @pl.when(step == 0)
    def _():
        for s in range(sents):
            cls_ref[s : s + 1, :] = final[s * part : s * part + 1, :]
        cls = cls_ref[...]
        pooled = cls * lax.rsqrt(jnp.sum(cls * cls, -1, keepdims=True) + EPS)
        for s in range(sents):
            rows_ref[s % 2, s // 2 : s // 2 + 1, :] = pooled[s : s + 1, :]
        for half in range(2):
            buf[half, z, y, core, narrow] = rows_ref[half].astype(BF)
        for copy in z_copies:
            copy.start()

    @pl.when(step == 1)
    def _():
        for copy in z_copies:
            copy.wait()
        for copy in second:
            copy.start()

    @pl.when(step == 3)
    def _():
        core_copy.wait()
        out = pltpu.make_async_copy(buf, all_ref, done)
        out.start()
        out.wait()


def forward(tokens, ctx, ow, ob, g1, s1, uw, ub, dw, db, g2, s2, sizes):
    sents, seq, width = tokens.shape
    depth = uw.shape[1]
    part = seq // 4
    nz, nx = sizes[0] // 4, sizes[1]
    tile = lambda lanes: pl.BlockSpec((sents, part, lanes), lambda i: (0, i, 0))
    whole = lambda lanes, dtype: shape_of((sents, seq, lanes), dtype)
    slots = (2, nz, 2, 2, nx, sents // 2, width)
    dma = pltpu.SemaphoreType.DMA
    return pl.pallas_call(
        forward_kernel,
        grid=(4,),
        in_specs=[
            tile(width), tile(width), resident(ow.shape), resident(ob.shape), resident(g1.shape),
            resident(s1.shape), pl.BlockSpec(memory_space=pl.ANY), resident(ub.shape),
            pl.BlockSpec(memory_space=pl.ANY),
            resident(db.shape), resident(g2.shape), resident(s2.shape),
        ],
        out_specs=[
            tile(width), tile(width), tile(128), tile(depth), tile(depth), tile(width),
            tile(128), pl.BlockSpec((sents, width), lambda i: (0, 0)), pl.BlockSpec(memory_space=pl.ANY),
        ],
        out_shape=[
            whole(width, BF), whole(width, BF), whole(128, F32), whole(depth, BF),
            whole(depth, BF), whole(width, BF), whole(128, F32), shape_of((sents, width), F32),
            shape_of(slots, BF),
        ],
        scratch_shapes=[
            pltpu.VMEM((2, sents // 2, width), F32), pltpu.VMEM(uw.shape, BF), pltpu.VMEM(dw.shape, BF), dma((2,)),
            pltpu.VMEM(slots, BF),
            dma((nz - 1,)), dma((nz - 1,)), dma((2,)), dma((2,)), dma((2 * nx - 2,)), dma((2 * nx - 2,)), dma((1,)),
            dma((1,)), dma,
        ],
        compiler_params=params(collective_id=0, has_side_effects=True),
        name="forward",
    )(tokens, ctx.reshape(sents, seq, width), ow, ob, g1, s1, uw, ub, dw, db, g2, s2)


def ranking_kernel(
    all_ref, group_ref, cls_ref, cot_ref, xh2_ref, rs2_ref, g2_ref, s2_ref,
    loss_ref, out_ref, down_ref, sums_ref, dcls, gcol_ref,
):
    _, pairs, width = all_ref.shape
    own = cls_ref.shape[0] // 2
    step = pl.program_id(0)

    @pl.when(step == 0)
    def _():
        first = (lax.axis_index("wide") * lax.axis_size("narrow") + lax.axis_index("narrow")) * own
        strip = min(256, pairs)
        groups = line(group_ref)
        gcol_ref[...] = jnp.transpose(jnp.broadcast_to(groups, (128, pairs)))
        own_rows = pl.ds(pl.multiple_of(first, own), own)

        def logits_of(left, right, start):
            count = left.shape[0]
            same_at = lax.broadcasted_iota(jnp.int32, (count, pairs), 0) + start
            pair_at = lax.broadcasted_iota(jnp.int32, (count, pairs), 1)
            hit = same_at == pair_at
            return nt(left, right) * SCALE - jnp.where(hit, SCALE * MARGIN, 0.0), hit

        def column_lse(left_at, right_at):
            right = all_ref[right_at]

            def strip_step(at, carry):
                top, total, diag = carry
                start = pl.multiple_of(at * strip, strip)
                left = all_ref[left_at, pl.ds(start, strip), :]
                logits, hit = logits_of(left, right, start)
                masked = jnp.where(gcol_ref[pl.ds(start, strip), :1] == groups, logits, -1e30)
                peak = jnp.maximum(top, jnp.max(masked, axis=0, keepdims=True))
                total = total * jnp.exp(top - peak) + jnp.sum(jnp.exp(masked - peak), axis=0, keepdims=True)
                diag = diag + jnp.sum(jnp.where(hit, logits, 0.0), axis=0, keepdims=True)
                return peak, total, diag

            start = (jnp.full((1, pairs), -1e30, F32), jnp.zeros((1, pairs), F32), jnp.zeros((1, pairs), F32))
            top, total, diag = lax.fori_loop(0, pairs // strip, strip_step, start)
            return top + jnp.log(total), diag

        col_lse, diag = column_lse(0, 1)
        row_lse, diag_again = column_lse(1, 0)
        loss_ref[...] = jnp.sum(col_lse - diag + row_lse - diag_again, axis=1, keepdims=True) / pairs

        same = gcol_ref[own_rows, :1] == groups

        def side(my_at, other_at, other_lse):
            other = all_ref[other_at]
            mine = all_ref[my_at, own_rows, :]
            logits, hit = logits_of(mine, other, first)
            eye = hit.astype(F32)
            masked = jnp.where(same, logits, -1e30)
            e = jnp.exp(masked - jnp.max(masked, axis=1, keepdims=True))
            d_mine = (e / jnp.sum(e, axis=1, keepdims=True) - eye).astype(BF)
            d_other = (jnp.where(same, jnp.exp(masked - other_lse), 0.0) - eye).astype(BF)
            return (nn(d_mine, other) + nn(d_other, other)) * SCALE

        for at, (other, lse) in enumerate(((1, col_lse), (0, row_lse))):
            terms = side(at, other, lse)
            for p in range(own):
                dcls[2 * p + at : 2 * p + at + 1, :] = terms[p : p + 1, :]
        d = dcls[...]
        c = cls_ref[...]
        root = lax.rsqrt(jnp.sum(c * c, -1, keepdims=True) + EPS)
        dcls[...] = root * d - root * root * root * c * jnp.sum(c * d, -1, keepdims=True)
        sums_ref[...] = jnp.zeros_like(sums_ref)

    side_sents, seq, _ = cot_ref.shape
    rows = side_sents * seq
    start = pl.multiple_of(step * side_sents, side_sents)
    extra = dcls[pl.ds(start, side_sents), :]
    at_zero = lax.broadcasted_iota(jnp.int32, (side_sents, seq, width), 1) == 0
    d_final = cot_ref[...].astype(F32) + jnp.where(at_zero, extra[:, None, :], 0.0)
    d_final = d_final.reshape(rows, width)
    xhat = xh2_ref[...].reshape(rows, width).astype(F32)
    root = rs2_ref[...].reshape(rows, 128)[:, :1]
    out_ref[...] = (xhat * line(g2_ref) + line(s2_ref)).astype(BF).reshape(out_ref.shape)
    e = d_final * line(g2_ref)
    d_pre = (e - jnp.mean(e, -1, keepdims=True) - xhat * jnp.mean(e * xhat, -1, keepdims=True)) * root
    d_down = d_pre.astype(BF)
    down_ref[...] = d_down
    sums_ref[0:1, :] += jnp.sum(d_final * xhat, axis=0, keepdims=True)
    sums_ref[1:2, :] += jnp.sum(d_final, axis=0, keepdims=True)
    sums_ref[2:3, :] += jnp.sum(d_down.astype(F32), axis=0, keepdims=True)


def ranking(gathered, groups, cls, cotangent, xh2, rs2, g2, s2):
    sents, seq, width = cotangent.shape
    pairs = gathered.shape[1]
    tile = lambda lanes: pl.BlockSpec((SIDE, seq, lanes), lambda i: (i, 0, 0))
    return pl.pallas_call(
        ranking_kernel,
        grid=(sents // SIDE,),
        in_specs=[
            resident(gathered.shape), resident(groups.shape), resident(cls.shape), tile(width), tile(width), tile(128),
            resident(g2.shape), resident(s2.shape),
        ],
        out_specs=[
            pl.BlockSpec((1, 1), lambda i: (0, 0)), tile(width),
            pl.BlockSpec((SIDE * seq, width), lambda i: (i, 0)),
            pl.BlockSpec((8, width), lambda i: (0, 0)),
        ],
        out_shape=[shape_of((1, 1), F32), shape_of(cotangent.shape, BF), shape_of((sents * seq, width), BF), shape_of((8, width), F32)],
        scratch_shapes=[pltpu.VMEM((sents, width), F32), pltpu.VMEM((pairs, 128), jnp.int32)],
        compiler_params=params(),
        name="ranking",
    )(gathered, groups, cls, cotangent, xh2, rs2, g2, s2)


def copy_to(src, dst, sends, recvs, at, device):
    return pltpu.make_async_remote_copy(
        src_ref=src, dst_ref=dst, send_sem=sends.at[at], recv_sem=recvs.at[at], device_id=device,
        device_id_type=MESH,
    )


def plus(*terms):
    if len(terms) == 2:
        return terms[0] + terms[1]
    return sum(t.astype(F32) for t in terms).astype(BF)


class Peers:
    def __init__(self, nz):
        self.nz = nz
        wide, self.x, self.z, self.y, self.core = place()
        self.sibling = (wide + 1 - 2 * self.core, self.x)
        self.over_x = (wide, 1 - self.x)
        self.over_y = (wide + 2 - 4 * self.y, self.x)
        self.zs = [lax.rem(self.z + k, nz) for k in range(1, nz)]
        self.over_z = [(lax.rem(wide + 4 * k, 4 * nz), self.x) for k in range(1, nz)]

    def greet(self, devices):
        barrier = pltpu.get_barrier_semaphore()
        for device in devices:
            pl.semaphore_signal(barrier, inc=1, device_id=device, device_id_type=MESH)

    def met(self, count):
        pl.semaphore_wait(pltpu.get_barrier_semaphore(), count)


class Stages:
    SEMS = 9

    def __init__(self, peers, terms, got, sends, recvs):
        self.peers, self.terms, self.got, self.sends, self.recvs = peers, terms, got, sends, recvs
        self.half = peers.nz // 2

    @staticmethod
    def scratch(nz, rows, cols):
        half = nz // 2
        return {
            "xa": (half, 2, rows, cols), "yb": (2, nz - half, rows, cols), "ya": (half, rows, cols),
            "xb": (nz - half, rows, cols),
        }

    def first_of(self, z, at):
        p = self.peers
        if z < self.half:
            return copy_to(self.terms.at[1 - p.x, z], self.got["xa"].at[z], self.sends, self.recvs, at, p.over_x)
        return copy_to(
            self.terms.at[:, z, 1 - p.y], self.got["yb"].at[:, z - self.half], self.sends, self.recvs, at, p.over_y
        )

    def first(self):
        p, h = self.peers, self.half
        return [
            copy_to(self.terms.at[1 - p.x, :h], self.got["xa"], self.sends, self.recvs, 1, p.over_x),
            copy_to(self.terms.at[:, h:, 1 - p.y], self.got["yb"], self.sends, self.recvs, 2, p.over_y),
        ]

    def second(self):
        p, h = self.peers, self.half
        return [
            copy_to(self.terms.at[p.x, :h, 1 - p.y], self.got["ya"], self.sends, self.recvs, 3, p.over_y),
            copy_to(self.terms.at[1 - p.x, h:, p.y], self.got["xb"], self.sends, self.recvs, 4, p.over_x),
        ]

    def add_first(self, copies=None):
        p, h = self.peers, self.half
        for copy in copies or self.first():
            copy.wait()
        self.terms[p.x, :h] = plus(self.terms[p.x, :h], self.got["xa"][...])
        for x in range(2):
            self.terms[x, h:, p.y] = plus(self.terms[x, h:, p.y], self.got["yb"][x])

    def add_second(self):
        p, h = self.peers, self.half
        for copy in self.second():
            copy.wait()
        self.terms[p.x, :h, p.y] = plus(self.terms[p.x, :h, p.y], self.got["ya"][...])
        self.terms[p.x, h:, p.y] = plus(self.terms[p.x, h:, p.y], self.got["xb"][...])


class Finish:
    def __init__(self, peers, shard, got_z, mine, other, sends, recvs):
        self.peers, self.shard, self.got_z, self.mine, self.other = peers, shard, got_z, mine, other
        self.sends, self.recvs = sends, recvs

    def along_z(self):
        p = self.peers
        return [
            copy_to(self.shard(to), self.got_z.at[k], self.sends, self.recvs, 5 + k, device)
            for k, (to, device) in enumerate(zip(p.zs, p.over_z, strict=True))
        ]

    def along_x(self):
        return copy_to(self.mine, self.other, self.sends, self.recvs, 8, self.peers.over_x)

    def add(self):
        for copy in self.along_z():
            copy.wait()
        got = [self.got_z[k] for k in range(self.peers.nz - 1)]
        self.mine[...] = plus(self.shard(self.peers.z)[...], *got)


def hand_out(value, keep, send):
    halves, nz, ny, rows, cols = keep.shape
    core = lax.axis_index("wide") % 2
    for z in range(nz):
        for y in range(ny):
            first = (z * ny + y) * 2 * rows
            for ref, side in ((keep, core), (send, 1 - core)):
                part = value[pl.ds(pl.multiple_of(first + side * rows, rows), rows), :].astype(BF)
                for h in range(halves):
                    ref[h, z, y] = part[:, h * cols : (h + 1) * cols]


def backward_kernel(fused, nz, *refs):
    (down_ref, hid_ref, slope_ref, dw_hbm, uw_hbm, xh1_ref, rs1_ref, g1_ref, ow_ref, actx_ref) = refs[:10]
    (up_ref, attn_ref, ctx_ref, sums_ref, upsum_ref, owg_ref, dwg_ref) = refs[10:17]
    dw_ref, uw_ref, w_sems, owg, *comm = refs[17:]
    blocks = 4
    width = down_ref.shape[1]
    rows, depth = slope_ref.shape
    step = pl.program_id(0)
    weights = [
        pltpu.make_async_copy(dw_hbm, dw_ref, w_sems.at[0]), pltpu.make_async_copy(uw_hbm, uw_ref, w_sems.at[1])
    ]

    if fused:
        terms, send, got, xa, yb, ya, xb, c_send, c_recv, s_send, s_recv = comm
        peers = Peers(nz)
        stages = Stages(peers, terms, {"xa": xa, "yb": yb, "ya": ya, "xb": xb}, s_send, s_recv)

        def exchange(i):
            return copy_to(send.at[i % 2], got.at[i % 2], c_send, c_recv, i, peers.sibling)

    @pl.when(step == 0)
    def _():
        for copy in weights:
            copy.start()
        sums_ref[...] = jnp.zeros_like(sums_ref)
        upsum_ref[...] = jnp.zeros_like(upsum_ref)
        if fused:
            peers.greet([peers.sibling, peers.over_x, peers.over_y])

    def settle(i):
        exchange(i).wait()
        for h in range(2):
            terms[h, i] = plus(terms[h, i], got[i % 2, h, 0])
        for z in range(blocks):
            if isinstance(i, int) and z != i:
                continue

            @pl.when(i == z)
            def _(z=z):
                stages.first_of(z, Stages.SEMS + z).start()

    @pl.when(step < blocks)
    def _():
        value = tn(hid_ref[...], down_ref[...])
        if fused:

            @pl.when(step == 0)
            def _():
                peers.met(3)

            @pl.when(step > 0)
            def _():
                settle(step - 1)

            owg[...] = value
            hand_out(owg, terms.at[:, pl.ds(step, 1)], send.at[step % 2])
            exchange(step).start()

        else:
            dwg_ref[...] = value.astype(BF)

    @pl.when(step == blocks)
    def _():
        for copy in weights:
            copy.wait()

    @pl.when(step >= blocks)
    def _():
        d_down = down_ref[pl.ds(pl.multiple_of((step - blocks) * rows, rows), rows), :]
        total = d_down.astype(F32)
        for c in range(depth // width):
            cols = slice(c * width, (c + 1) * width)
            d_up = (nt(d_down, dw_ref[cols, :]) * slope_ref[:, cols].astype(F32)).astype(BF)
            up_ref[:, cols] = d_up
            upsum_ref[:, cols] += jnp.sum(d_up.astype(F32), axis=0, keepdims=True)
            total = total + nt(d_up, uw_ref[:, cols])
        xhat = xh1_ref[...].astype(F32)
        root = rs1_ref[:, :1]
        e = total * g1_ref[...].reshape(1, width)
        d_pre = (e - jnp.mean(e, -1, keepdims=True) - xhat * jnp.mean(e * xhat, -1, keepdims=True)) * root
        d_attn = d_pre.astype(BF)
        attn_ref[...] = d_attn
        ctx_ref[...] = nt(d_attn, ow_ref[...]).astype(BF)
        sums_ref[0:1, :] += jnp.sum(total * xhat, axis=0, keepdims=True)
        sums_ref[1:2, :] += jnp.sum(total, axis=0, keepdims=True)
        sums_ref[2:3, :] += jnp.sum(d_attn.astype(F32), axis=0, keepdims=True)
        part = tn(actx_ref[...], d_attn)

        @pl.when(step == blocks)
        def _():
            owg[...] = part

        @pl.when(step > blocks)
        def _():
            owg[...] += part

    if fused:

        @pl.when(step == blocks)
        def _():
            settle(blocks - 1)

        @pl.when(step == blocks + 1)
        def _():
            stages.add_first([stages.first_of(z, Stages.SEMS + z) for z in range(blocks)])
            for copy in stages.second():
                copy.start()

    @pl.when(step == pl.num_programs(0) - 1)
    def _():
        if fused:
            hand_out(owg, owg_ref.at[0], owg_ref.at[1])
            stages.add_second()
            dwg_ref[...] = terms[peers.x, :, peers.y]
        else:
            owg_ref[...] = owg[...].astype(BF)


def backward(d_down, hidden, slope, dw, uw, xh1, rs1, g1, ow, ctx, sizes):
    fused = sizes == (16, 2)
    nz = sizes[0] // 4
    rows, width = d_down.shape
    depth = uw.shape[1]
    side = rows // 4
    tile = lambda lanes: pl.BlockSpec((side, lanes), lambda i: (jnp.maximum(i - 4, 0), 0))
    once = lambda *shape: pl.BlockSpec(shape, lambda i: (0,) * len(shape))
    shard = depth // sizes[0]
    half = width // 2
    dma = pltpu.SemaphoreType.DMA
    scratch = [
        pltpu.VMEM(dw.shape, BF), pltpu.VMEM(uw.shape, BF), dma((2,)), pltpu.VMEM((width, width), F32)
    ]
    if fused:
        scratch += [
            pltpu.VMEM((2, nz, 2, shard, half), BF), pltpu.VMEM((2, 2, 1, 2, shard, half), BF),
            pltpu.VMEM((2, 2, 1, 2, shard, half), BF),
        ]
        scratch += [pltpu.VMEM(s, BF) for s in Stages.scratch(nz, shard, half).values()]
        scratch += [dma((4,)), dma((4,)), dma((Stages.SEMS + 4,)), dma((Stages.SEMS + 4,))]
        dwg_spec, dwg_shape = once(nz, shard, half), (nz, shard, half)
        owg_shape = (2, 2, nz, 2, width // sizes[0], half)
        extra = dict(collective_id=1, has_side_effects=True)
    else:
        dwg_spec, dwg_shape = pl.BlockSpec((width, width), lambda i: (jnp.minimum(i, 3), 0)), (depth, width)
        owg_shape = (width, width)
        extra = {}
    return pl.pallas_call(
        functools.partial(backward_kernel, fused, nz),
        grid=(8,),
        in_specs=[
            resident((rows, width)), pl.BlockSpec((rows, width), lambda i: (0, jnp.minimum(i, 3))), tile(depth),
            pl.BlockSpec(memory_space=pl.ANY), pl.BlockSpec(memory_space=pl.ANY), tile(width), tile(128),
            resident(g1.shape), resident(ow.shape), tile(width),
        ],
        out_specs=[
            tile(depth), tile(width), tile(width), once(8, width), once(1, depth), once(*owg_shape), dwg_spec
        ],
        out_shape=[
            shape_of((rows, depth), BF), shape_of((rows, width), BF), shape_of((rows, width), BF),
            shape_of((8, width), F32), shape_of((1, depth), F32), shape_of(owg_shape, BF),
            shape_of(dwg_shape, BF),
        ],
        scratch_shapes=scratch,
        compiler_params=params(**extra),
        name="backward",
    )(d_down, hidden, slope, dw, uw, xh1, rs1, g1, ow, ctx)


UPS, QUADS, TILES = 4, 3, 4
FIRST_QUAD = UPS
FIRST_INPUT = UPS + QUADS * TILES
STEPS = FIRST_INPUT + TILES
UP_PIECE, OUT_PIECE, QUAD_PIECE = 0, UPS, 1 + UPS
PIECES = UPS + 1 + QUADS
VECTORS = 16


def tail_kernel(fused, nz, *refs):
    (low_ref, up_ref, q_ref, k_ref, v_ref, dctx_ref, p_ref, x_ref, w_hbm, owg_ref, dsum_ref,
     one_ref, two_ref, upsum_ref) = refs[:14]
    out_ref, vec_out = refs[14:16]
    if fused:
        outs = refs[16:20]
        w_ref, w_sem, dqkv, acc, vec, *comm = refs[20:]
    else:
        upg_ref, qkvg_ref = refs[16:18]
        w_ref, w_sem, dqkv, acc, vec = refs[18:]
    rows, quad = q_ref.shape
    sents, seq, _ = p_ref.shape
    width = acc.shape[0]
    step = pl.program_id(0)
    weight = pltpu.make_async_copy(w_hbm, w_ref, w_sem)
    at_quad = jnp.clip(step - FIRST_QUAD, 0, QUADS * TILES - 1)
    g, tile = at_quad // TILES, at_quad % TILES

    if fused:
        (mine, other, dmine, dother, terms, send, got, xa, yb, ya, xb, gz, dz, vlow, vgot, sends, recvs, d_sends, d_recvs,
         v_sends, v_recvs) = comm
        peers = Peers(nz)
        down = Finish(peers, lambda at: dsum_ref.at[at], dz, dmine, dother, d_sends, d_recvs)

        def stages_of(n):
            return Stages(
                peers, terms.at[n], {"xa": xa.at[n], "yb": yb.at[n], "ya": ya.at[n], "xb": xb.at[n]}, sends.at[n],
                recvs.at[n],
            )

        def finish_of(n):
            return Finish(
                peers, lambda at: terms.at[n, peers.x, at, peers.y], gz.at[n], mine.at[n], other.at[n],
                sends.at[n], recvs.at[n],
            )

        def chip(n):
            return copy_to(send.at[n % 2], got.at[n % 2], sends.at[n], recvs.at[n], 0, peers.sibling)

        def add_chip(n):
            chip(n).wait()
            for h in range(2):
                terms[n, h] = plus(terms[n, h], got[n % 2, h])
            for copy in stages_of(n).first():
                copy.start()

        def add_first(n):
            stages_of(n).add_first()
            for copy in stages_of(n).second():
                copy.start()

        def add_second(n):
            stages_of(n).add_second()
            for copy in finish_of(n).along_z():
                copy.start()

        def add_z(n):
            finish_of(n).add()
            finish_of(n).along_x().start()

        def last(n):
            finish_of(n).along_x().wait()

        usual, hurried = (1, 3, 5, 7, 8), (1, 2, 3, 4, STEPS)
        ready = [*range(UPS + 1)] + [FIRST_QUAD + TILES * (q + 1) - 1 for q in range(QUADS)]

        def settle():
            for stage, action in enumerate((add_chip, add_first, add_second, add_z, last)):
                at = [t + (hurried if n == PIECES - 1 else usual)[stage] for n, t in enumerate(ready)]
                due, piece = step == at[0], jnp.int32(0)
                for n in range(1, PIECES):
                    due = due | (step == at[n])
                    piece = jnp.where(step == at[n], n, piece)
                pl.when(due)(functools.partial(action, piece))

        def vector_copy(n, device):
            return copy_to(vlow, vgot.at[n], v_sends, v_recvs, n, device)

        routes = [[peers.sibling], [peers.over_x], [peers.over_y], peers.over_z]

        def vector_copies(hop):
            return [vector_copy(hop + k, device) for k, device in enumerate(routes[hop])]

        @pl.when(step == 0)
        def _():
            peers.greet([peers.sibling, peers.over_x, peers.over_y, *peers.over_z])

    @pl.when(step == 0)
    def _():
        weight.start()
        vec[...] = jnp.zeros_like(vec)
        vec[2:3, :] = one_ref[2:3, :]
        vec[3:5, :] = one_ref[0:2, :]
        vec[5:6, :] = two_ref[2:3, :]
        vec[6:8, :] = two_ref[0:2, :]
        for c in range(UPS):
            vec[8 + c : 9 + c, :] = upsum_ref[:, c * width : (c + 1) * width]

    @pl.when(step < UPS)
    def _():
        value = tn(low_ref[...], up_ref[...])
        if fused:
            acc[...] = value
        else:
            upg_ref[...] = value.astype(BF)

    @pl.when((step >= FIRST_QUAD) & (step < FIRST_INPUT))
    def _():
        mask = head_mask(quad)
        scale = (quad // QUAD) ** -0.5
        here = lambda size, s=0: pl.ds(pl.multiple_of(tile * rows + s * seq, seq), size)
        def sentences(which):
            k = [k_ref[s * seq : (s + 1) * seq, :] for s in which]
            low = [p_ref[s] for s in which]
            p = [v.astype(F32) for v in low]
            dctx = [blocked(dctx_ref[s * seq : (s + 1) * seq, :], mask) for s in which]
            d_probs = [nt(v_ref[s * seq : (s + 1) * seq, :], c) for s, c in zip(which, dctx, strict=True)]
            d_scores = [
                (a * (b - jnp.sum(a * b, axis=0, keepdims=True))).astype(BF) for a, b in zip(p, d_probs, strict=True)
            ]
            d_value = [nn(a, b).astype(BF) for a, b in zip(low, dctx, strict=True)]
            d_query = [(paired(a, b, seq) * scale).astype(BF) for a, b in zip(d_scores, k, strict=True)]
            d_key = [
                (nn(a, blocked(q_ref[s * seq : (s + 1) * seq, :], mask)) * scale).astype(BF)
                for s, a in zip(which, d_scores, strict=True)
            ]
            out = []
            for s, *three in zip(which, d_query, d_key, d_value, strict=True):
                out.append(jnp.concatenate(three, axis=1))
                dqkv[g, here(seq, s), :] = out[-1]
            return out

        grads = jnp.concatenate(sentences(range(sents)), axis=0)
        part = tn(x_ref[...], grads)
        q_sum = jnp.sum(grads[:, :quad].astype(F32), axis=0, keepdims=True)
        v_sum = jnp.sum(grads[:, 2 * quad :].astype(F32), axis=0, keepdims=True)
        for q in range(QUADS):

            @pl.when(g == q)
            def _(q=q):
                vec[0:1, q * quad : (q + 1) * quad] += q_sum
                vec[1:2, q * quad : (q + 1) * quad] += v_sum

        @pl.when(tile == 0)
        def _():
            acc[...] = part

        @pl.when(tile > 0)
        def _():
            acc[...] += part

    if fused:

        @pl.when(step == 0)
        def _():
            peers.met(2 + nz)
            for copy in down.along_z():
                copy.start()

        settle()

        @pl.when(step == UPS)
        def _():
            for h in range(2):
                terms[OUT_PIECE, h] = owg_ref[0, h]
                send[OUT_PIECE % 2, h] = owg_ref[1, h]
            chip(OUT_PIECE).start()

        done_quad = (step >= FIRST_QUAD) & (step < FIRST_INPUT) & (tile == TILES - 1)

        @pl.when((step < UPS) | done_quad)
        def _():
            n = jnp.where(step < UPS, UP_PIECE + step, QUAD_PIECE + g)
            hand_out(acc, terms.at[n], send.at[n % 2])
            chip(n).start()

        @pl.when(step == FIRST_INPUT - 1)
        def _():
            vlow[...] = vec[...].astype(BF)
            for copy in vector_copies(0):
                copy.start()

        for hop in range(4):

            @pl.when(step == FIRST_INPUT + hop)
            def _(hop=hop):
                for copy in vector_copies(hop):
                    copy.wait()
                vec[...] = vlow[...].astype(F32) + sum(vgot[hop + k].astype(F32) for k in range(len(routes[hop])))
                if hop < 3:
                    vlow[...] = vec[...].astype(BF)
                    for copy in vector_copies(hop + 1):
                        copy.start()

        @pl.when(step == 4)
        def _():
            down.add()
            down.along_x().start()

        @pl.when(step == 7)
        def _():
            down.along_x().wait()

    else:

        @pl.when((step >= FIRST_QUAD) & (step < FIRST_INPUT) & (tile == TILES - 1))
        def _():
            qkvg_ref[...] = acc[...].astype(BF)

    @pl.when(step == FIRST_INPUT)
    def _():
        weight.wait()

    @pl.when(step >= FIRST_INPUT)
    def _():
        here = pl.ds(pl.multiple_of((step - FIRST_INPUT) * rows, rows), rows)
        grads = jnp.concatenate(
            [dqkv[q, here, part * quad : (part + 1) * quad] for part in range(3) for q in range(QUADS)], axis=1
        )
        out_ref[...] = nt(grads, w_ref[...]).astype(BF)

    @pl.when(step == STEPS - 1)
    def _():
        if fused:
            last(PIECES - 1)
        vec_out[...] = vec[...]
        if fused:
            for ref, value in zip(outs, (mine, other, dmine, dother), strict=True):
                ref[...] = value[...]


def tail(low, d_up, qkv, d_ctx, probs, token_rows, qkv_weight, owg, dsum, one, two, upsum, sizes):
    fused = sizes == (16, 2)
    nz = sizes[0] // 4
    sents, seq, width = probs.shape
    rows = sents * seq
    side = rows // TILES
    quad = width // QUADS
    shard, half = width // sizes[0], width // 2
    at = lambda i: jnp.clip(i - FIRST_QUAD, 0, QUADS * TILES - 1)
    cols = lambda part: pl.BlockSpec((side, quad), lambda i: (at(i) % TILES, part * QUADS + at(i) // TILES))
    once = lambda *shape: pl.BlockSpec(shape, lambda i: (0,) * len(shape))
    finish = lambda lanes: pl.BlockSpec((side, lanes), lambda i: (jnp.maximum(i - FIRST_INPUT, 0), 0))
    dma = pltpu.SemaphoreType.DMA
    scratch = [
        pltpu.VMEM(qkv_weight.shape, BF), dma, pltpu.VMEM((QUADS, rows, width), BF),
        pltpu.VMEM((width, width), F32), pltpu.VMEM((VECTORS, width), F32),
    ]
    out_specs = [finish(width), once(VECTORS, width)]
    out_shape = [shape_of((rows, width), BF), shape_of((VECTORS, width), F32)]
    if fused:
        piece = (2, nz, 2, shard, half)
        scratch += [pltpu.VMEM((PIECES, shard, half), BF)] * 2 + [pltpu.VMEM(dsum.shape[1:], BF)] * 2
        scratch += [pltpu.VMEM((PIECES, *piece), BF), pltpu.VMEM((2, *piece), BF), pltpu.VMEM((2, *piece), BF)]
        scratch += [pltpu.VMEM((PIECES, *s), BF) for s in Stages.scratch(nz, shard, half).values()]
        scratch += [
            pltpu.VMEM((PIECES, nz - 1, shard, half), BF), pltpu.VMEM((nz - 1, *dsum.shape[1:]), BF),
            pltpu.VMEM((VECTORS, width), BF), pltpu.VMEM((2 + nz, VECTORS, width), BF),
        ]
        scratch += [dma((PIECES, Stages.SEMS))] * 2 + [dma((Stages.SEMS,))] * 2 + [dma((2 + nz,))] * 2
        out_specs += [once(PIECES, shard, half)] * 2 + [once(*dsum.shape[1:])] * 2
        out_shape += [shape_of((PIECES, shard, half), BF)] * 2 + [shape_of(dsum.shape[1:], BF)] * 2
        extra = dict(collective_id=2, has_side_effects=True)
    else:
        out_specs += [
            pl.BlockSpec((width, width), lambda i: (0, jnp.minimum(i, UPS - 1))),
            pl.BlockSpec((width, width), lambda i: (0, at(i) // TILES)),
        ]
        out_shape += [shape_of((width, UPS * width), BF), shape_of((width, QUADS * width), BF)]
        extra = {}
    return pl.pallas_call(
        functools.partial(tail_kernel, fused, nz),
        grid=(STEPS,),
        in_specs=[
            resident((rows, width)), pl.BlockSpec((rows, width), lambda i: (0, jnp.minimum(i, UPS - 1))),
            cols(0), cols(1), cols(2), cols(0),
            pl.BlockSpec((SIDE, seq, quad), lambda i: (at(i) % TILES, 0, at(i) // TILES)),
            pl.BlockSpec((side, width), lambda i: (at(i) % TILES, 0)),
            pl.BlockSpec(memory_space=pl.ANY), resident(owg.shape), resident(dsum.shape), resident(one.shape),
            resident(two.shape), resident(upsum.shape),
        ],
        out_specs=out_specs,
        out_shape=out_shape,
        scratch_shapes=scratch,
        compiler_params=params(**extra),
        name="tail",
    )(low, d_up, qkv, qkv, qkv, d_ctx, probs, token_rows, qkv_weight, owg, dsum, one, two, upsum)


def finish_kernel(fused, part_ref, attn_ref, *refs):
    if not fused:
        (input_ref,) = refs
    else:
        (mine_ref, other_ref, dmine_ref, dother_ref, vec_ref, input_ref, qkv_ref, qb_ref, vb_ref, out_ref, ob_ref,
         g1_ref, s1_ref, up_ref, ub_ref, down_ref, db_ref, g2_ref, s2_ref) = refs
    input_ref[...] = part_ref[...].astype(F32) + attn_ref[...].astype(F32)
    if not fused:
        return

    @pl.when(pl.program_id(0) == 0)
    def _():
        wide, narrow, z, _, _ = place()
        width = vec_ref.shape[1]
        shard = qb_ref.shape[0]

        def whole(mine, other):
            mine, other = mine.astype(F32), other.astype(F32)
            return jnp.concatenate([jnp.where(narrow == 0, mine, other), jnp.where(narrow == 0, other, mine)], axis=-1)

        for n in range(UPS):
            up_ref[:, n * width : (n + 1) * width] = whole(mine_ref[UP_PIECE + n], other_ref[UP_PIECE + n])
        out_ref[...] = whole(mine_ref[OUT_PIECE], other_ref[OUT_PIECE])
        quad = width // QUADS
        for q in range(QUADS):
            block = whole(mine_ref[QUAD_PIECE + q], other_ref[QUAD_PIECE + q])
            for part in range(3):
                to = part * width + q * quad
                qkv_ref[:, to : to + quad] = block[:, part * quad : (part + 1) * quad]
        down_ref[...] = whole(dmine_ref[...], dother_ref[...])
        rolled = pltpu.roll(vec_ref[...], lax.rem(width - wide * shard, width), 1)
        for n, ref in enumerate((qb_ref, vb_ref, ob_ref, g1_ref, s1_ref, db_ref, g2_ref, s2_ref)):
            ref[...] = rolled[n, :shard]
        depth = ub_ref.shape[0]
        ups = jnp.concatenate([vec_ref[pl.ds(8 + z, 1), :]] * 8, axis=0)
        ub_ref[...] = pltpu.roll(ups, lax.rem(width - lax.rem(wide, 4) * depth, width), 1)[0, :depth]


def finish(part, d_attn, sums, sizes, depth):
    fused = bool(sums)
    rows, width = part.shape
    side = rows // TILES
    shard = width // sizes[0]
    tile = pl.BlockSpec((side, width), lambda i: (i, 0))
    shapes = [(rows, width)]
    if fused:
        up = depth // sizes[0]
        vector = (shard,)
        shapes += [
            (shard, 3 * width), vector, vector, (shard, width), vector, vector, vector, (shard, depth), (up,),
            (up, width), vector, vector, vector,
        ]
    return pl.pallas_call(
        functools.partial(finish_kernel, fused),
        grid=(TILES,),
        in_specs=[tile, tile] + [resident(a.shape) for a in sums],
        out_specs=[tile] + [pl.BlockSpec(s, lambda i, n=len(s): (0,) * n) for s in shapes[1:]],
        out_shape=[shape_of(s, F32) for s in shapes],
        compiler_params=params(),
        name="finish",
    )(part, d_attn, *sums)


def per_device(
    sizes, tokens, cotangent, groups, qkv_weight, query_bias, value_bias, out_weight, out_bias, gain_one,
    shift_one, up_weight, up_bias, down_weight, down_bias, gain_two, shift_two,
):
    n_wide, n_narrow = sizes
    sents, seq, width = tokens.shape
    depth = up_weight.shape[1]
    rows = sents * seq
    flat = lambda v: v.reshape(rows, v.shape[-1])

    qkv, probs, ctx = attend(tokens, qkv_weight, query_bias, value_bias)
    low, xh1, rs1, hidden, slope, xh2, rs2, cls, slots = forward(
        tokens, ctx, out_weight, out_bias, gain_one, shift_one, up_weight, up_bias, down_weight, down_bias,
        gain_two, shift_two, sizes,
    )
    gathered = slots.reshape(2, n_wide * n_narrow * (sents // 2), width)
    loss, block_out, d_down, sums_two = ranking(
        gathered, groups, cls, cotangent, xh2, rs2, gain_two, shift_two
    )
    d_up, d_attn, d_ctx, sums_one, up_sum, out_terms, down_terms = backward(
        d_down, flat(hidden), flat(slope), down_weight, up_weight, flat(xh1), flat(rs1), gain_one, out_weight,
        ctx, sizes,
    )
    part, vectors, *sums = tail(
        flat(low), d_up, qkv, d_ctx, probs, flat(tokens), qkv_weight, out_terms, down_terms, sums_one, sums_two,
        up_sum, sizes,
    )
    if sizes == (16, 2):
        input_grad, *grads = finish(part, d_attn, [*sums, vectors], sizes, depth)
    else:
        (input_grad,) = finish(part, d_attn, [], sizes, depth)
        up_terms, qkv_terms = sums
        quad = width // QUADS
        qkv_terms = qkv_terms.reshape(width, QUADS, 3, quad).transpose(0, 2, 1, 3).reshape(width, 3 * width)
        total = lambda v: lax.psum(
            lax.psum_scatter(v, "wide", scatter_dimension=0, tiled=True).astype(F32), "narrow"
        )
        vector = lambda n: total(vectors[n])
        grads = (
            total(qkv_terms), vector(0), vector(1), total(out_terms), vector(2), vector(3), vector(4),
            total(up_terms), total(vectors[8 : 8 + UPS].reshape(-1)), total(down_terms), vector(5), vector(6),
            vector(7),
        )
    return (loss.reshape(()), block_out, input_grad.reshape(sents, seq, width), *grads)


def solution(mesh):
    sizes = (mesh.shape["wide"], mesh.shape["narrow"])
    split = P(("wide", "narrow"), None, None)
    matrix, vector = P("wide", None), P("wide")
    return jax.shard_map(
        functools.partial(per_device, sizes),
        mesh=mesh,
        in_specs=(split, split) + (P(),) * 14,
        out_specs=(
            P(), split, split, matrix, vector, vector, matrix, vector, vector, vector, matrix, vector,
            matrix, vector, vector, vector,
        ),
        check_vma=False,
    )
```

```python
import functools

import jax
import jax.numpy as jnp
from jax import lax
from jax.experimental import pallas as pl
from jax.experimental.pallas import tpu as pltpu
from jax.sharding import PartitionSpec as P

BF = jnp.bfloat16
F32 = jnp.float32
MESH = pl.DeviceIdType.MESH

HEADS = 12
QUAD = 4
SCALE = 40.0
MARGIN = 0.3
EPS = 1e-06
SIDE = 8
VMEM_BYTES = 60 * 2**20


def nn(a, b):
    return lax.dot_general(a, b, (((1,), (0,)), ((), ())), preferred_element_type=F32)


def nt(a, b):
    return lax.dot_general(a, b, (((1,), (1,)), ((), ())), preferred_element_type=F32)


def tn(a, b):
    return lax.dot_general(a, b, (((0,), (0,)), ((), ())), preferred_element_type=F32)


def params(**more):
    return pltpu.CompilerParams(vmem_limit_bytes=VMEM_BYTES, **more)


def resident(shape):
    return pl.BlockSpec(shape, lambda *_: (0,) * len(shape), pipeline_mode=pl.Buffered(1))


def shape_of(shape, dtype):
    return jax.ShapeDtypeStruct(shape, dtype)


def head_mask(quad):
    head = quad // QUAD
    at = lambda axis: lax.broadcasted_iota(jnp.int32, (quad, quad), axis) // head
    return (at(0) == at(1)).astype(F32).astype(BF)


def line(ref):
    return ref[...].reshape(1, ref.shape[0])


def blocked(rows, mask):
    return jnp.concatenate([rows] * QUAD, axis=0) * mask


def diagonal(full, seq):
    half = full.shape[1] // 2
    lane = lax.broadcasted_iota(jnp.int32, (seq, half), 1) < half // 2
    left = jnp.where(lane, full[:seq, :half], full[seq : 2 * seq, :half])
    right = jnp.where(lane, full[2 * seq : 3 * seq, half:], full[3 * seq :, half:])
    return jnp.concatenate([left, right], axis=1)


def paired(left, right, seq):
    half = left.shape[1] // 2
    lane = lax.broadcasted_iota(jnp.int32, (seq, half), 1) < half // 2
    parts = []
    for at in (slice(0, half), slice(half, 2 * half)):
        full = tn(left[:, at], right[:, at])
        parts.append(jnp.where(lane, full[:seq], full[seq:]))
    return jnp.concatenate(parts, axis=1)


def attend_kernel(x_ref, w_ref, qb_ref, vb_ref, qkv_ref, p_ref, ctx_ref):
    sents, seq, width = x_ref.shape
    rows = x_ref[...].reshape(sents * seq, width)
    quad = width // QUADS
    for part, bias in ((0, qb_ref), (1, None), (2, vb_ref)):
        cols = slice(part * width, (part + 1) * width)
        y = nn(rows, w_ref[:, cols])
        if bias is not None:
            y = y + line(bias)
        qkv_ref[:, cols] = y.astype(BF)
    mask = head_mask(quad)
    scale = (width // HEADS) ** -0.5
    units = [(s, g) for s in range(sents) for g in range(width // quad)]
    for first in range(0, len(units), 12):
        some = units[first : first + 12]
        rows_of = lambda s: slice(s * seq, (s + 1) * seq)
        cols_of = lambda g, part: slice(part * width + g * quad, part * width + (g + 1) * quad)
        scores = [
            nt(qkv_ref[rows_of(s), cols_of(g, 1)], blocked(qkv_ref[rows_of(s), cols_of(g, 0)], mask)) * scale
            for s, g in some
        ]
        e = [jnp.exp(v - jnp.max(v, axis=0, keepdims=True)) for v in scores]
        p = [(v * (1.0 / jnp.sum(v, axis=0, keepdims=True))).astype(BF) for v in e]
        for (s, g), low in zip(some, p, strict=True):
            p_ref[s, :, cols_of(g, 0)] = low
            v = qkv_ref[rows_of(s), cols_of(g, 2)]
            ctx_ref[rows_of(s), cols_of(g, 0)] = diagonal(tn(low, v), seq).astype(BF)


def attend(tokens, qkv_weight, query_bias, value_bias):
    sents, seq, width = tokens.shape
    rows = sents * seq
    side = SIDE * seq
    return pl.pallas_call(
        attend_kernel,
        grid=(sents // SIDE,),
        in_specs=[
            pl.BlockSpec((SIDE, seq, width), lambda i: (i, 0, 0)),
            resident((width, 3 * width)),
            resident((width,)),
            resident((width,)),
        ],
        out_specs=[
            pl.BlockSpec((side, 3 * width), lambda i: (i, 0)),
            pl.BlockSpec((SIDE, seq, width), lambda i: (i, 0, 0)),
            pl.BlockSpec((side, width), lambda i: (i, 0)),
        ],
        out_shape=[
            shape_of((rows, 3 * width), BF),
            shape_of((sents, seq, width), BF),
            shape_of((rows, width), BF),
        ],
        compiler_params=params(),
        name="attend",
    )(tokens, qkv_weight, query_bias, value_bias)


def norm(values):
    mean = jnp.mean(values, -1, keepdims=True)
    centred = values - mean
    root = lax.rsqrt(jnp.mean(centred * centred, -1, keepdims=True) + EPS)
    return centred * root, root


def place():
    wide, narrow = lax.axis_index("wide"), lax.axis_index("narrow")
    return wide, narrow, wide // 4, (wide // 2) % 2, wide % 2


def forward_kernel(
    x_ref, ctx_ref, ow_ref, ob_ref, g1_ref, s1_ref, uw_hbm, ub_ref, dw_hbm, db_ref, g2_ref, s2_ref,
    low_ref, xh1_ref, rs1_ref, hid_ref, slope_ref, xh2_ref, rs2_ref, cls_ref, all_ref,
    rows_ref, uw_ref, dw_ref, w_sems, buf, zs, zr, ys, yr, xs, xr, cs, cr, done,
):
    sents, part, width = x_ref.shape
    depth = uw_ref.shape[1]
    rows = sents * part
    step = pl.program_id(0)
    wide, narrow, z, y, core = place()
    nz, nx = buf.shape[1], buf.shape[4]
    wide_of = lambda a, b, c: (a * 2 + b) * 2 + c
    z_peers = [(lax.rem(z + k, nz), k) for k in range(1, nz)]
    x_peers = [(lax.rem(narrow + k, nx), k) for k in range(1, nx)]

    def gather_copy(slots, sems, at, device):
        return pltpu.make_async_remote_copy(
            src_ref=buf.at[slots], dst_ref=buf.at[slots], send_sem=sems[0].at[at], recv_sem=sems[1].at[at],
            device_id=device, device_id_type=MESH,
        )

    every = slice(None)
    z_copies = [
        gather_copy((every, z, y, core, narrow), (zs, zr), k - 1, (wide_of(to, y, core), narrow))
        for to, k in z_peers
    ]

    def over_y(half, xs_held, at):
        return gather_copy((half, every, y, core, xs_held), (ys, yr), at, (wide_of(z, 1 - y, core), narrow))

    def over_x(half, ys_held, first):
        return [
            gather_copy((half, every, ys_held, core, narrow), (xs, xr), first + k - 1, (wide, to)) for to, k in x_peers
        ]

    second = [over_y(0, narrow, 0), *over_x(1, y, 0)]
    third = [*over_x(0, every, nx - 1), over_y(1, every, 1)]
    core_copy = gather_copy((every, every, every, core), (cs, cr), 0, (wide_of(z, y, 1 - core), narrow))

    barrier = pltpu.get_barrier_semaphore()
    weights = [
        pltpu.make_async_copy(uw_hbm, uw_ref, w_sems.at[0]), pltpu.make_async_copy(dw_hbm, dw_ref, w_sems.at[1])
    ]

    @pl.when(step == 0)
    def _():
        for copy in weights:
            copy.start()
        for to, _ in z_peers:
            pl.semaphore_signal(barrier, inc=1, device_id=(wide_of(to, y, core), narrow), device_id_type=MESH)
        pl.semaphore_signal(barrier, inc=1, device_id=(wide_of(z, 1 - y, core), narrow), device_id_type=MESH)
        for to, _ in x_peers:
            pl.semaphore_signal(barrier, inc=1, device_id=(wide, to), device_id_type=MESH)
        pl.semaphore_signal(barrier, inc=1, device_id=(wide_of(z, y, 1 - core), narrow), device_id_type=MESH)

    block = lambda ref: ref[...].reshape(rows, ref.shape[2])

    def put(ref, value):
        ref[...] = value.astype(ref.dtype).reshape(ref.shape)

    x, ctx = block(x_ref), block(ctx_ref)
    some = rows // 4
    cuts = [slice(i * some, (i + 1) * some) for i in range(4)]
    pre, normals = [], []
    for i, at in enumerate(cuts):
        pre.append(x[at].astype(F32) + nn(ctx[at], ow_ref[...]) + line(ob_ref))
        if i:
            normals.append(norm(pre[i - 1]))
    normals.append(norm(pre[-1]))
    xh1 = jnp.concatenate([a for a, _ in normals], axis=0)
    rs1 = jnp.concatenate([b for _, b in normals], axis=0)
    normed = xh1 * line(g1_ref) + line(s1_ref)
    low = normed.astype(BF)
    put(low_ref, low)
    put(xh1_ref, xh1)
    put(rs1_ref, jnp.broadcast_to(rs1, (rows, 128)))
    total = normed + line(db_ref)

    @pl.when(step == 0)
    def _():
        for copy in weights:
            copy.wait()

    def up_of(c):
        cols = slice(c * width, (c + 1) * width)
        return nn(low, uw_ref[:, cols]) + ub_ref[cols].reshape(1, width)

    chunks = depth // width
    ahead = up_of(0)
    for c in range(chunks):
        if c == 2:

            @pl.when(step == 0)
            def _():
                pl.semaphore_wait(barrier, nz + nx)

            @pl.when(step == 2)
            def _():
                for copy in second:
                    copy.wait()
                for copy in third:
                    copy.start()

            @pl.when(step == 3)
            def _():
                for copy in third:
                    copy.wait()
                core_copy.start()

        cols = slice(c * width, (c + 1) * width)
        up = ahead
        if c + 1 < chunks:
            ahead = up_of(c + 1)
        cdf = 0.5 * (lax.erf(up * 0.7071067811865476) + 1.0)
        slope = cdf + up * (0.3989422804014327 * jnp.exp(-0.5 * up * up))
        hidden = (up * cdf).astype(BF)
        hid_ref[:, :, cols] = hidden.reshape(sents, part, width)
        slope_ref[:, :, cols] = slope.astype(BF).reshape(sents, part, width)
        total = total + nn(hidden, dw_ref[cols, :])
    xh2, rs2 = norm(total)
    final = xh2 * line(g2_ref) + line(s2_ref)
    put(xh2_ref, xh2)
    put(rs2_ref, jnp.broadcast_to(rs2, (rows, 128)))

    @pl.when(step == 0)
    def _():
        for s in range(sents):
            cls_ref[s : s + 1, :] = final[s * part : s * part + 1, :]
        cls = cls_ref[...]
        pooled = cls * lax.rsqrt(jnp.sum(cls * cls, -1, keepdims=True) + EPS)
        for s in range(sents):
            rows_ref[s % 2, s // 2 : s // 2 + 1, :] = pooled[s : s + 1, :]
        for half in range(2):
            buf[half, z, y, core, narrow] = rows_ref[half].astype(BF)
        for copy in z_copies:
            copy.start()

    @pl.when(step == 1)
    def _():
        for copy in z_copies:
            copy.wait()
        for copy in second:
            copy.start()

    @pl.when(step == 3)
    def _():
        core_copy.wait()
        out = pltpu.make_async_copy(buf, all_ref, done)
        out.start()
        out.wait()


def forward(tokens, ctx, ow, ob, g1, s1, uw, ub, dw, db, g2, s2, sizes):
    sents, seq, width = tokens.shape
    depth = uw.shape[1]
    part = seq // 4
    nz, nx = sizes[0] // 4, sizes[1]
    tile = lambda lanes: pl.BlockSpec((sents, part, lanes), lambda i: (0, i, 0))
    whole = lambda lanes, dtype: shape_of((sents, seq, lanes), dtype)
    slots = (2, nz, 2, 2, nx, sents // 2, width)
    dma = pltpu.SemaphoreType.DMA
    return pl.pallas_call(
        forward_kernel,
        grid=(4,),
        in_specs=[
            tile(width), tile(width), resident(ow.shape), resident(ob.shape), resident(g1.shape),
            resident(s1.shape), pl.BlockSpec(memory_space=pl.ANY), resident(ub.shape),
            pl.BlockSpec(memory_space=pl.ANY),
            resident(db.shape), resident(g2.shape), resident(s2.shape),
        ],
        out_specs=[
            tile(width), tile(width), tile(128), tile(depth), tile(depth), tile(width),
            tile(128), pl.BlockSpec((sents, width), lambda i: (0, 0)), pl.BlockSpec(memory_space=pl.ANY),
        ],
        out_shape=[
            whole(width, BF), whole(width, BF), whole(128, F32), whole(depth, BF),
            whole(depth, BF), whole(width, BF), whole(128, F32), shape_of((sents, width), F32),
            shape_of(slots, BF),
        ],
        scratch_shapes=[
            pltpu.VMEM((2, sents // 2, width), F32), pltpu.VMEM(uw.shape, BF), pltpu.VMEM(dw.shape, BF), dma((2,)),
            pltpu.VMEM(slots, BF),
            dma((nz - 1,)), dma((nz - 1,)), dma((2,)), dma((2,)), dma((2 * nx - 2,)), dma((2 * nx - 2,)), dma((1,)),
            dma((1,)), dma,
        ],
        compiler_params=params(collective_id=0, has_side_effects=True),
        name="forward",
    )(tokens, ctx.reshape(sents, seq, width), ow, ob, g1, s1, uw, ub, dw, db, g2, s2)


def ranking_kernel(
    all_ref, group_ref, cls_ref, cot_ref, xh2_ref, rs2_ref, g2_ref, s2_ref,
    loss_ref, out_ref, down_ref, sums_ref, dcls, gcol_ref,
):
    _, pairs, width = all_ref.shape
    own = cls_ref.shape[0] // 2
    step = pl.program_id(0)

    @pl.when(step == 0)
    def _():
        first = (lax.axis_index("wide") * lax.axis_size("narrow") + lax.axis_index("narrow")) * own
        strip = min(256, pairs)
        groups = line(group_ref)
        gcol_ref[...] = jnp.transpose(jnp.broadcast_to(groups, (128, pairs)))
        own_rows = pl.ds(pl.multiple_of(first, own), own)

        def logits_of(left, right, start):
            count = left.shape[0]
            same_at = lax.broadcasted_iota(jnp.int32, (count, pairs), 0) + start
            pair_at = lax.broadcasted_iota(jnp.int32, (count, pairs), 1)
            hit = same_at == pair_at
            return nt(left, right) * SCALE - jnp.where(hit, SCALE * MARGIN, 0.0), hit

        def column_lse(left_at, right_at):
            right = all_ref[right_at]

            def strip_step(at, carry):
                top, total, diag = carry
                start = pl.multiple_of(at * strip, strip)
                left = all_ref[left_at, pl.ds(start, strip), :]
                logits, hit = logits_of(left, right, start)
                masked = jnp.where(gcol_ref[pl.ds(start, strip), :1] == groups, logits, -1e30)
                peak = jnp.maximum(top, jnp.max(masked, axis=0, keepdims=True))
                total = total * jnp.exp(top - peak) + jnp.sum(jnp.exp(masked - peak), axis=0, keepdims=True)
                diag = diag + jnp.sum(jnp.where(hit, logits, 0.0), axis=0, keepdims=True)
                return peak, total, diag

            start = (jnp.full((1, pairs), -1e30, F32), jnp.zeros((1, pairs), F32), jnp.zeros((1, pairs), F32))
            top, total, diag = lax.fori_loop(0, pairs // strip, strip_step, start)
            return top + jnp.log(total), diag

        col_lse, diag = column_lse(0, 1)
        row_lse, diag_again = column_lse(1, 0)
        loss_ref[...] = jnp.sum(col_lse - diag + row_lse - diag_again, axis=1, keepdims=True) / pairs

        same = gcol_ref[own_rows, :1] == groups

        def side(my_at, other_at, other_lse):
            other = all_ref[other_at]
            mine = all_ref[my_at, own_rows, :]
            logits, hit = logits_of(mine, other, first)
            eye = hit.astype(F32)
            masked = jnp.where(same, logits, -1e30)
            e = jnp.exp(masked - jnp.max(masked, axis=1, keepdims=True))
            d_mine = (e / jnp.sum(e, axis=1, keepdims=True) - eye).astype(BF)
            d_other = (jnp.where(same, jnp.exp(masked - other_lse), 0.0) - eye).astype(BF)
            return (nn(d_mine, other) + nn(d_other, other)) * SCALE

        for at, (other, lse) in enumerate(((1, col_lse), (0, row_lse))):
            terms = side(at, other, lse)
            for p in range(own):
                dcls[2 * p + at : 2 * p + at + 1, :] = terms[p : p + 1, :]
        d = dcls[...]
        c = cls_ref[...]
        root = lax.rsqrt(jnp.sum(c * c, -1, keepdims=True) + EPS)
        dcls[...] = root * d - root * root * root * c * jnp.sum(c * d, -1, keepdims=True)
        sums_ref[...] = jnp.zeros_like(sums_ref)

    side_sents, seq, _ = cot_ref.shape
    rows = side_sents * seq
    start = pl.multiple_of(step * side_sents, side_sents)
    extra = dcls[pl.ds(start, side_sents), :]
    at_zero = lax.broadcasted_iota(jnp.int32, (side_sents, seq, width), 1) == 0
    d_final = cot_ref[...].astype(F32) + jnp.where(at_zero, extra[:, None, :], 0.0)
    d_final = d_final.reshape(rows, width)
    xhat = xh2_ref[...].reshape(rows, width).astype(F32)
    root = rs2_ref[...].reshape(rows, 128)[:, :1]
    out_ref[...] = (xhat * line(g2_ref) + line(s2_ref)).astype(BF).reshape(out_ref.shape)
    e = d_final * line(g2_ref)
    d_pre = (e - jnp.mean(e, -1, keepdims=True) - xhat * jnp.mean(e * xhat, -1, keepdims=True)) * root
    d_down = d_pre.astype(BF)
    down_ref[...] = d_down
    sums_ref[0:1, :] += jnp.sum(d_final * xhat, axis=0, keepdims=True)
    sums_ref[1:2, :] += jnp.sum(d_final, axis=0, keepdims=True)
    sums_ref[2:3, :] += jnp.sum(d_down.astype(F32), axis=0, keepdims=True)


def ranking(gathered, groups, cls, cotangent, xh2, rs2, g2, s2):
    sents, seq, width = cotangent.shape
    pairs = gathered.shape[1]
    tile = lambda lanes: pl.BlockSpec((SIDE, seq, lanes), lambda i: (i, 0, 0))
    return pl.pallas_call(
        ranking_kernel,
        grid=(sents // SIDE,),
        in_specs=[
            resident(gathered.shape), resident(groups.shape), resident(cls.shape), tile(width), tile(width), tile(128),
            resident(g2.shape), resident(s2.shape),
        ],
        out_specs=[
            pl.BlockSpec((1, 1), lambda i: (0, 0)), tile(width),
            pl.BlockSpec((SIDE * seq, width), lambda i: (i, 0)),
            pl.BlockSpec((8, width), lambda i: (0, 0)),
        ],
        out_shape=[shape_of((1, 1), F32), shape_of(cotangent.shape, BF), shape_of((sents * seq, width), BF), shape_of((8, width), F32)],
        scratch_shapes=[pltpu.VMEM((sents, width), F32), pltpu.VMEM((pairs, 128), jnp.int32)],
        compiler_params=params(),
        name="ranking",
    )(gathered, groups, cls, cotangent, xh2, rs2, g2, s2)


def copy_to(src, dst, sends, recvs, at, device):
    return pltpu.make_async_remote_copy(
        src_ref=src, dst_ref=dst, send_sem=sends.at[at], recv_sem=recvs.at[at], device_id=device,
        device_id_type=MESH,
    )


def plus(*terms):
    if len(terms) == 2:
        return terms[0] + terms[1]
    return sum(t.astype(F32) for t in terms).astype(BF)


class Peers:
    def __init__(self, nz):
        self.nz = nz
        wide, self.x, self.z, self.y, self.core = place()
        self.sibling = (wide + 1 - 2 * self.core, self.x)
        self.over_x = (wide, 1 - self.x)
        self.over_y = (wide + 2 - 4 * self.y, self.x)
        self.zs = [lax.rem(self.z + k, nz) for k in range(1, nz)]
        self.over_z = [(lax.rem(wide + 4 * k, 4 * nz), self.x) for k in range(1, nz)]

    def greet(self, devices):
        barrier = pltpu.get_barrier_semaphore()
        for device in devices:
            pl.semaphore_signal(barrier, inc=1, device_id=device, device_id_type=MESH)

    def met(self, count):
        pl.semaphore_wait(pltpu.get_barrier_semaphore(), count)


class Stages:
    SEMS = 9

    def __init__(self, peers, terms, got, sends, recvs):
        self.peers, self.terms, self.got, self.sends, self.recvs = peers, terms, got, sends, recvs
        self.half = peers.nz // 2

    @staticmethod
    def scratch(nz, rows, cols):
        half = nz // 2
        return {
            "xa": (half, 2, rows, cols), "yb": (2, nz - half, rows, cols), "ya": (half, rows, cols),
            "xb": (nz - half, rows, cols),
        }

    def first_of(self, z, at):
        p = self.peers
        if z < self.half:
            return copy_to(self.terms.at[1 - p.x, z], self.got["xa"].at[z], self.sends, self.recvs, at, p.over_x)
        return copy_to(
            self.terms.at[:, z, 1 - p.y], self.got["yb"].at[:, z - self.half], self.sends, self.recvs, at, p.over_y
        )

    def first(self):
        p, h = self.peers, self.half
        return [
            copy_to(self.terms.at[1 - p.x, :h], self.got["xa"], self.sends, self.recvs, 1, p.over_x),
            copy_to(self.terms.at[:, h:, 1 - p.y], self.got["yb"], self.sends, self.recvs, 2, p.over_y),
        ]

    def second(self):
        p, h = self.peers, self.half
        return [
            copy_to(self.terms.at[p.x, :h, 1 - p.y], self.got["ya"], self.sends, self.recvs, 3, p.over_y),
            copy_to(self.terms.at[1 - p.x, h:, p.y], self.got["xb"], self.sends, self.recvs, 4, p.over_x),
        ]

    def add_first(self, copies=None):
        p, h = self.peers, self.half
        for copy in copies or self.first():
            copy.wait()
        self.terms[p.x, :h] = plus(self.terms[p.x, :h], self.got["xa"][...])
        for x in range(2):
            self.terms[x, h:, p.y] = plus(self.terms[x, h:, p.y], self.got["yb"][x])

    def add_second(self):
        p, h = self.peers, self.half
        for copy in self.second():
            copy.wait()
        self.terms[p.x, :h, p.y] = plus(self.terms[p.x, :h, p.y], self.got["ya"][...])
        self.terms[p.x, h:, p.y] = plus(self.terms[p.x, h:, p.y], self.got["xb"][...])


class Finish:
    def __init__(self, peers, shard, got_z, mine, other, sends, recvs):
        self.peers, self.shard, self.got_z, self.mine, self.other = peers, shard, got_z, mine, other
        self.sends, self.recvs = sends, recvs

    def along_z(self):
        p = self.peers
        return [
            copy_to(self.shard(to), self.got_z.at[k], self.sends, self.recvs, 5 + k, device)
            for k, (to, device) in enumerate(zip(p.zs, p.over_z, strict=True))
        ]

    def along_x(self):
        return copy_to(self.mine, self.other, self.sends, self.recvs, 8, self.peers.over_x)

    def add(self):
        for copy in self.along_z():
            copy.wait()
        got = [self.got_z[k] for k in range(self.peers.nz - 1)]
        self.mine[...] = plus(self.shard(self.peers.z)[...], *got)


def hand_out(value, keep, send):
    halves, nz, ny, rows, cols = keep.shape
    core = lax.axis_index("wide") % 2
    for z in range(nz):
        for y in range(ny):
            first = (z * ny + y) * 2 * rows
            for ref, side in ((keep, core), (send, 1 - core)):
                part = value[pl.ds(pl.multiple_of(first + side * rows, rows), rows), :].astype(BF)
                for h in range(halves):
                    ref[h, z, y] = part[:, h * cols : (h + 1) * cols]


def backward_kernel(fused, nz, *refs):
    (down_ref, hid_ref, slope_ref, dw_hbm, uw_hbm, xh1_ref, rs1_ref, g1_ref, ow_ref, actx_ref) = refs[:10]
    (up_ref, attn_ref, ctx_ref, sums_ref, upsum_ref, owg_ref, dwg_ref) = refs[10:17]
    dw_ref, uw_ref, w_sems, owg, *comm = refs[17:]
    blocks = 4
    width = down_ref.shape[1]
    rows, depth = slope_ref.shape
    step = pl.program_id(0)
    weights = [
        pltpu.make_async_copy(dw_hbm, dw_ref, w_sems.at[0]), pltpu.make_async_copy(uw_hbm, uw_ref, w_sems.at[1])
    ]

    if fused:
        terms, send, got, xa, yb, ya, xb, c_send, c_recv, s_send, s_recv = comm
        peers = Peers(nz)
        stages = Stages(peers, terms, {"xa": xa, "yb": yb, "ya": ya, "xb": xb}, s_send, s_recv)

        def exchange(i):
            return copy_to(send.at[i % 2], got.at[i % 2], c_send, c_recv, i, peers.sibling)

    @pl.when(step == 0)
    def _():
        for copy in weights:
            copy.start()
        sums_ref[...] = jnp.zeros_like(sums_ref)
        upsum_ref[...] = jnp.zeros_like(upsum_ref)
        if fused:
            peers.greet([peers.sibling, peers.over_x, peers.over_y])

    def settle(i):
        exchange(i).wait()
        for h in range(2):
            terms[h, i] = plus(terms[h, i], got[i % 2, h, 0])
        for z in range(blocks):
            if isinstance(i, int) and z != i:
                continue

            @pl.when(i == z)
            def _(z=z):
                stages.first_of(z, Stages.SEMS + z).start()

    @pl.when(step < blocks)
    def _():
        value = tn(hid_ref[...], down_ref[...])
        if fused:

            @pl.when(step == 0)
            def _():
                peers.met(3)

            @pl.when(step > 0)
            def _():
                settle(step - 1)

            owg[...] = value
            hand_out(owg, terms.at[:, pl.ds(step, 1)], send.at[step % 2])
            exchange(step).start()

        else:
            dwg_ref[...] = value.astype(BF)

    @pl.when(step == blocks)
    def _():
        for copy in weights:
            copy.wait()

    @pl.when(step >= blocks)
    def _():
        d_down = down_ref[pl.ds(pl.multiple_of((step - blocks) * rows, rows), rows), :]
        total = d_down.astype(F32)
        for c in range(depth // width):
            cols = slice(c * width, (c + 1) * width)
            d_up = (nt(d_down, dw_ref[cols, :]) * slope_ref[:, cols].astype(F32)).astype(BF)
            up_ref[:, cols] = d_up
            upsum_ref[:, cols] += jnp.sum(d_up.astype(F32), axis=0, keepdims=True)
            total = total + nt(d_up, uw_ref[:, cols])
        xhat = xh1_ref[...].astype(F32)
        root = rs1_ref[:, :1]
        e = total * g1_ref[...].reshape(1, width)
        d_pre = (e - jnp.mean(e, -1, keepdims=True) - xhat * jnp.mean(e * xhat, -1, keepdims=True)) * root
        d_attn = d_pre.astype(BF)
        attn_ref[...] = d_attn
        ctx_ref[...] = nt(d_attn, ow_ref[...]).astype(BF)
        sums_ref[0:1, :] += jnp.sum(total * xhat, axis=0, keepdims=True)
        sums_ref[1:2, :] += jnp.sum(total, axis=0, keepdims=True)
        sums_ref[2:3, :] += jnp.sum(d_attn.astype(F32), axis=0, keepdims=True)
        part = tn(actx_ref[...], d_attn)

        @pl.when(step == blocks)
        def _():
            owg[...] = part

        @pl.when(step > blocks)
        def _():
            owg[...] += part

    if fused:

        @pl.when(step == blocks)
        def _():
            settle(blocks - 1)

        @pl.when(step == blocks + 1)
        def _():
            stages.add_first([stages.first_of(z, Stages.SEMS + z) for z in range(blocks)])
            for copy in stages.second():
                copy.start()

    @pl.when(step == pl.num_programs(0) - 1)
    def _():
        if fused:
            hand_out(owg, owg_ref.at[0], owg_ref.at[1])
            stages.add_second()
            dwg_ref[...] = terms[peers.x, :, peers.y]
        else:
            owg_ref[...] = owg[...].astype(BF)


def backward(d_down, hidden, slope, dw, uw, xh1, rs1, g1, ow, ctx, sizes):
    fused = sizes == (16, 2)
    nz = sizes[0] // 4
    rows, width = d_down.shape
    depth = uw.shape[1]
    side = rows // 4
    tile = lambda lanes: pl.BlockSpec((side, lanes), lambda i: (jnp.maximum(i - 4, 0), 0))
    once = lambda *shape: pl.BlockSpec(shape, lambda i: (0,) * len(shape))
    shard = depth // sizes[0]
    half = width // 2
    dma = pltpu.SemaphoreType.DMA
    scratch = [
        pltpu.VMEM(dw.shape, BF), pltpu.VMEM(uw.shape, BF), dma((2,)), pltpu.VMEM((width, width), F32)
    ]
    if fused:
        scratch += [
            pltpu.VMEM((2, nz, 2, shard, half), BF), pltpu.VMEM((2, 2, 1, 2, shard, half), BF),
            pltpu.VMEM((2, 2, 1, 2, shard, half), BF),
        ]
        scratch += [pltpu.VMEM(s, BF) for s in Stages.scratch(nz, shard, half).values()]
        scratch += [dma((4,)), dma((4,)), dma((Stages.SEMS + 4,)), dma((Stages.SEMS + 4,))]
        dwg_spec, dwg_shape = once(nz, shard, half), (nz, shard, half)
        owg_shape = (2, 2, nz, 2, width // sizes[0], half)
        extra = dict(collective_id=1, has_side_effects=True)
    else:
        dwg_spec, dwg_shape = pl.BlockSpec((width, width), lambda i: (jnp.minimum(i, 3), 0)), (depth, width)
        owg_shape = (width, width)
        extra = {}
    return pl.pallas_call(
        functools.partial(backward_kernel, fused, nz),
        grid=(8,),
        in_specs=[
            resident((rows, width)), pl.BlockSpec((rows, width), lambda i: (0, jnp.minimum(i, 3))), tile(depth),
            pl.BlockSpec(memory_space=pl.ANY), pl.BlockSpec(memory_space=pl.ANY), tile(width), tile(128),
            resident(g1.shape), resident(ow.shape), tile(width),
        ],
        out_specs=[
            tile(depth), tile(width), tile(width), once(8, width), once(1, depth), once(*owg_shape), dwg_spec
        ],
        out_shape=[
            shape_of((rows, depth), BF), shape_of((rows, width), BF), shape_of((rows, width), BF),
            shape_of((8, width), F32), shape_of((1, depth), F32), shape_of(owg_shape, BF),
            shape_of(dwg_shape, BF),
        ],
        scratch_shapes=scratch,
        compiler_params=params(**extra),
        name="backward",
    )(d_down, hidden, slope, dw, uw, xh1, rs1, g1, ow, ctx)


UPS, QUADS, TILES = 4, 3, 4
FIRST_QUAD = UPS
FIRST_INPUT = UPS + QUADS * TILES
STEPS = FIRST_INPUT + TILES
UP_PIECE, OUT_PIECE, QUAD_PIECE = 0, UPS, 1 + UPS
PIECES = UPS + 1 + QUADS
VECTORS = 16


def tail_kernel(fused, nz, *refs):
    (low_ref, up_ref, q_ref, k_ref, v_ref, dctx_ref, p_ref, x_ref, w_hbm, owg_ref, dsum_ref,
     one_ref, two_ref, upsum_ref) = refs[:14]
    out_ref, vec_out = refs[14:16]
    if fused:
        outs = refs[16:20]
        w_ref, w_sem, dqkv, acc, vec, *comm = refs[20:]
    else:
        upg_ref, qkvg_ref = refs[16:18]
        w_ref, w_sem, dqkv, acc, vec = refs[18:]
    rows, quad = q_ref.shape
    sents, seq, _ = p_ref.shape
    width = acc.shape[0]
    step = pl.program_id(0)
    weight = pltpu.make_async_copy(w_hbm, w_ref, w_sem)
    at_quad = jnp.clip(step - FIRST_QUAD, 0, QUADS * TILES - 1)
    g, tile = at_quad // TILES, at_quad % TILES

    if fused:
        (mine, other, dmine, dother, terms, send, got, xa, yb, ya, xb, gz, dz, vlow, vgot, sends, recvs, d_sends, d_recvs,
         v_sends, v_recvs) = comm
        peers = Peers(nz)
        down = Finish(peers, lambda at: dsum_ref.at[at], dz, dmine, dother, d_sends, d_recvs)

        def stages_of(n):
            return Stages(
                peers, terms.at[n], {"xa": xa.at[n], "yb": yb.at[n], "ya": ya.at[n], "xb": xb.at[n]}, sends.at[n],
                recvs.at[n],
            )

        def finish_of(n):
            return Finish(
                peers, lambda at: terms.at[n, peers.x, at, peers.y], gz.at[n], mine.at[n], other.at[n],
                sends.at[n], recvs.at[n],
            )

        def chip(n):
            return copy_to(send.at[n % 2], got.at[n % 2], sends.at[n], recvs.at[n], 0, peers.sibling)

        def add_chip(n):
            chip(n).wait()
            for h in range(2):
                terms[n, h] = plus(terms[n, h], got[n % 2, h])
            for copy in stages_of(n).first():
                copy.start()

        def add_first(n):
            stages_of(n).add_first()
            for copy in stages_of(n).second():
                copy.start()

        def add_second(n):
            stages_of(n).add_second()
            for copy in finish_of(n).along_z():
                copy.start()

        def add_z(n):
            finish_of(n).add()
            finish_of(n).along_x().start()

        def last(n):
            finish_of(n).along_x().wait()

        usual, hurried = (1, 3, 5, 7, 8), (1, 2, 3, 4, STEPS)
        ready = [*range(UPS + 1)] + [FIRST_QUAD + TILES * (q + 1) - 1 for q in range(QUADS)]

        def settle():
            for stage, action in enumerate((add_chip, add_first, add_second, add_z, last)):
                at = [t + (hurried if n == PIECES - 1 else usual)[stage] for n, t in enumerate(ready)]
                due, piece = step == at[0], jnp.int32(0)
                for n in range(1, PIECES):
                    due = due | (step == at[n])
                    piece = jnp.where(step == at[n], n, piece)
                pl.when(due)(functools.partial(action, piece))

        def vector_copy(n, device):
            return copy_to(vlow, vgot.at[n], v_sends, v_recvs, n, device)

        routes = [[peers.sibling], [peers.over_x], [peers.over_y], peers.over_z]

        def vector_copies(hop):
            return [vector_copy(hop + k, device) for k, device in enumerate(routes[hop])]

        @pl.when(step == 0)
        def _():
            peers.greet([peers.sibling, peers.over_x, peers.over_y, *peers.over_z])

    @pl.when(step == 0)
    def _():
        weight.start()
        vec[...] = jnp.zeros_like(vec)
        vec[2:3, :] = one_ref[2:3, :]
        vec[3:5, :] = one_ref[0:2, :]
        vec[5:6, :] = two_ref[2:3, :]
        vec[6:8, :] = two_ref[0:2, :]
        for c in range(UPS):
            vec[8 + c : 9 + c, :] = upsum_ref[:, c * width : (c + 1) * width]

    @pl.when(step < UPS)
    def _():
        value = tn(low_ref[...], up_ref[...])
        if fused:
            acc[...] = value
        else:
            upg_ref[...] = value.astype(BF)

    @pl.when((step >= FIRST_QUAD) & (step < FIRST_INPUT))
    def _():
        mask = head_mask(quad)
        scale = (quad // QUAD) ** -0.5
        here = lambda size, s=0: pl.ds(pl.multiple_of(tile * rows + s * seq, seq), size)
        def sentences(which):
            k = [k_ref[s * seq : (s + 1) * seq, :] for s in which]
            low = [p_ref[s] for s in which]
            p = [v.astype(F32) for v in low]
            dctx = [blocked(dctx_ref[s * seq : (s + 1) * seq, :], mask) for s in which]
            d_probs = [nt(v_ref[s * seq : (s + 1) * seq, :], c) for s, c in zip(which, dctx, strict=True)]
            d_scores, d_value = [], []
            for a, b, v, c in zip(p, d_probs, low, dctx, strict=True):
                d_value.append(nn(v, c).astype(BF))
                d_scores.append((a * (b - jnp.sum(a * b, axis=0, keepdims=True))).astype(BF))
            d_query = [(paired(a, b, seq) * scale).astype(BF) for a, b in zip(d_scores, k, strict=True)]
            d_key = [
                (nn(a, blocked(q_ref[s * seq : (s + 1) * seq, :], mask)) * scale).astype(BF)
                for s, a in zip(which, d_scores, strict=True)
            ]
            out = []
            for s, *three in zip(which, d_query, d_key, d_value, strict=True):
                out.append(jnp.concatenate(three, axis=1))
                dqkv[g, here(seq, s), :] = out[-1]
            return out

        grads = jnp.concatenate(sentences(range(sents)), axis=0)
        part = tn(x_ref[...], grads)
        q_sum = jnp.sum(grads[:, :quad].astype(F32), axis=0, keepdims=True)
        v_sum = jnp.sum(grads[:, 2 * quad :].astype(F32), axis=0, keepdims=True)
        for q in range(QUADS):

            @pl.when(g == q)
            def _(q=q):
                vec[0:1, q * quad : (q + 1) * quad] += q_sum
                vec[1:2, q * quad : (q + 1) * quad] += v_sum

        @pl.when(tile == 0)
        def _():
            acc[...] = part

        @pl.when(tile > 0)
        def _():
            acc[...] += part

    if fused:

        @pl.when(step == 0)
        def _():
            peers.met(2 + nz)
            for copy in down.along_z():
                copy.start()

        settle()

        @pl.when(step == UPS)
        def _():
            for h in range(2):
                terms[OUT_PIECE, h] = owg_ref[0, h]
                send[OUT_PIECE % 2, h] = owg_ref[1, h]
            chip(OUT_PIECE).start()

        done_quad = (step >= FIRST_QUAD) & (step < FIRST_INPUT) & (tile == TILES - 1)

        @pl.when((step < UPS) | done_quad)
        def _():
            n = jnp.where(step < UPS, UP_PIECE + step, QUAD_PIECE + g)
            hand_out(acc, terms.at[n], send.at[n % 2])
            chip(n).start()

        @pl.when(step == FIRST_INPUT - 1)
        def _():
            vlow[...] = vec[...].astype(BF)
            for copy in vector_copies(0):
                copy.start()

        for hop in range(4):

            @pl.when(step == FIRST_INPUT + hop)
            def _(hop=hop):
                for copy in vector_copies(hop):
                    copy.wait()
                vec[...] = vlow[...].astype(F32) + sum(vgot[hop + k].astype(F32) for k in range(len(routes[hop])))
                if hop < 3:
                    vlow[...] = vec[...].astype(BF)
                    for copy in vector_copies(hop + 1):
                        copy.start()

        @pl.when(step == 4)
        def _():
            down.add()
            down.along_x().start()

        @pl.when(step == 7)
        def _():
            down.along_x().wait()

    else:

        @pl.when((step >= FIRST_QUAD) & (step < FIRST_INPUT) & (tile == TILES - 1))
        def _():
            qkvg_ref[...] = acc[...].astype(BF)

    @pl.when(step == FIRST_INPUT)
    def _():
        weight.wait()

    @pl.when(step >= FIRST_INPUT)
    def _():
        here = pl.ds(pl.multiple_of((step - FIRST_INPUT) * rows, rows), rows)
        grads = jnp.concatenate(
            [dqkv[q, here, part * quad : (part + 1) * quad] for part in range(3) for q in range(QUADS)], axis=1
        )
        out_ref[...] = nt(grads, w_ref[...]).astype(BF)

    @pl.when(step == STEPS - 1)
    def _():
        if fused:
            last(PIECES - 1)
        vec_out[...] = vec[...]
        if fused:
            for ref, value in zip(outs, (mine, other, dmine, dother), strict=True):
                ref[...] = value[...]


def tail(low, d_up, qkv, d_ctx, probs, token_rows, qkv_weight, owg, dsum, one, two, upsum, sizes):
    fused = sizes == (16, 2)
    nz = sizes[0] // 4
    sents, seq, width = probs.shape
    rows = sents * seq
    side = rows // TILES
    quad = width // QUADS
    shard, half = width // sizes[0], width // 2
    at = lambda i: jnp.clip(i - FIRST_QUAD, 0, QUADS * TILES - 1)
    cols = lambda part: pl.BlockSpec((side, quad), lambda i: (at(i) % TILES, part * QUADS + at(i) // TILES))
    once = lambda *shape: pl.BlockSpec(shape, lambda i: (0,) * len(shape))
    finish = lambda lanes: pl.BlockSpec((side, lanes), lambda i: (jnp.maximum(i - FIRST_INPUT, 0), 0))
    dma = pltpu.SemaphoreType.DMA
    scratch = [
        pltpu.VMEM(qkv_weight.shape, BF), dma, pltpu.VMEM((QUADS, rows, width), BF),
        pltpu.VMEM((width, width), F32), pltpu.VMEM((VECTORS, width), F32),
    ]
    out_specs = [finish(width), once(VECTORS, width)]
    out_shape = [shape_of((rows, width), BF), shape_of((VECTORS, width), F32)]
    if fused:
        piece = (2, nz, 2, shard, half)
        scratch += [pltpu.VMEM((PIECES, shard, half), BF)] * 2 + [pltpu.VMEM(dsum.shape[1:], BF)] * 2
        scratch += [pltpu.VMEM((PIECES, *piece), BF), pltpu.VMEM((2, *piece), BF), pltpu.VMEM((2, *piece), BF)]
        scratch += [pltpu.VMEM((PIECES, *s), BF) for s in Stages.scratch(nz, shard, half).values()]
        scratch += [
            pltpu.VMEM((PIECES, nz - 1, shard, half), BF), pltpu.VMEM((nz - 1, *dsum.shape[1:]), BF),
            pltpu.VMEM((VECTORS, width), BF), pltpu.VMEM((2 + nz, VECTORS, width), BF),
        ]
        scratch += [dma((PIECES, Stages.SEMS))] * 2 + [dma((Stages.SEMS,))] * 2 + [dma((2 + nz,))] * 2
        out_specs += [once(PIECES, shard, half)] * 2 + [once(*dsum.shape[1:])] * 2
        out_shape += [shape_of((PIECES, shard, half), BF)] * 2 + [shape_of(dsum.shape[1:], BF)] * 2
        extra = dict(collective_id=2, has_side_effects=True)
    else:
        out_specs += [
            pl.BlockSpec((width, width), lambda i: (0, jnp.minimum(i, UPS - 1))),
            pl.BlockSpec((width, width), lambda i: (0, at(i) // TILES)),
        ]
        out_shape += [shape_of((width, UPS * width), BF), shape_of((width, QUADS * width), BF)]
        extra = {}
    return pl.pallas_call(
        functools.partial(tail_kernel, fused, nz),
        grid=(STEPS,),
        in_specs=[
            resident((rows, width)), pl.BlockSpec((rows, width), lambda i: (0, jnp.minimum(i, UPS - 1))),
            cols(0), cols(1), cols(2), cols(0),
            pl.BlockSpec((SIDE, seq, quad), lambda i: (at(i) % TILES, 0, at(i) // TILES)),
            pl.BlockSpec((side, width), lambda i: (at(i) % TILES, 0)),
            pl.BlockSpec(memory_space=pl.ANY), resident(owg.shape), resident(dsum.shape), resident(one.shape),
            resident(two.shape), resident(upsum.shape),
        ],
        out_specs=out_specs,
        out_shape=out_shape,
        scratch_shapes=scratch,
        compiler_params=params(**extra),
        name="tail",
    )(low, d_up, qkv, qkv, qkv, d_ctx, probs, token_rows, qkv_weight, owg, dsum, one, two, upsum)


def finish_kernel(fused, part_ref, attn_ref, *refs):
    if not fused:
        (input_ref,) = refs
    else:
        (mine_ref, other_ref, dmine_ref, dother_ref, vec_ref, input_ref, qkv_ref, qb_ref, vb_ref, out_ref, ob_ref,
         g1_ref, s1_ref, up_ref, ub_ref, down_ref, db_ref, g2_ref, s2_ref) = refs
    input_ref[...] = part_ref[...].astype(F32) + attn_ref[...].astype(F32)
    if not fused:
        return

    @pl.when(pl.program_id(0) == 1)
    def _():
        wide, narrow, z, _, _ = place()
        width = vec_ref.shape[1]
        shard = qb_ref.shape[0]

        def whole(mine, other):
            mine, other = mine.astype(F32), other.astype(F32)
            return jnp.concatenate([jnp.where(narrow == 0, mine, other), jnp.where(narrow == 0, other, mine)], axis=-1)

        for n in range(UPS):
            up_ref[:, n * width : (n + 1) * width] = whole(mine_ref[UP_PIECE + n], other_ref[UP_PIECE + n])
        out_ref[...] = whole(mine_ref[OUT_PIECE], other_ref[OUT_PIECE])
        quad = width // QUADS
        for q in range(QUADS):
            block = whole(mine_ref[QUAD_PIECE + q], other_ref[QUAD_PIECE + q])
            for part in range(3):
                to = part * width + q * quad
                qkv_ref[:, to : to + quad] = block[:, part * quad : (part + 1) * quad]
        down_ref[...] = whole(dmine_ref[...], dother_ref[...])
        rolled = pltpu.roll(vec_ref[...], lax.rem(width - wide * shard, width), 1)
        for n, ref in enumerate((qb_ref, vb_ref, ob_ref, g1_ref, s1_ref, db_ref, g2_ref, s2_ref)):
            ref[...] = rolled[n, :shard]
        depth = ub_ref.shape[0]
        ups = jnp.concatenate([vec_ref[pl.ds(8 + z, 1), :]] * 8, axis=0)
        ub_ref[...] = pltpu.roll(ups, lax.rem(width - lax.rem(wide, 4) * depth, width), 1)[0, :depth]


def finish(part, d_attn, sums, sizes, depth):
    fused = bool(sums)
    rows, width = part.shape
    side = rows // TILES
    shard = width // sizes[0]
    tile = pl.BlockSpec((side, width), lambda i: (i, 0))
    shapes = [(rows, width)]
    if fused:
        up = depth // sizes[0]
        vector = (shard,)
        shapes += [
            (shard, 3 * width), vector, vector, (shard, width), vector, vector, vector, (shard, depth), (up,),
            (up, width), vector, vector, vector,
        ]
    return pl.pallas_call(
        functools.partial(finish_kernel, fused),
        grid=(TILES,),
        in_specs=[tile, tile] + [resident(a.shape) for a in sums],
        out_specs=[tile] + [pl.BlockSpec(s, lambda i, n=len(s): (0,) * n) for s in shapes[1:]],
        out_shape=[shape_of(s, F32) for s in shapes],
        compiler_params=params(),
        name="finish",
    )(part, d_attn, *sums)


def per_device(
    sizes, tokens, cotangent, groups, qkv_weight, query_bias, value_bias, out_weight, out_bias, gain_one,
    shift_one, up_weight, up_bias, down_weight, down_bias, gain_two, shift_two,
):
    n_wide, n_narrow = sizes
    sents, seq, width = tokens.shape
    depth = up_weight.shape[1]
    rows = sents * seq
    flat = lambda v: v.reshape(rows, v.shape[-1])

    qkv, probs, ctx = attend(tokens, qkv_weight, query_bias, value_bias)
    low, xh1, rs1, hidden, slope, xh2, rs2, cls, slots = forward(
        tokens, ctx, out_weight, out_bias, gain_one, shift_one, up_weight, up_bias, down_weight, down_bias,
        gain_two, shift_two, sizes,
    )
    gathered = slots.reshape(2, n_wide * n_narrow * (sents // 2), width)
    loss, block_out, d_down, sums_two = ranking(
        gathered, groups, cls, cotangent, xh2, rs2, gain_two, shift_two
    )
    d_up, d_attn, d_ctx, sums_one, up_sum, out_terms, down_terms = backward(
        d_down, flat(hidden), flat(slope), down_weight, up_weight, flat(xh1), flat(rs1), gain_one, out_weight,
        ctx, sizes,
    )
    part, vectors, *sums = tail(
        flat(low), d_up, qkv, d_ctx, probs, flat(tokens), qkv_weight, out_terms, down_terms, sums_one, sums_two,
        up_sum, sizes,
    )
    if sizes == (16, 2):
        input_grad, *grads = finish(part, d_attn, [*sums, vectors], sizes, depth)
    else:
        (input_grad,) = finish(part, d_attn, [], sizes, depth)
        up_terms, qkv_terms = sums
        quad = width // QUADS
        qkv_terms = qkv_terms.reshape(width, QUADS, 3, quad).transpose(0, 2, 1, 3).reshape(width, 3 * width)
        total = lambda v: lax.psum(
            lax.psum_scatter(v, "wide", scatter_dimension=0, tiled=True).astype(F32), "narrow"
        )
        vector = lambda n: total(vectors[n])
        grads = (
            total(qkv_terms), vector(0), vector(1), total(out_terms), vector(2), vector(3), vector(4),
            total(up_terms), total(vectors[8 : 8 + UPS].reshape(-1)), total(down_terms), vector(5), vector(6),
            vector(7),
        )
    return (loss.reshape(()), block_out, input_grad.reshape(sents, seq, width), *grads)


def solution(mesh):
    sizes = (mesh.shape["wide"], mesh.shape["narrow"])
    split = P(("wide", "narrow"), None, None)
    matrix, vector = P("wide", None), P("wide")
    return jax.shard_map(
        functools.partial(per_device, sizes),
        mesh=mesh,
        in_specs=(split, split) + (P(),) * 14,
        out_specs=(
            P(), split, split, matrix, vector, vector, matrix, vector, vector, vector, matrix, vector,
            matrix, vector, vector, vector,
        ),
        check_vma=False,
    )
```
